32 devices in a mesh: tiles: 16 (over z, y, x), grp: 2 (over core).
Axes of the slice: x: 2, y: 2, z: 4, core: 2. Of those that a mesh axis runs over, the one named last changes fastest.
Arguments:
- strips: bfloat16 [64, 256, 4096], P(('tiles', 'grp'))
- edge_colour: int32 [32, 2], P(('tiles', 'grp')), may hold values from 0 to 1, as said below
- patch_offsets: int32 [32, 2, 16, 2], P(('tiles', 'grp')), may hold values from 0 to 3968, as said below
- patch_live: int32 [32, 2], P(('tiles', 'grp')), may hold values from 4 to 16
- node_ids: int32 [32, 2, 16], P(('tiles', 'grp')), may hold values from 0 to 4095
Outputs:
- node_sums: float32 [2, 4096], P(None, ('tiles', 'grp'))
The draws below stay inside these ranges and needn't reach their ends.
Inputs may be any that keep to these rules, and one draw needn't show every extreme that they name: `edge_colour`: for each device its 2 entries name different strips. `patch_offsets`: A device and the device it is paired with in a round have the same offsets in that round. Rows are at most 128.
All inputs are finite; a program needn't handle non-finite values.
Results may differ from the reference program's by a relative error of at most 0.0003.
Values may be sent and summed in bfloat16 or wider, within the bound.
A program may use at most 64 MiB of HBM per device.

```python
import math
import jax
import jax.numpy as jnp
from jax import lax

PATCH = 128
STRIP_R = 256
WIDTH = 4096
ROUNDS = 2
PATCH_DEV = 16
NODES = 4096
N_TILES = 16
N_GRP = 2
DEVICES = 32


def device_flips(key):
    return jax.random.randint(jax.random.fold_in(key, 7), (DEVICES,), 0, 2)


def pair_number(device, round_index):
    tile_index = device // N_GRP
    group_index = device % N_GRP
    pair_bit = jnp.where(round_index == 0, 0, N_TILES.bit_length() - 2)
    side = jnp.right_shift(tile_index, pair_bit) % 2
    lower = tile_index - side * jnp.left_shift(1, pair_bit)
    return ((lower * N_GRP + group_index) * ROUNDS + round_index, side)


def draw_edge_colour(key, part):
    flips = device_flips(key)
    rounds = jnp.arange(ROUNDS, dtype=jnp.int32)
    return jnp.bitwise_xor(rounds[None, :], flips[:, None]).astype(jnp.int32)


def draw_patch_offsets(key, part):

    def single(device, round_index):
        number, side = pair_number(device, round_index)
        pair_key = jax.random.fold_in(key, 5000 + number)
        rows = jax.random.randint(jax.random.fold_in(pair_key, 1), (PATCH_DEV,), 0, STRIP_R - PATCH + 1)
        cols = jax.random.randint(jax.random.fold_in(pair_key, 2), (PATCH_DEV,), 0, WIDTH - PATCH + 1)
        rows = rows.at[0].set(0)
        cols = cols.at[0].set(WIDTH - PATCH)
        return jnp.stack([rows, cols], axis=1)
    devices = jnp.arange(DEVICES, dtype=jnp.int32)
    rounds = jnp.arange(ROUNDS, dtype=jnp.int32)
    table = jax.vmap(lambda device: jax.vmap(lambda rnd: single(device, rnd))(rounds))(devices)
    return table.astype(jnp.int32)


def draw_patch_live(key, part):
    counts = jax.random.randint(jax.random.fold_in(key, 11), (DEVICES, ROUNDS), PATCH_DEV // 4, PATCH_DEV + 1)
    return counts.at[0, 0].set(PATCH_DEV).astype(jnp.int32)


def draw_strips(key, part):
    flips = device_flips(key)
    reach = 3 * PATCH // 8
    block_count = WIDTH // PATCH
    row_positions = jnp.arange(STRIP_R, dtype=jnp.int32)
    col_positions = jnp.arange(WIDTH, dtype=jnp.int32)
    block_of_col = col_positions // PATCH

    def single(index):
        device = index // ROUNDS
        strip_index = index % ROUNDS
        round_index = jnp.bitwise_xor(strip_index, flips[device])
        number, side = pair_number(device, round_index)
        base_key = jax.random.fold_in(key, 100000 + number)
        base = jax.random.normal(base_key, (STRIP_R, WIDTH), jnp.float32)
        row_moves = jax.random.randint(jax.random.fold_in(base_key, 1), (block_count,), -reach, reach + 1)
        col_moves = jax.random.randint(jax.random.fold_in(base_key, 2), (block_count,), -reach, reach + 1)
        row_source = (row_positions[:, None] - side * row_moves[block_of_col][None, :]) % STRIP_R
        col_source = (col_positions[None, :] - side * col_moves[block_of_col][None, :]) % WIDTH
        col_source = jnp.broadcast_to(col_source, (STRIP_R, WIDTH))
        moved = base[row_source, col_source]
        noise = jax.random.normal(jax.random.fold_in(jax.random.fold_in(key, 3), index), (STRIP_R, WIDTH), jnp.float32)
        result = moved + 0.5 * noise
        return result
    return lax.map(single, jnp.arange(DEVICES * ROUNDS, dtype=jnp.int32)).astype(jnp.bfloat16)


def set_ends(drawn, key, least, top_value):
    shape = drawn.shape
    index_at = [jax.random.randint(jax.random.fold_in(key, axis), (), 0, shape[axis]) for axis in range(len(shape))]
    drawn = drawn.at[tuple(index_at)].set(least)
    longest = shape.index(max(shape))
    index_at[longest] = (index_at[longest] + 1) % shape[longest]
    return drawn.at[tuple(index_at)].set(top_value)


def setup_inputs(seed: int = 0) -> dict:
    key_of = jax.random.split(jax.random.key(seed), 6)
    return {
        "strips": draw_strips(jax.random.fold_in(key_of[5], 71), 0),
        "edge_colour": draw_edge_colour(jax.random.fold_in(key_of[5], 71), 0),
        "patch_offsets": draw_patch_offsets(jax.random.fold_in(key_of[5], 71), 0),
        "patch_live": draw_patch_live(jax.random.fold_in(key_of[5], 71), 0),
        "node_ids": set_ends(jax.random.randint(key_of[4], (DEVICES, ROUNDS, PATCH_DEV), 0, NODES), jax.random.fold_in(key_of[4], 1), 0, NODES - 1).astype(jnp.int32),
    }


highest = lax.Precision.HIGHEST

def tables(length):
    indices = jnp.arange(length, dtype=jnp.int32)
    product = indices[:, None] * indices[None, :] % length
    angles = product.astype(jnp.float32) * (2.0 * math.pi / length)
    return (jnp.cos(angles), jnp.sin(angles))

def right_mul(patches, matrix):
    return jnp.einsum('pab,bc->pac', patches, matrix, precision=highest)

def left_mul(matrix, patches):
    return jnp.einsum('ab,pbc->pac', matrix, patches, precision=highest)

def forward(patches, cosine, sine):
    real_half = right_mul(patches, cosine)
    imag_half = -right_mul(patches, sine)
    return (left_mul(cosine, real_half) + left_mul(sine, imag_half), left_mul(cosine, imag_half) - left_mul(sine, real_half))

def displacement(first_set, second_set):
    length = first_set.shape[-1]
    cosine, sine = tables(length)
    first_real, first_imag = forward(first_set, cosine, sine)
    second_real, second_imag = forward(second_set, cosine, sine)
    cross_real = first_real * second_real + first_imag * second_imag
    cross_imag = first_imag * second_real - first_real * second_imag
    magnitude = jnp.sqrt(cross_real * cross_real + cross_imag * cross_imag)
    denominator = magnitude + 0.1 * lax.optimization_barrier(jnp.mean(magnitude, axis=(1, 2), keepdims=True)) + 1e-06
    white_real = cross_real / denominator
    white_imag = cross_imag / denominator
    back_real = left_mul(cosine, white_real) - left_mul(sine, white_imag)
    back_imag = left_mul(cosine, white_imag) + left_mul(sine, white_real)
    surface = (right_mul(back_real, cosine) - right_mul(back_imag, sine)) / float(length * length)
    flattened = surface.reshape(surface.shape[0], length * length)
    centre = lax.optimization_barrier(jnp.mean(flattened, axis=1, keepdims=True))
    spread = jnp.sqrt(lax.optimization_barrier(jnp.mean((flattened - centre) * (flattened - centre), axis=1, keepdims=True)) + 1e-06)
    scores = 2.0 * (flattened - centre) / spread
    weights = jax.nn.softmax(scores, axis=-1).reshape(surface.shape)
    coords = ((jnp.arange(length, dtype=jnp.int32) + length // 2) % length - length // 2).astype(jnp.float32)
    coord_scale = float(length // 8)
    row_shift = lax.optimization_barrier(jnp.sum(weights * coords[None, :, None], axis=(1, 2))) / coord_scale
    col_shift = lax.optimization_barrier(jnp.sum(weights * coords[None, None, :], axis=(1, 2))) / coord_scale
    return jnp.stack([row_shift, col_shift])

def window_stack(strip, offsets):

    def single(corner):
        return lax.dynamic_slice(strip, (corner[0], corner[1]), (PATCH, PATCH))
    return jax.vmap(single)(offsets)

def reference(strips, edge_colour, patch_offsets, patch_live, node_ids):
    stacked = strips.reshape(DEVICES, ROUNDS, STRIP_R, WIDTH)

    def one_device(device):
        tile_index = device // N_GRP
        group_index = device % N_GRP
        first_list = []
        second_list = []
        for round_index in range(ROUNDS):
            pair_bit = 0 if round_index == 0 else N_TILES.bit_length() - 2
            partner = ((tile_index ^ 1 << pair_bit) * N_GRP + group_index).astype(jnp.int32)
            own_strip = stacked[device, edge_colour[device, round_index]]
            other_strip = stacked[partner, edge_colour[partner, round_index]]
            corners = patch_offsets[device, round_index]
            first_list.append(window_stack(own_strip, corners))
            second_list.append(window_stack(other_strip, corners))
        first_set = jnp.concatenate(first_list, axis=0).astype(jnp.float32)
        second_set = jnp.concatenate(second_list, axis=0).astype(jnp.float32)
        shifts = displacement(first_set, second_set)
        slot_index = jnp.arange(PATCH_DEV, dtype=jnp.int32)
        live_mask = (slot_index[None, :] < patch_live[device][:, None]).reshape(ROUNDS * PATCH_DEV)
        return jnp.where(live_mask[None, :], shifts, jnp.zeros_like(shifts))
    values = lax.map(one_device, jnp.arange(DEVICES).astype(jnp.int32))
    values = jnp.transpose(values, (0, 2, 1)).reshape(DEVICES * ROUNDS * PATCH_DEV, 2)
    node_list = node_ids.reshape(DEVICES * ROUNDS * PATCH_DEV)
    summed = jax.ops.segment_sum(values, node_list, num_segments=NODES)
    return jnp.transpose(summed)
```

```python
import functools
import math

import jax
import jax.numpy as jnp
import numpy as np
from jax import lax
from jax.experimental import pallas as pl
from jax.experimental.pallas import tpu as pltpu
from jax.sharding import PartitionSpec as P

PATCH = 128
NODE_DEV = 128
LANES = 128
GROUP = 4
PAIR = 2
SUB = 16
LAST = ((0, 2), (2, 1), (3, 1))
VMEM_LIMIT = 67043328 - 16384

F32 = jnp.float32
BF16 = jnp.bfloat16
VMEM = pltpu.MemorySpace.VMEM
SMEM = pltpu.MemorySpace.SMEM


def split_np(x):
    hi = np.asarray(x, np.float32).astype(BF16)
    lo = (np.asarray(x, np.float64) - hi.astype(np.float64)).astype(np.float32).astype(BF16)
    return hi, lo


def tables():
    n = PATCH
    j = np.arange(n)
    angle = 2.0 * math.pi / n * ((j[:, None] * j[None, :]) % n)
    c, s = np.cos(angle), np.sin(angle)
    chi, clo = split_np(np.concatenate([c, s], axis=1))
    col = np.concatenate([chi, clo], axis=0)
    rhi, rlo = split_np(np.block([[c, -s], [s, c]]))
    row = np.concatenate([rhi, rlo, rhi], axis=1)
    ihi, ilo = split_np(np.concatenate([c, s], axis=1))
    inv_row = np.concatenate([ihi, ilo, ihi], axis=1)
    weight = np.where((j == 0) | (j == n // 2), 1.0, 2.0)[:, None]
    packed = np.where(j[:, None] <= n // 2, weight * c, -2.0 * s) / float(n * n)
    vhi, vlo = split_np(packed)
    inv_col = np.concatenate([vhi, vlo, vhi], axis=0)
    return col, row, inv_row, inv_col


def split(x):
    hi = x.astype(BF16)
    return hi, (x - hi.astype(F32)).astype(BF16)


def dot(a, b):
    return jnp.dot(a, b, preferred_element_type=F32)


def row_place(column, base):
    count = column.shape[0]
    lane = lax.broadcasted_iota(jnp.int32, (count, LANES), 1)
    sub = lax.broadcasted_iota(jnp.int32, (count, LANES), 0)
    return jnp.sum(jnp.where(lane == sub + base, column, 0.0), axis=0, keepdims=True)


def spectra(windows, col, row):
    n = PATCH
    if len(windows) == 1:
        x = windows[0]
        hi, lo = split(dot(jnp.concatenate([x, x], axis=1), col))
        hi, lo = (jnp.concatenate([v[:, :n], v[:, n:]], axis=0) for v in (hi, lo))
        f = dot(row, jnp.concatenate([hi, hi, lo], axis=0))
        return [(f[:n], f[n:])]
    x = jnp.concatenate(windows, axis=0)
    hi, lo = split(dot(jnp.concatenate([x, x], axis=1), col))

    def stack(v):
        return jnp.concatenate(
            [
                jnp.concatenate([v[:n, :n], v[n:, :n]], axis=1),
                jnp.concatenate([v[:n, n:], v[n:, n:]], axis=1),
            ],
            axis=0,
        )

    hi, lo = stack(hi), stack(lo)
    f = dot(row, jnp.concatenate([hi, hi, lo], axis=0))
    return [(f[:n, :n], f[n:, :n]), (f[:n, n:], f[n:, n:])]


def correlate(first, second, inv_row, inv_col):
    n = PATCH
    count = len(first)
    lane = lax.broadcasted_iota(jnp.int32, (n, n), 1)
    low = lane <= n // 2
    crosses = []
    mag_sums = []
    for (r1, i1), (r2, i2) in zip(first, second):
        cross_r = r1 * r2 + i1 * i2
        cross_i = r1 * i2 - i1 * r2
        mag = jnp.sqrt(cross_r * cross_r + cross_i * cross_i)
        crosses.append((cross_r, cross_i, mag))
        mag_sums.append(jnp.sum(mag, axis=0, keepdims=True))
    mean = jnp.sum(jnp.concatenate(mag_sums, axis=0), axis=1, keepdims=True) / float(n * n)
    extra = 0.1 * mean + 1e-06
    surfaces = []
    packed = []
    sums = []
    for p in range(count):
        cross_r, cross_i, mag = crosses[p]
        inverse = 1.0 / (mag + extra[p : p + 1])
        g_r = cross_r * inverse
        g_i = cross_i * inverse
        packed.append(
            split(jnp.concatenate([jnp.where(low, g_r, g_i), jnp.where(low, -g_i, g_r)], axis=0))
        )
    surfaces_wide = []
    for p in range(0, count, 2):
        some = packed[p : p + 2]
        hi = jnp.concatenate([v[0] for v in some], axis=1)
        lo = jnp.concatenate([v[1] for v in some], axis=1)
        b = dot(inv_row, jnp.concatenate([hi, hi, lo], axis=0))
        bhi, blo = split(jnp.concatenate([b[:, i * n : (i + 1) * n] for i in range(len(some))], axis=0))
        wide = dot(jnp.concatenate([bhi, bhi, blo], axis=1), inv_col)
        surfaces_wide += [wide[i * n : (i + 1) * n] for i in range(len(some))]
    for surface in surfaces_wide:
        surfaces.append(surface)
        sums.append(jnp.sum(surface, axis=0, keepdims=True))
    centre = jnp.sum(jnp.concatenate(sums, axis=0), axis=1, keepdims=True) / float(n * n)
    squares = []
    tops = []
    for p in range(count):
        deviation = surfaces[p] - centre[p : p + 1]
        squares.append(jnp.sum(deviation * deviation, axis=0, keepdims=True))
        tops.append(jnp.max(surfaces[p], axis=0, keepdims=True))
    variance = jnp.sum(jnp.concatenate(squares, axis=0), axis=1, keepdims=True) / float(n * n)
    top = jnp.max(jnp.concatenate(tops, axis=0), axis=1, keepdims=True)
    scale = 2.0 / jnp.sqrt(variance + 1e-06)
    sub = lax.broadcasted_iota(jnp.int32, (n, n), 0)
    sub_coord = ((sub + n // 2) % n - n // 2).astype(F32)
    columns = []
    rows = []
    edges = []
    for p in range(count):
        e = jnp.exp((surfaces[p] - top[p : p + 1]) * scale[p : p + 1])
        columns.append(jnp.sum(e, axis=0, keepdims=True))
        rows.append(jnp.sum(e * sub_coord, axis=0, keepdims=True))
        edges.append(e[n // 2 : n // 2 + 1, :])
    columns = jnp.concatenate(columns, axis=0)
    rows = jnp.concatenate(rows, axis=0)
    edges = jnp.concatenate(edges, axis=0)
    lane = lax.broadcasted_iota(jnp.int32, (count, n), 1)
    lane_coord = ((lane + n // 2) % n - n // 2).astype(F32)

    def total(v):
        return jnp.sum(v, axis=1, keepdims=True)

    unit = float(n // 8)
    norm = 1.0 / total(columns)
    row_shift = total(rows) * norm / unit
    col_shift = total(columns * lane_coord) * norm / unit
    row_edge = total(edges) * norm * (float(n) / unit)
    col_edge = total(jnp.where(lane == n // 2, columns, 0.0)) * norm * (float(n) / unit)
    return row_shift, col_shift, -row_shift - row_edge, -col_shift - col_edge


MESH = pl.DeviceIdType.MESH


def stitch(
    colour_ref,
    offset_ref,
    live_ref,
    ids_ref,
    strips_hbm,
    col_hbm,
    row_hbm,
    inv_row_hbm,
    inv_col_hbm,
    out_ref,
    strips,
    col_ref,
    row_ref,
    inv_row_ref,
    inv_col_ref,
    shifted,
    sent,
    firsts,
    arrived,
    line,
    lines,
    tile_out,
    tiles,
    strip_sem,
    table_sem,
    window_send,
    window_recv,
    line_send,
    line_recv,
    tile_send,
    tile_recv,
    hello,
):
    n = PATCH
    rounds, blocks, layers = strips.shape[:3]
    slots = offset_ref.shape[3]
    half = slots // 2
    entries = rounds * slots
    groups = lax.axis_size("grp")
    tile_count = lax.axis_size("tiles")
    devices = tile_count * groups
    tile_index = lax.axis_index("tiles")
    group_index = lax.axis_index("grp")
    me = tile_index * groups + group_index
    strides = [1] + [tile_count // 2] * (rounds - 1)
    sides = [(tile_index // s) % 2 for s in strides]
    partners = [tile_index + s * (1 - 2 * side) for s, side in zip(strides, sides)]

    barrier = pltpu.get_barrier_semaphore()
    neighbours = []
    stride = 1
    while stride < tile_count:
        bit = (tile_index // stride) % 2
        neighbours.append((tile_index + stride * (1 - 2 * bit), group_index))
        stride *= 2
    stride = 1
    while stride < groups:
        bit = (group_index // stride) % 2
        neighbours.append((tile_index, group_index + stride * (1 - 2 * bit)))
        stride *= 2
    stages = len(neighbours)
    for at in neighbours:
        pl.semaphore_signal(barrier, inc=1, device_id=at, device_id_type=MESH)

    strip_loads = [
        pltpu.make_async_copy(strips_hbm.at[:, :, :, pl.ds(i * LANES, LANES)], strips.at[:, i], strip_sem)
        for i in range(blocks)
    ]
    for load in strip_loads:
        load.start()
    table_loads = [
        pltpu.make_async_copy(a, b, table_sem.at[i])
        for i, (a, b) in enumerate(
            [(col_hbm, col_ref), (row_hbm, row_ref), (inv_row_hbm, inv_row_ref), (inv_col_hbm, inv_col_ref)]
        )
    ]
    for load in table_loads:
        load.start()
    pltpu.make_async_copy(strips, strips, strip_sem).wait()

    def extract(r, picks):
        rests = []
        lane = lax.broadcasted_iota(jnp.int32, (n + SUB, LANES), 1)
        for i, k in enumerate(picks):
            row, column = offset_ref[0, r, 0, k], offset_ref[0, r, 1, k]
            block = jnp.minimum(lax.div(column, LANES), blocks - 2)
            layer = jnp.minimum(lax.div(row, SUB), layers - n // SUB - 1)
            shift = column - block * LANES
            turn = lax.rem(2 * LANES - shift, LANES)
            left, right = (
                pltpu.roll(
                    strips[colour_ref[0, r], block + side, pl.ds(layer, n // SUB + 1)]
                    .reshape(n + SUB, LANES)
                    .astype(F32),
                    turn,
                    1,
                )
                for side in range(2)
            )
            shifted[i] = jnp.where(lane < LANES - shift, left, right)
            rests.append(row - layer * SUB)
        return [shifted[i, pl.ds(rest, n), :].astype(BF16) for i, rest in enumerate(rests)]

    def window_copy(r, j):
        return pltpu.make_async_remote_copy(
            src_ref=sent.at[r, j],
            dst_ref=arrived.at[r, j],
            send_sem=window_send.at[r, j],
            recv_sem=window_recv.at[r, j],
            device_id=(partners[r], group_index),
            device_id_type=MESH,
        )

    def line_copy(r):
        return pltpu.make_async_remote_copy(
            src_ref=line,
            dst_ref=lines.at[r],
            send_sem=line_send.at[r],
            recv_sem=line_recv.at[r],
            device_id=(partners[r], group_index),
            device_id_type=MESH,
        )

    def produce(r, j):
        base = (1 - sides[r]) * half
        for i, window in enumerate(extract(r, [base + j + i for i in range(PAIR)])):
            sent[r, j + i] = window

    order = list(range(rounds))[::-1]
    produce(order[0], 0)
    pl.semaphore_wait(barrier, stages)
    for r in order:
        if r != order[0]:
            produce(r, 0)
            for i in range(PAIR):
                window_copy(r + 1, half - PAIR + i).start()

        def step(p, carry, r=r):
            produce(r, p * PAIR)
            for i in range(PAIR):
                window_copy(r, (p - 1) * PAIR + i).start()
            return carry

        lax.fori_loop(1, half // PAIR, step, 0)

    lane = lax.broadcasted_iota(jnp.int32, (1, LANES), 1)
    ids = jnp.zeros((1, LANES), jnp.int32)
    for r in range(rounds):
        for k in range(slots):
            node = jnp.where(k < live_ref[0, r], ids_ref[0, r, k], -1)
            ids = jnp.where(lane == r * slots + k, node, ids)
    line[...] = ids.astype(F32)
    for i in range(PAIR):
        window_copy(0, half - PAIR + i).start()
    for load in table_loads:
        load.wait()

    def prepare(r):
        def step(p, carry):
            j = p * PAIR
            windows = extract(r, [sides[r] * half + j + i for i in range(PAIR)])
            for q in range(0, PAIR, 2):
                pair = spectra(windows[q : q + 2], col_ref[...], row_ref[...])
                for i in range(2):
                    for c in range(2):
                        firsts[r, j + q + i, c] = pair[i][c]
            return carry

        return step

    lax.fori_loop(0, 1, prepare(0), 0)
    for r in range(rounds):
        line_copy(r).start()
    lax.fori_loop(1, half // PAIR, prepare(0), 0)
    for r in range(1, rounds):
        lax.fori_loop(0, half // PAIR, prepare(r), 0)

    def hail(stage):
        pl.semaphore_signal(hello.at[stage], inc=1, device_id=neighbours[stage], device_id_type=MESH)

    def greet(stage):
        if stage > 0:
            pl.semaphore_wait(hello.at[stage - 1], 1)
        if stage < stages:
            hail(stage)

    def work(r, j, count, carry):
        for i in range(count):
            pltpu.make_async_remote_copy(
                src_ref=sent.at[r, j + i],
                dst_ref=arrived.at[r, j + i],
                send_sem=window_send.at[r, j + i],
                recv_sem=window_recv.at[r, j + i],
                device_id=(partners[r], group_index),
                device_id_type=MESH,
            ).wait_recv()
        seconds = []
        for p in range(0, count, 2):
            seconds += spectra([arrived[r, j + i] for i in range(p, min(p + 2, count))], col_ref[...], row_ref[...])
        a, b, c, d = correlate(
            [(firsts[r, j + i, 0], firsts[r, j + i, 1]) for i in range(count)],
            seconds,
            inv_row_ref[...],
            inv_col_ref[...],
        )
        own = r * slots + sides[r] * half + j
        other = r * slots + (1 - sides[r]) * half + j
        return (
            carry
            + row_place(a, own)
            + row_place(c, other)
            + row_place(b, own + entries)
            + row_place(d, other + entries)
        )

    disp = jnp.zeros((1, LANES), F32)
    plan = [(r, j, GROUP) for r in range(rounds) for j in range(0, half, GROUP)]
    plan = plan[:-1] + [(rounds - 1, half - GROUP + i, c) for i, c in LAST]
    stage = 0
    for r, j, count in plan:
        if stage <= stages:
            greet(stage)
            stage += 1
        disp = work(r, j, count, disp)
        if (r, j) == (0, 0):
            for s in range(rounds):
                line_copy(s).wait()
            ids = line[...]
            id_line = jnp.zeros((1, LANES), F32)
            for s in range(rounds):
                theirs = pltpu.roll(lines[s], jnp.where(sides[s] == 0, half, LANES - half), 1)
                in_round = (lane >= s * slots) & (lane < (s + 1) * slots)
                mine = (lane // half) % 2 == sides[s]
                id_line = id_line + jnp.where(in_round, jnp.where(mine, ids, theirs), 0.0)
            disp = disp + pltpu.roll(id_line, 2 * entries, 1)
    while stage <= stages:
        greet(stage)
        stage += 1

    tile_out[...] = disp
    tiles[me] = disp

    def start(i, carry):
        to = i + jnp.where(i >= me, 1, 0)
        pltpu.make_async_remote_copy(
            src_ref=tile_out,
            dst_ref=tiles.at[me],
            send_sem=tile_send,
            recv_sem=tile_recv,
            device_id=(to // groups, to % groups),
            device_id_type=MESH,
        ).start()
        return carry

    lax.fori_loop(0, devices - 1, start, 0)
    for r in range(rounds):
        for j in range(half):
            window_copy(r, j).wait_send()
    everyone = pltpu.make_async_remote_copy(
        src_ref=tiles.at[pl.ds(0, devices - 1)],
        dst_ref=tiles.at[pl.ds(0, devices - 1)],
        send_sem=tile_send,
        recv_sem=tile_recv,
        device_id=neighbours[0],
        device_id_type=MESH,
    )
    everyone.wait_recv()

    pack = LANES // entries
    node = lax.broadcasted_iota(jnp.int32, (NODE_DEV, LANES), 0).astype(F32)
    first_node = (me * NODE_DEV).astype(F32)
    lane = lax.broadcasted_iota(jnp.int32, (1, LANES), 1)
    onehots = []
    values = []
    for g in range(devices // pack):
        parts = [jnp.zeros((1, LANES), F32)] * 3
        for i in range(pack):
            tile = tiles[g * pack + i]
            here = (lane >= i * entries) & (lane < (i + 1) * entries)
            for c in range(3):
                moved = pltpu.roll(tile, ((i - c) * entries) % LANES, 1) if i != c else tile
                parts[c] = jnp.where(here, moved, parts[c])
        onehots.append(jnp.where(parts[2] - first_node == node, 1.0, 0.0).astype(BF16))
        tile = jnp.concatenate(parts[:2], axis=0)
        hi = tile.astype(BF16).astype(F32)
        rest = tile - hi
        mid = rest.astype(BF16).astype(F32)
        values.append(jnp.concatenate([hi, mid, rest - mid, jnp.zeros_like(hi)], axis=0).astype(BF16))
    result = lax.dot_general(
        jnp.concatenate(values, axis=1),
        jnp.concatenate(onehots, axis=1),
        (((1,), (1,)), ((), ())),
        preferred_element_type=F32,
    )
    out_ref[0:2] = result[0:2]
    out_ref[2:4] = result[2:4] + result[4:6]
    everyone.wait_send()


def on_device(strips, edge_colour, patch_offsets, patch_live, node_ids):
    rounds, height, width = strips.shape
    n = PATCH
    slot_count = patch_offsets.shape[2]
    half = slot_count // 2
    devices = lax.axis_size("tiles") * lax.axis_size("grp")
    whole = pl.BlockSpec(memory_space=VMEM)
    anywhere = pl.BlockSpec(memory_space=pl.ANY)
    sem = pltpu.SemaphoreType.DMA
    windows = (rounds, half, n, n)
    scalars = [jnp.transpose(patch_offsets, (0, 1, 3, 2)), edge_colour, patch_live, node_ids]
    constants = [jnp.asarray(t) for t in tables()]
    sums = pl.pallas_call(
        stitch,
        out_shape=jax.ShapeDtypeStruct((4, NODE_DEV), F32),
        in_specs=[pl.BlockSpec(memory_space=SMEM)] * 4 + [anywhere] * 5,
        out_specs=whole,
        scratch_shapes=[
            pltpu.VMEM((rounds, width // LANES, height // SUB, SUB, LANES), BF16),
            *(pltpu.VMEM(t.shape, BF16) for t in constants),
            pltpu.VMEM((PAIR, n + 16, n), F32),
            pltpu.VMEM(windows, BF16),
            pltpu.VMEM((rounds, half, 2, n, n), F32),
            pltpu.VMEM(windows, BF16),
            pltpu.VMEM((1, LANES), F32),
            pltpu.VMEM((rounds, 1, LANES), F32),
            pltpu.VMEM((1, LANES), F32),
            pltpu.VMEM((devices, 1, LANES), F32),
            sem(()),
            sem((4,)),
            sem((rounds, half)),
            sem((rounds, half)),
            sem((rounds,)),
            sem((rounds,)),
            sem(()),
            sem(()),
            pltpu.SemaphoreType.REGULAR((devices.bit_length() - 1,)),
        ],
        compiler_params=pltpu.CompilerParams(collective_id=0, has_side_effects=True, vmem_limit_bytes=VMEM_LIMIT),
        name="stitch",
    )(edge_colour, scalars[0], patch_live, node_ids, strips.reshape(rounds, height // SUB, SUB, width), *constants)
    return sums[0:2] + sums[2:4]


def solution(mesh):
    placed = (
        P(("tiles", "grp"), None, None),
        P(("tiles", "grp"), None),
        P(("tiles", "grp"), None, None, None),
        P(("tiles", "grp"), None),
        P(("tiles", "grp"), None, None),
    )
    return jax.shard_map(
        on_device, mesh=mesh, in_specs=placed, out_specs=P(None, ("tiles", "grp")), check_vma=False
    )
```

```python
import functools
import math

import jax
import jax.numpy as jnp
import numpy as np
from jax import lax
from jax.experimental import pallas as pl
from jax.experimental.pallas import tpu as pltpu
from jax.sharding import PartitionSpec as P

PATCH = 128
NODE_DEV = 128
LANES = 128
GROUP = 4
PAIR = 2
SUB = 16
LAST = ((0, 4),)
VMEM_LIMIT = 67043328 - 16384

F32 = jnp.float32
BF16 = jnp.bfloat16
VMEM = pltpu.MemorySpace.VMEM
SMEM = pltpu.MemorySpace.SMEM


def split_np(x):
    hi = np.asarray(x, np.float32).astype(BF16)
    lo = (np.asarray(x, np.float64) - hi.astype(np.float64)).astype(np.float32).astype(BF16)
    return hi, lo


def tables():
    n = PATCH
    j = np.arange(n)
    angle = 2.0 * math.pi / n * ((j[:, None] * j[None, :]) % n)
    c, s = np.cos(angle), np.sin(angle)
    chi, clo = split_np(np.concatenate([c, s], axis=1))
    col = np.concatenate([chi, clo], axis=0)
    rhi, rlo = split_np(np.block([[c, -s], [s, c]]))
    row = np.concatenate([rhi, rlo, rhi], axis=1)
    ihi, ilo = split_np(np.concatenate([c, s], axis=1))
    inv_row = np.concatenate([ihi, ilo, ihi], axis=1)
    weight = np.where((j == 0) | (j == n // 2), 1.0, 2.0)[:, None]
    packed = np.where(j[:, None] <= n // 2, weight * c, -2.0 * s) / float(n * n)
    vhi, vlo = split_np(packed)
    inv_col = np.concatenate([vhi, vlo, vhi], axis=0)
    return col, row, inv_row, inv_col


def split(x):
    hi = x.astype(BF16)
    return hi, (x - hi.astype(F32)).astype(BF16)


def dot(a, b):
    return jnp.dot(a, b, preferred_element_type=F32)


def row_place(column, base):
    count = column.shape[0]
    lane = lax.broadcasted_iota(jnp.int32, (count, LANES), 1)
    sub = lax.broadcasted_iota(jnp.int32, (count, LANES), 0)
    return jnp.sum(jnp.where(lane == sub + base, column, 0.0), axis=0, keepdims=True)


def spectra(windows, col, row):
    n = PATCH
    if len(windows) == 1:
        x = windows[0]
        hi, lo = split(dot(jnp.concatenate([x, x], axis=1), col))
        hi, lo = (jnp.concatenate([v[:, :n], v[:, n:]], axis=0) for v in (hi, lo))
        f = dot(row, jnp.concatenate([hi, hi, lo], axis=0))
        return [(f[:n], f[n:])]
    x = jnp.concatenate(windows, axis=0)
    hi, lo = split(dot(jnp.concatenate([x, x], axis=1), col))

    def stack(v):
        return jnp.concatenate(
            [
                jnp.concatenate([v[:n, :n], v[n:, :n]], axis=1),
                jnp.concatenate([v[:n, n:], v[n:, n:]], axis=1),
            ],
            axis=0,
        )

    hi, lo = stack(hi), stack(lo)
    f = dot(row, jnp.concatenate([hi, hi, lo], axis=0))
    return [(f[:n, :n], f[n:, :n]), (f[:n, n:], f[n:, n:])]


def correlate(first, second, inv_row, inv_col):
    n = PATCH
    count = len(first)
    lane = lax.broadcasted_iota(jnp.int32, (n, n), 1)
    low = lane <= n // 2
    crosses = []
    mag_sums = []
    for (r1, i1), (r2, i2) in zip(first, second):
        cross_r = r1 * r2 + i1 * i2
        cross_i = r1 * i2 - i1 * r2
        mag = jnp.sqrt(cross_r * cross_r + cross_i * cross_i)
        crosses.append((cross_r, cross_i, mag))
        mag_sums.append(jnp.sum(mag, axis=0, keepdims=True))
    mean = jnp.sum(jnp.concatenate(mag_sums, axis=0), axis=1, keepdims=True) / float(n * n)
    extra = 0.1 * mean + 1e-06
    surfaces = []
    packed = []
    sums = []
    for p in range(count):
        cross_r, cross_i, mag = crosses[p]
        inverse = 1.0 / (mag + extra[p : p + 1])
        g_r = cross_r * inverse
        g_i = cross_i * inverse
        packed.append(
            split(jnp.concatenate([jnp.where(low, g_r, g_i), jnp.where(low, -g_i, g_r)], axis=0))
        )
    surfaces_wide = []
    for p in range(0, count, 2):
        some = packed[p : p + 2]
        hi = jnp.concatenate([v[0] for v in some], axis=1)
        lo = jnp.concatenate([v[1] for v in some], axis=1)
        b = dot(inv_row, jnp.concatenate([hi, hi, lo], axis=0))
        bhi, blo = split(jnp.concatenate([b[:, i * n : (i + 1) * n] for i in range(len(some))], axis=0))
        wide = dot(jnp.concatenate([bhi, bhi, blo], axis=1), inv_col)
        surfaces_wide += [wide[i * n : (i + 1) * n] for i in range(len(some))]
    for surface in surfaces_wide:
        surfaces.append(surface)
        sums.append(jnp.sum(surface, axis=0, keepdims=True))
    centre = jnp.sum(jnp.concatenate(sums, axis=0), axis=1, keepdims=True) / float(n * n)
    squares = []
    tops = []
    for p in range(count):
        deviation = surfaces[p] - centre[p : p + 1]
        squares.append(jnp.sum(deviation * deviation, axis=0, keepdims=True))
        tops.append(jnp.max(surfaces[p], axis=0, keepdims=True))
    variance = jnp.sum(jnp.concatenate(squares, axis=0), axis=1, keepdims=True) / float(n * n)
    top = jnp.max(jnp.concatenate(tops, axis=0), axis=1, keepdims=True)
    scale = 2.0 / jnp.sqrt(variance + 1e-06)
    sub = lax.broadcasted_iota(jnp.int32, (n, n), 0)
    sub_coord = ((sub + n // 2) % n - n // 2).astype(F32)
    columns = []
    rows = []
    edges = []
    for p in range(count):
        e = jnp.exp((surfaces[p] - top[p : p + 1]) * scale[p : p + 1])
        columns.append(jnp.sum(e, axis=0, keepdims=True))
        rows.append(jnp.sum(e * sub_coord, axis=0, keepdims=True))
        edges.append(e[n // 2 : n // 2 + 1, :])
    columns = jnp.concatenate(columns, axis=0)
    rows = jnp.concatenate(rows, axis=0)
    edges = jnp.concatenate(edges, axis=0)
    lane = lax.broadcasted_iota(jnp.int32, (count, n), 1)
    lane_coord = ((lane + n // 2) % n - n // 2).astype(F32)

    def total(v):
        return jnp.sum(v, axis=1, keepdims=True)

    unit = float(n // 8)
    norm = 1.0 / total(columns)
    row_shift = total(rows) * norm / unit
    col_shift = total(columns * lane_coord) * norm / unit
    row_edge = total(edges) * norm * (float(n) / unit)
    col_edge = total(jnp.where(lane == n // 2, columns, 0.0)) * norm * (float(n) / unit)
    return row_shift, col_shift, -row_shift - row_edge, -col_shift - col_edge


MESH = pl.DeviceIdType.MESH


def stitch(
    colour_ref,
    offset_ref,
    live_ref,
    ids_ref,
    strips_hbm,
    col_hbm,
    row_hbm,
    inv_row_hbm,
    inv_col_hbm,
    out_ref,
    strips,
    col_ref,
    row_ref,
    inv_row_ref,
    inv_col_ref,
    shifted,
    sent,
    firsts,
    arrived,
    line,
    lines,
    tile_out,
    tiles,
    strip_sem,
    table_sem,
    window_send,
    window_recv,
    line_send,
    line_recv,
    tile_send,
    tile_recv,
    hello,
):
    n = PATCH
    rounds, blocks, layers = strips.shape[:3]
    slots = offset_ref.shape[3]
    half = slots // 2
    entries = rounds * slots
    groups = lax.axis_size("grp")
    tile_count = lax.axis_size("tiles")
    devices = tile_count * groups
    tile_index = lax.axis_index("tiles")
    group_index = lax.axis_index("grp")
    me = tile_index * groups + group_index
    strides = [1] + [tile_count // 2] * (rounds - 1)
    sides = [(tile_index // s) % 2 for s in strides]
    partners = [tile_index + s * (1 - 2 * side) for s, side in zip(strides, sides)]

    barrier = pltpu.get_barrier_semaphore()
    neighbours = []
    stride = 1
    while stride < tile_count:
        bit = (tile_index // stride) % 2
        neighbours.append((tile_index + stride * (1 - 2 * bit), group_index))
        stride *= 2
    stride = 1
    while stride < groups:
        bit = (group_index // stride) % 2
        neighbours.append((tile_index, group_index + stride * (1 - 2 * bit)))
        stride *= 2
    stages = len(neighbours)
    for at in neighbours:
        pl.semaphore_signal(barrier, inc=1, device_id=at, device_id_type=MESH)

    strip_loads = [
        pltpu.make_async_copy(strips_hbm.at[:, :, :, pl.ds(i * LANES, LANES)], strips.at[:, i], strip_sem)
        for i in range(blocks)
    ]
    for load in strip_loads:
        load.start()
    table_loads = [
        pltpu.make_async_copy(a, b, table_sem.at[i])
        for i, (a, b) in enumerate(
            [(col_hbm, col_ref), (row_hbm, row_ref), (inv_row_hbm, inv_row_ref), (inv_col_hbm, inv_col_ref)]
        )
    ]
    for load in table_loads:
        load.start()
    pltpu.make_async_copy(strips, strips, strip_sem).wait()

    def extract(r, picks):
        rests = []
        lane = lax.broadcasted_iota(jnp.int32, (n + SUB, LANES), 1)
        for i, k in enumerate(picks):
            row, column = offset_ref[0, r, 0, k], offset_ref[0, r, 1, k]
            block = jnp.minimum(lax.div(column, LANES), blocks - 2)
            layer = jnp.minimum(lax.div(row, SUB), layers - n // SUB - 1)
            shift = column - block * LANES
            turn = lax.rem(2 * LANES - shift, LANES)
            left, right = (
                pltpu.roll(
                    strips[colour_ref[0, r], block + side, pl.ds(layer, n // SUB + 1)]
                    .reshape(n + SUB, LANES)
                    .astype(F32),
                    turn,
                    1,
                )
                for side in range(2)
            )
            shifted[i] = jnp.where(lane < LANES - shift, left, right)
            rests.append(row - layer * SUB)
        return [shifted[i, pl.ds(rest, n), :].astype(BF16) for i, rest in enumerate(rests)]

    def window_copy(r, j):
        return pltpu.make_async_remote_copy(
            src_ref=sent.at[r, j],
            dst_ref=arrived.at[r, j],
            send_sem=window_send.at[r, j],
            recv_sem=window_recv.at[r, j],
            device_id=(partners[r], group_index),
            device_id_type=MESH,
        )

    def line_copy(r):
        return pltpu.make_async_remote_copy(
            src_ref=line,
            dst_ref=lines.at[r],
            send_sem=line_send.at[r],
            recv_sem=line_recv.at[r],
            device_id=(partners[r], group_index),
            device_id_type=MESH,
        )

    def produce(r, j):
        base = (1 - sides[r]) * half
        for i, window in enumerate(extract(r, [base + j + i for i in range(PAIR)])):
            sent[r, j + i] = window

    def launch(r, j):
        for i in range(PAIR):
            window_copy(r, j + i).start()

    produce(rounds - 1, 0)
    pl.semaphore_wait(barrier, stages)

    def step(p, carry):
        for r in reversed(range(rounds)):
            if r < rounds - 1:
                produce(r, p * PAIR)
                launch(r + 1, p * PAIR)
        produce(rounds - 1, p * PAIR + PAIR)
        launch(0, p * PAIR)
        return carry

    lane = lax.broadcasted_iota(jnp.int32, (1, LANES), 1)
    ids = jnp.zeros((1, LANES), jnp.int32)
    for r in range(rounds):
        for k in range(slots):
            node = jnp.where(k < live_ref[0, r], ids_ref[0, r, k], -1)
            ids = jnp.where(lane == r * slots + k, node, ids)
    line[...] = ids.astype(F32)
    lax.fori_loop(0, 1, step, 0)
    for r in range(rounds):
        line_copy(r).start()
    last = half - PAIR
    lax.fori_loop(1, half // PAIR - 1, step, 0)
    for r in reversed(range(rounds - 1)):
        produce(r, last)
        launch(r + 1, last)

    launch(0, last)
    for load in table_loads:
        load.wait()

    def prepare(r):
        def step(p, carry):
            j = p * PAIR
            windows = extract(r, [sides[r] * half + j + i for i in range(PAIR)])
            for q in range(0, PAIR, 2):
                pair = spectra(windows[q : q + 2], col_ref[...], row_ref[...])
                for i in range(2):
                    for c in range(2):
                        firsts[r, j + q + i, c] = pair[i][c]
            return carry

        return step

    for r in range(rounds):
        lax.fori_loop(0, half // PAIR, prepare(r), 0)

    def hail(stage):
        pl.semaphore_signal(hello.at[stage], inc=1, device_id=neighbours[stage], device_id_type=MESH)

    def greet(stage):
        if stage > 0:
            pl.semaphore_wait(hello.at[stage - 1], 1)
        if stage < stages:
            hail(stage)

    def work(r, j, count, carry):
        for i in range(count):
            pltpu.make_async_remote_copy(
                src_ref=sent.at[r, j + i],
                dst_ref=arrived.at[r, j + i],
                send_sem=window_send.at[r, j + i],
                recv_sem=window_recv.at[r, j + i],
                device_id=(partners[r], group_index),
                device_id_type=MESH,
            ).wait_recv()
        seconds = []
        for p in range(0, count, 2):
            seconds += spectra([arrived[r, j + i] for i in range(p, min(p + 2, count))], col_ref[...], row_ref[...])
        a, b, c, d = correlate(
            [(firsts[r, j + i, 0], firsts[r, j + i, 1]) for i in range(count)],
            seconds,
            inv_row_ref[...],
            inv_col_ref[...],
        )
        own = r * slots + sides[r] * half + j
        other = r * slots + (1 - sides[r]) * half + j
        return (
            carry
            + row_place(a, own)
            + row_place(c, other)
            + row_place(b, own + entries)
            + row_place(d, other + entries)
        )

    disp = jnp.zeros((1, LANES), F32)
    plan = [(r, j, GROUP) for r in range(rounds) for j in range(0, half, GROUP)]
    plan = plan[:-1] + [(rounds - 1, half - GROUP + i, c) for i, c in LAST]
    stage = 0
    for r, j, count in plan:
        if stage <= stages:
            greet(stage)
            stage += 1
        disp = work(r, j, count, disp)
        if (r, j) == (rounds - 1, 0):
            for s in range(rounds):
                line_copy(s).wait()
            ids = line[...]
            id_line = jnp.zeros((1, LANES), F32)
            for s in range(rounds):
                theirs = pltpu.roll(lines[s], jnp.where(sides[s] == 0, half, LANES - half), 1)
                in_round = (lane >= s * slots) & (lane < (s + 1) * slots)
                mine = (lane // half) % 2 == sides[s]
                id_line = id_line + jnp.where(in_round, jnp.where(mine, ids, theirs), 0.0)
            disp = disp + pltpu.roll(id_line, 2 * entries, 1)
    while stage <= stages:
        greet(stage)
        stage += 1

    tile_out[...] = disp
    tiles[me] = disp

    def start(i, carry):
        to = i + jnp.where(i >= me, 1, 0)
        pltpu.make_async_remote_copy(
            src_ref=tile_out,
            dst_ref=tiles.at[me],
            send_sem=tile_send,
            recv_sem=tile_recv,
            device_id=(to // groups, to % groups),
            device_id_type=MESH,
        ).start()
        return carry

    lax.fori_loop(0, devices - 1, start, 0)
    for r in range(rounds):
        for j in range(half):
            window_copy(r, j).wait_send()
    everyone = pltpu.make_async_remote_copy(
        src_ref=tiles.at[pl.ds(0, devices - 1)],
        dst_ref=tiles.at[pl.ds(0, devices - 1)],
        send_sem=tile_send,
        recv_sem=tile_recv,
        device_id=neighbours[0],
        device_id_type=MESH,
    )
    everyone.wait_recv()

    pack = LANES // entries
    node = lax.broadcasted_iota(jnp.int32, (NODE_DEV, LANES), 0).astype(F32)
    first_node = (me * NODE_DEV).astype(F32)
    lane = lax.broadcasted_iota(jnp.int32, (1, LANES), 1)
    onehots = []
    values = []
    for g in range(devices // pack):
        parts = [jnp.zeros((1, LANES), F32)] * 3
        for i in range(pack):
            tile = tiles[g * pack + i]
            here = (lane >= i * entries) & (lane < (i + 1) * entries)
            for c in range(3):
                moved = pltpu.roll(tile, ((i - c) * entries) % LANES, 1) if i != c else tile
                parts[c] = jnp.where(here, moved, parts[c])
        onehots.append(jnp.where(parts[2] - first_node == node, 1.0, 0.0).astype(BF16))
        tile = jnp.concatenate(parts[:2], axis=0)
        hi = tile.astype(BF16).astype(F32)
        rest = tile - hi
        mid = rest.astype(BF16).astype(F32)
        values.append(jnp.concatenate([hi, mid, rest - mid, jnp.zeros_like(hi)], axis=0).astype(BF16))
    result = lax.dot_general(
        jnp.concatenate(values, axis=1),
        jnp.concatenate(onehots, axis=1),
        (((1,), (1,)), ((), ())),
        preferred_element_type=F32,
    )
    out_ref[0:2] = result[0:2]
    out_ref[2:4] = result[2:4] + result[4:6]
    everyone.wait_send()


def on_device(strips, edge_colour, patch_offsets, patch_live, node_ids):
    rounds, height, width = strips.shape
    n = PATCH
    slot_count = patch_offsets.shape[2]
    half = slot_count // 2
    devices = lax.axis_size("tiles") * lax.axis_size("grp")
    whole = pl.BlockSpec(memory_space=VMEM)
    anywhere = pl.BlockSpec(memory_space=pl.ANY)
    sem = pltpu.SemaphoreType.DMA
    windows = (rounds, half, n, n)
    scalars = [jnp.transpose(patch_offsets, (0, 1, 3, 2)), edge_colour, patch_live, node_ids]
    constants = [jnp.asarray(t) for t in tables()]
    sums = pl.pallas_call(
        stitch,
        out_shape=jax.ShapeDtypeStruct((4, NODE_DEV), F32),
        in_specs=[pl.BlockSpec(memory_space=SMEM)] * 4 + [anywhere] * 5,
        out_specs=whole,
        scratch_shapes=[
            pltpu.VMEM((rounds, width // LANES, height // SUB, SUB, LANES), BF16),
            *(pltpu.VMEM(t.shape, BF16) for t in constants),
            pltpu.VMEM((PAIR, n + 16, n), F32),
            pltpu.VMEM(windows, BF16),
            pltpu.VMEM((rounds, half, 2, n, n), F32),
            pltpu.VMEM(windows, BF16),
            pltpu.VMEM((1, LANES), F32),
            pltpu.VMEM((rounds, 1, LANES), F32),
            pltpu.VMEM((1, LANES), F32),
            pltpu.VMEM((devices, 1, LANES), F32),
            sem(()),
            sem((4,)),
            sem((rounds, half)),
            sem((rounds, half)),
            sem((rounds,)),
            sem((rounds,)),
            sem(()),
            sem(()),
            pltpu.SemaphoreType.REGULAR((devices.bit_length() - 1,)),
        ],
        compiler_params=pltpu.CompilerParams(collective_id=0, has_side_effects=True, vmem_limit_bytes=VMEM_LIMIT),
        name="stitch",
    )(edge_colour, scalars[0], patch_live, node_ids, strips.reshape(rounds, height // SUB, SUB, width), *constants)
    return sums[0:2] + sums[2:4]


def solution(mesh):
    placed = (
        P(("tiles", "grp"), None, None),
        P(("tiles", "grp"), None),
        P(("tiles", "grp"), None, None, None),
        P(("tiles", "grp"), None),
        P(("tiles", "grp"), None, None),
    )
    return jax.shard_map(
        on_device, mesh=mesh, in_specs=placed, out_specs=P(None, ("tiles", "grp")), check_vma=False
    )
```

```python
import functools
import math

import jax
import jax.numpy as jnp
import numpy as np
from jax import lax
from jax.experimental import pallas as pl
from jax.experimental.pallas import tpu as pltpu
from jax.sharding import PartitionSpec as P

PATCH = 128
NODE_DEV = 128
LANES = 128
GROUP = 4
PAIR = 2
SUB = 16
LAST = ((0, 4),)
VMEM_LIMIT = 67043328 - 16384

F32 = jnp.float32
BF16 = jnp.bfloat16
VMEM = pltpu.MemorySpace.VMEM
SMEM = pltpu.MemorySpace.SMEM


def split_np(x):
    hi = np.asarray(x, np.float32).astype(BF16)
    lo = (np.asarray(x, np.float64) - hi.astype(np.float64)).astype(np.float32).astype(BF16)
    return hi, lo


def tables():
    n = PATCH
    h = n // 2
    j = np.arange(n)
    angle = 2.0 * math.pi / n * ((j[:, None] * j[None, :]) % n)
    c, s = np.cos(angle), np.sin(angle)
    rhi, rlo = split_np(np.concatenate([c[: h + 1], s[1:h]], axis=0))
    fore_row = np.concatenate([rhi, rlo], axis=1)
    chi, clo = split_np(np.block([[c, -s], [-s, -c]]))
    fore_col = np.concatenate([chi, clo, chi], axis=0)
    bhi, blo = split_np(np.block([[c, s], [-s, c]]))
    back_col = np.concatenate([bhi, blo, bhi], axis=0)
    weight = np.where(j[:h] == 0, 1.0, 2.0)[None, :]
    ihi, ilo = split_np(np.concatenate([weight * c[:, :h], c[:, h : h + 1], -2.0 * s[:, 1:h]], axis=1) / float(n * n))
    back_row = np.concatenate([ihi, ilo, ihi], axis=1)
    return fore_row, fore_col, back_col, back_row


def split(x):
    hi = x.astype(BF16)
    return hi, (x - hi.astype(F32)).astype(BF16)


def dot(a, b):
    return jnp.dot(a, b, preferred_element_type=F32)


def row_place(column, base):
    count = column.shape[0]
    lane = lax.broadcasted_iota(jnp.int32, (count, LANES), 1)
    sub = lax.broadcasted_iota(jnp.int32, (count, LANES), 0)
    return jnp.sum(jnp.where(lane == sub + base, column, 0.0), axis=0, keepdims=True)


def triple(x):
    hi, lo = split(x)
    return jnp.concatenate([hi, hi, lo], axis=1)


def gather_rows(rows):
    sub = lax.broadcasted_iota(jnp.int32, (8, LANES), 0)
    out = jnp.zeros((8, LANES), F32)
    for i, row in enumerate(rows):
        out = jnp.where(sub == i, row, out)
    return out


def spectra(windows, fore_row, fore_col):
    n = PATCH
    h = n // 2
    count = len(windows)
    first = lax.broadcasted_iota(jnp.int32, (8, n), 0) == 0
    mains = []
    middles = []
    for p in range(0, count, 2):
        x = jnp.concatenate(windows[p : p + 2], axis=1)
        y = dot(fore_row, jnp.concatenate([x, x], axis=0))
        for i in range(2):
            part = y[:, i * n : (i + 1) * n]
            middles.append(part[h : h + 1])
            sine = jnp.concatenate([jnp.where(first, 0.0, part[h : h + 8]), part[h + 8 :]], axis=0)
            mains.append(jnp.concatenate([part[:h], sine], axis=1))
    middle = gather_rows(middles)
    mains.append(jnp.concatenate([jnp.concatenate([middle, jnp.zeros_like(middle)], axis=1)] * 2, axis=0))
    f = dot(jnp.concatenate([triple(m) for m in mains], axis=0), fore_col)
    main = [(f[i * h : (i + 1) * h, :n], f[i * h : (i + 1) * h, n:]) for i in range(count)]
    return main, (f[count * h : count * h + 8, :n], f[count * h : count * h + 8, n:])


def fold(v):
    return sum(v[i : i + 8] for i in range(8, v.shape[0], 8)) + v[:8]


def whiten_terms(first, second):
    (r1, i1), (r2, i2) = first, second
    cross_r = r1 * r2 + i1 * i2
    cross_i = i1 * r2 - r1 * i2
    return cross_r, cross_i, jnp.sqrt(cross_r * cross_r + cross_i * cross_i)


def total(v):
    return jnp.sum(v, axis=1, keepdims=True)


def correlate(first, second, back_row, back_col):
    n = PATCH
    h = n // 2
    cells = float(n * n)
    count = len(first[0])
    terms = [whiten_terms(a, b) for a, b in zip(first[0], second[0])]
    middle = whiten_terms(first[1], second[1])

    def spectrum_sum(values, middle_value):
        folded = jnp.concatenate([jnp.sum(fold(v), axis=0, keepdims=True) for v in values], axis=0)
        edge = jnp.concatenate([v[:1] for v in values], axis=0)
        return 2.0 * folded - edge + middle_value[:count], edge

    mag_sum, _ = spectrum_sum([t[2] for t in terms], middle[2])
    extra = 0.1 * (total(mag_sum) / cells) + 1e-06
    inverses = [1.0 / (t[2] + extra[p : p + 1]) for p, t in enumerate(terms)]
    middle_inverse = 1.0 / (middle[2] + gather_rows([extra[p : p + 1] for p in range(count)]))
    rows = [jnp.concatenate([t[0] * v, t[1] * v], axis=1) for t, v in zip(terms, inverses)]
    middle_row = jnp.concatenate([middle[0] * middle_inverse, middle[1] * middle_inverse], axis=1)
    rows.append(jnp.concatenate([middle_row, middle_row], axis=0))

    def power(m, v):
        return (m * v) * (m * v)

    power_sum, edge = spectrum_sum(
        [power(t[2], v) for t, v in zip(terms, inverses)], power(middle[2], middle_inverse)
    )
    lane = lax.broadcasted_iota(jnp.int32, (count, n), 1)
    variance = total(power_sum - jnp.where(lane == 0, edge, 0.0)) / (cells * cells)
    scale = 2.0 / jnp.sqrt(variance + 1e-06) * math.log2(math.e)

    back = dot(jnp.concatenate([triple(r) for r in rows], axis=0), back_col)
    middle_back = back[count * h : count * h + 8, :n]
    first_row = lax.broadcasted_iota(jnp.int32, (8, n), 0) == 0
    surfaces = []
    for p in range(0, count, 2):
        columns = []
        for q in range(p, p + 2):
            part = back[q * h : (q + 1) * h]
            imag = part[:, n:]
            head = jnp.where(first_row, middle_back[q : q + 1], imag[:8])
            columns.append(jnp.concatenate([part[:, :n], head, imag[8:]], axis=0))
        hi, lo = split(jnp.concatenate(columns, axis=1))
        wide = dot(back_row, jnp.concatenate([hi, hi, lo], axis=0))
        surfaces += [wide[:, :n], wide[:, n:]]

    tops = []
    for surface in surfaces:
        peak = surface[:8]
        for i in range(8, n, 8):
            peak = jnp.maximum(peak, surface[i : i + 8])
        tops.append(jnp.max(peak, axis=0, keepdims=True))
    top = jnp.max(jnp.concatenate(tops, axis=0), axis=1, keepdims=True)
    sub = lax.broadcasted_iota(jnp.int32, (8, n), 0).astype(F32)
    columns = []
    rows = []
    edges = []
    for p in range(count):
        e = jnp.exp2((surfaces[p] - top[p : p + 1]) * scale[p : p + 1])
        part = [e[i : i + 8] for i in range(0, n, 8)]
        upper = part[h // 8 - 1]
        step = upper
        for v in part[h // 8 - 2 : 0 : -1]:
            upper = upper + v
            step = step + upper
        upper = upper + part[0]
        lower = part[h // 8]
        down = lower
        for v in part[h // 8 + 1 :]:
            lower = lower + v
            down = down + lower
        column = upper + lower
        columns.append(jnp.sum(column, axis=0, keepdims=True))
        rows.append(jnp.sum(8.0 * (step - down) + sub * column, axis=0, keepdims=True))
        edges.append(e[h : h + 1, :])
    columns = jnp.concatenate(columns, axis=0)
    rows = jnp.concatenate(rows, axis=0)
    edges = jnp.concatenate(edges, axis=0)
    lane_coord = ((lane + h) % n - h).astype(F32)
    unit = float(n // 8)
    norm = 1.0 / total(columns)
    row_shift = total(rows) * norm / unit
    col_shift = total(columns * lane_coord) * norm / unit
    row_edge = total(edges) * norm * (float(n) / unit)
    col_edge = total(jnp.where(lane == h, columns, 0.0)) * norm * (float(n) / unit)
    return row_shift, col_shift, -row_shift - row_edge, -col_shift - col_edge


MESH = pl.DeviceIdType.MESH


def stitch(
    colour_ref,
    offset_ref,
    live_ref,
    ids_ref,
    strips_hbm,
    fore_row_hbm,
    fore_col_hbm,
    back_col_hbm,
    back_row_hbm,
    out_ref,
    strips,
    fore_row_ref,
    fore_col_ref,
    back_col_ref,
    back_row_ref,
    shifted,
    sent,
    firsts,
    middles,
    arrived,
    line,
    lines,
    tile_out,
    tiles,
    strip_sem,
    table_sem,
    window_send,
    window_recv,
    line_send,
    line_recv,
    tile_send,
    tile_recv,
    hello,
):
    n = PATCH
    rounds, blocks, layers = strips.shape[:3]
    slots = offset_ref.shape[3]
    half = slots // 2
    entries = rounds * slots
    groups = lax.axis_size("grp")
    tile_count = lax.axis_size("tiles")
    devices = tile_count * groups
    tile_index = lax.axis_index("tiles")
    group_index = lax.axis_index("grp")
    me = tile_index * groups + group_index
    strides = [1] + [tile_count // 2] * (rounds - 1)
    sides = [(tile_index // s) % 2 for s in strides]
    partners = [tile_index + s * (1 - 2 * side) for s, side in zip(strides, sides)]

    barrier = pltpu.get_barrier_semaphore()
    neighbours = []
    stride = 1
    while stride < tile_count:
        bit = (tile_index // stride) % 2
        neighbours.append((tile_index + stride * (1 - 2 * bit), group_index))
        stride *= 2
    stride = 1
    while stride < groups:
        bit = (group_index // stride) % 2
        neighbours.append((tile_index, group_index + stride * (1 - 2 * bit)))
        stride *= 2
    stages = len(neighbours)
    for at in neighbours:
        pl.semaphore_signal(barrier, inc=1, device_id=at, device_id_type=MESH)

    strip_loads = [
        pltpu.make_async_copy(strips_hbm.at[:, :, :, pl.ds(i * LANES, LANES)], strips.at[:, i], strip_sem)
        for i in range(blocks)
    ]
    for load in strip_loads:
        load.start()
    table_loads = [
        pltpu.make_async_copy(a, b, table_sem.at[i])
        for i, (a, b) in enumerate(
            [(fore_row_hbm, fore_row_ref), (fore_col_hbm, fore_col_ref), (back_col_hbm, back_col_ref), (back_row_hbm, back_row_ref)]
        )
    ]
    for load in table_loads:
        load.start()
    pltpu.make_async_copy(strips, strips, strip_sem).wait()

    def extract(r, picks):
        rests = []
        lane = lax.broadcasted_iota(jnp.int32, (n + SUB, LANES), 1)
        for i, k in enumerate(picks):
            row, column = offset_ref[0, r, 0, k], offset_ref[0, r, 1, k]
            block = jnp.minimum(lax.div(column, LANES), blocks - 2)
            layer = jnp.minimum(lax.div(row, SUB), layers - n // SUB - 1)
            shift = column - block * LANES
            turn = lax.rem(2 * LANES - shift, LANES)
            left, right = (
                pltpu.roll(
                    strips[colour_ref[0, r], block + side, pl.ds(layer, n // SUB + 1)]
                    .reshape(n + SUB, LANES)
                    .astype(F32),
                    turn,
                    1,
                )
                for side in range(2)
            )
            shifted[i] = jnp.where(lane < LANES - shift, left, right)
            rests.append(row - layer * SUB)
        return [shifted[i, pl.ds(rest, n), :].astype(BF16) for i, rest in enumerate(rests)]

    def window_copy(r, j):
        return pltpu.make_async_remote_copy(
            src_ref=sent.at[r, j],
            dst_ref=arrived.at[r, j],
            send_sem=window_send.at[r, j],
            recv_sem=window_recv.at[r, j],
            device_id=(partners[r], group_index),
            device_id_type=MESH,
        )

    def line_copy(r):
        return pltpu.make_async_remote_copy(
            src_ref=line,
            dst_ref=lines.at[r],
            send_sem=line_send.at[r],
            recv_sem=line_recv.at[r],
            device_id=(partners[r], group_index),
            device_id_type=MESH,
        )

    def produce(r, j):
        base = (1 - sides[r]) * half
        for i, window in enumerate(extract(r, [base + j + i for i in range(PAIR)])):
            sent[r, j + i] = window

    def launch(r, j):
        for i in range(PAIR):
            window_copy(r, j + i).start()

    produce(rounds - 1, 0)
    pl.semaphore_wait(barrier, stages)

    def step(p, carry):
        for r in reversed(range(rounds)):
            if r < rounds - 1:
                produce(r, p * PAIR)
                launch(r + 1, p * PAIR)
        produce(rounds - 1, p * PAIR + PAIR)
        launch(0, p * PAIR)
        return carry

    lane = lax.broadcasted_iota(jnp.int32, (1, LANES), 1)
    ids = jnp.zeros((1, LANES), jnp.int32)
    for r in range(rounds):
        for k in range(slots):
            node = jnp.where(k < live_ref[0, r], ids_ref[0, r, k], -1)
            ids = jnp.where(lane == r * slots + k, node, ids)
    line[...] = ids.astype(F32)
    lax.fori_loop(0, 1, step, 0)
    for r in range(rounds):
        line_copy(r).start()
    last = half - PAIR
    lax.fori_loop(1, half // PAIR - 1, step, 0)
    for r in reversed(range(rounds - 1)):
        produce(r, last)
        launch(r + 1, last)

    launch(0, last)
    for load in table_loads:
        load.wait()

    def prepare(r):
        def step(g, carry):
            j = g * GROUP
            windows = extract(r, [sides[r] * half + j + i for i in range(GROUP)])
            main, middle = spectra(windows, fore_row_ref[...], fore_col_ref[...])
            for c in range(2):
                for i in range(GROUP):
                    firsts[r, j + i, c] = main[i][c]
                middles[r, g, c] = middle[c]
            return carry

        return step

    for r in range(rounds):
        lax.fori_loop(0, half // GROUP, prepare(r), 0)

    def hail(stage):
        pl.semaphore_signal(hello.at[stage], inc=1, device_id=neighbours[stage], device_id_type=MESH)

    def greet(stage):
        if stage > 0:
            pl.semaphore_wait(hello.at[stage - 1], 1)
        if stage < stages:
            hail(stage)

    def work(r, j, count, carry):
        for i in range(count):
            pltpu.make_async_remote_copy(
                src_ref=sent.at[r, j + i],
                dst_ref=arrived.at[r, j + i],
                send_sem=window_send.at[r, j + i],
                recv_sem=window_recv.at[r, j + i],
                device_id=(partners[r], group_index),
                device_id_type=MESH,
            ).wait_recv()
        g = j // GROUP
        seconds = spectra([arrived[r, j + i] for i in range(count)], fore_row_ref[...], fore_col_ref[...])
        a, b, c, d = correlate(
            ([(firsts[r, j + i, 0], firsts[r, j + i, 1]) for i in range(count)], (middles[r, g, 0], middles[r, g, 1])),
            seconds,
            back_row_ref[...],
            back_col_ref[...],
        )
        own = r * slots + sides[r] * half + j
        other = r * slots + (1 - sides[r]) * half + j
        return (
            carry
            + row_place(a, own)
            + row_place(c, other)
            + row_place(b, own + entries)
            + row_place(d, other + entries)
        )

    disp = jnp.zeros((1, LANES), F32)
    plan = [(r, j, GROUP) for r in range(rounds) for j in range(0, half, GROUP)]
    plan = plan[:-1] + [(rounds - 1, half - GROUP + i, c) for i, c in LAST]
    stage = 0
    for r, j, count in plan:
        if stage <= stages:
            greet(stage)
            stage += 1
        disp = work(r, j, count, disp)
        if (r, j) == (rounds - 1, 0):
            for s in range(rounds):
                line_copy(s).wait()
            ids = line[...]
            id_line = jnp.zeros((1, LANES), F32)
            for s in range(rounds):
                theirs = pltpu.roll(lines[s], jnp.where(sides[s] == 0, half, LANES - half), 1)
                in_round = (lane >= s * slots) & (lane < (s + 1) * slots)
                mine = (lane // half) % 2 == sides[s]
                id_line = id_line + jnp.where(in_round, jnp.where(mine, ids, theirs), 0.0)
            disp = disp + pltpu.roll(id_line, 2 * entries, 1)
    while stage <= stages:
        greet(stage)
        stage += 1

    tile_out[...] = disp
    tiles[me] = disp

    def start(i, carry):
        to = i + jnp.where(i >= me, 1, 0)
        pltpu.make_async_remote_copy(
            src_ref=tile_out,
            dst_ref=tiles.at[me],
            send_sem=tile_send,
            recv_sem=tile_recv,
            device_id=(to // groups, to % groups),
            device_id_type=MESH,
        ).start()
        return carry

    lax.fori_loop(0, devices - 1, start, 0)
    for r in range(rounds):
        for j in range(half):
            window_copy(r, j).wait_send()
    everyone = pltpu.make_async_remote_copy(
        src_ref=tiles.at[pl.ds(0, devices - 1)],
        dst_ref=tiles.at[pl.ds(0, devices - 1)],
        send_sem=tile_send,
        recv_sem=tile_recv,
        device_id=neighbours[0],
        device_id_type=MESH,
    )
    everyone.wait_recv()

    pack = LANES // entries
    node = lax.broadcasted_iota(jnp.int32, (NODE_DEV, LANES), 0).astype(F32)
    first_node = (me * NODE_DEV).astype(F32)
    lane = lax.broadcasted_iota(jnp.int32, (1, LANES), 1)
    onehots = []
    values = []
    for g in range(devices // pack):
        parts = [jnp.zeros((1, LANES), F32)] * 3
        for i in range(pack):
            tile = tiles[g * pack + i]
            here = (lane >= i * entries) & (lane < (i + 1) * entries)
            for c in range(3):
                moved = pltpu.roll(tile, ((i - c) * entries) % LANES, 1) if i != c else tile
                parts[c] = jnp.where(here, moved, parts[c])
        onehots.append(jnp.where(parts[2] - first_node == node, 1.0, 0.0).astype(BF16))
        tile = jnp.concatenate(parts[:2], axis=0)
        hi = tile.astype(BF16).astype(F32)
        rest = tile - hi
        mid = rest.astype(BF16).astype(F32)
        values.append(jnp.concatenate([hi, mid, rest - mid, jnp.zeros_like(hi)], axis=0).astype(BF16))
    result = lax.dot_general(
        jnp.concatenate(values, axis=1),
        jnp.concatenate(onehots, axis=1),
        (((1,), (1,)), ((), ())),
        preferred_element_type=F32,
    )
    out_ref[0:2] = result[0:2]
    out_ref[2:4] = result[2:4] + result[4:6]
    everyone.wait_send()


def on_device(strips, edge_colour, patch_offsets, patch_live, node_ids):
    rounds, height, width = strips.shape
    n = PATCH
    slot_count = patch_offsets.shape[2]
    half = slot_count // 2
    devices = lax.axis_size("tiles") * lax.axis_size("grp")
    whole = pl.BlockSpec(memory_space=VMEM)
    anywhere = pl.BlockSpec(memory_space=pl.ANY)
    sem = pltpu.SemaphoreType.DMA
    windows = (rounds, half, n, n)
    scalars = [jnp.transpose(patch_offsets, (0, 1, 3, 2)), edge_colour, patch_live, node_ids]
    constants = [jnp.asarray(t) for t in tables()]
    sums = pl.pallas_call(
        stitch,
        out_shape=jax.ShapeDtypeStruct((4, NODE_DEV), F32),
        in_specs=[pl.BlockSpec(memory_space=SMEM)] * 4 + [anywhere] * 5,
        out_specs=whole,
        scratch_shapes=[
            pltpu.VMEM((rounds, width // LANES, height // SUB, SUB, LANES), BF16),
            *(pltpu.VMEM(t.shape, BF16) for t in constants),
            pltpu.VMEM((GROUP, n + 16, n), F32),
            pltpu.VMEM(windows, BF16),
            pltpu.VMEM((rounds, half, 2, n // 2, n), F32),
            pltpu.VMEM((rounds, half // GROUP, 2, 8, n), F32),
            pltpu.VMEM(windows, BF16),
            pltpu.VMEM((1, LANES), F32),
            pltpu.VMEM((rounds, 1, LANES), F32),
            pltpu.VMEM((1, LANES), F32),
            pltpu.VMEM((devices, 1, LANES), F32),
            sem(()),
            sem((4,)),
            sem((rounds, half)),
            sem((rounds, half)),
            sem((rounds,)),
            sem((rounds,)),
            sem(()),
            sem(()),
            pltpu.SemaphoreType.REGULAR((devices.bit_length() - 1,)),
        ],
        compiler_params=pltpu.CompilerParams(collective_id=0, has_side_effects=True, vmem_limit_bytes=VMEM_LIMIT),
        name="stitch",
    )(edge_colour, scalars[0], patch_live, node_ids, strips.reshape(rounds, height // SUB, SUB, width), *constants)
    return sums[0:2] + sums[2:4]


def solution(mesh):
    placed = (
        P(("tiles", "grp"), None, None),
        P(("tiles", "grp"), None),
        P(("tiles", "grp"), None, None, None),
        P(("tiles", "grp"), None),
        P(("tiles", "grp"), None, None),
    )
    return jax.shard_map(
        on_device, mesh=mesh, in_specs=placed, out_specs=P(None, ("tiles", "grp")), check_vma=False
    )
```

```python
import functools
import math

import jax
import jax.numpy as jnp
import numpy as np
from jax import lax
from jax.experimental import pallas as pl
from jax.experimental.pallas import tpu as pltpu
from jax.sharding import PartitionSpec as P

PATCH = 128
NODE_DEV = 128
LANES = 128
GROUP = 4
PAIR = 2
SUB = 8
DOT = 2
VMEM_LIMIT = 67043328 - 16384

F32 = jnp.float32
BF16 = jnp.bfloat16
VMEM = pltpu.MemorySpace.VMEM
SMEM = pltpu.MemorySpace.SMEM


def split_np(x):
    hi = np.asarray(x, np.float32).astype(BF16)
    lo = (np.asarray(x, np.float64) - hi.astype(np.float64)).astype(np.float32).astype(BF16)
    return hi, lo


def tables():
    n = PATCH
    h = n // 2
    j = np.arange(n)
    angle = 2.0 * math.pi / n * ((j[:, None] * j[None, :]) % n)
    c, s = np.cos(angle), np.sin(angle)
    rhi, rlo = split_np(np.concatenate([c[: h + 1], s[1:h]], axis=0))
    fore_row = np.concatenate([rhi, rlo], axis=1)
    chi, clo = split_np(np.block([[c, -s], [-s, -c]]))
    fore_col = np.concatenate([chi, clo, chi], axis=0)
    bhi, blo = split_np(np.block([[c, s], [-s, c]]))
    back_col = np.concatenate([bhi, blo, bhi], axis=0)
    weight = np.where(j[:h] == 0, 1.0, 2.0)[None, :]
    ihi, ilo = split_np(np.concatenate([weight * c[:, :h], c[:, h : h + 1], -2.0 * s[:, 1:h]], axis=1) / float(n * n))
    back_row = np.concatenate([ihi, ilo, ihi], axis=1)
    return fore_row, fore_col, back_col, back_row


def split(x):
    hi = x.astype(BF16)
    return hi, (x - hi.astype(F32)).astype(BF16)


def dot(a, b):
    return jnp.dot(a, b, preferred_element_type=F32)


def row_place(column, base):
    count = column.shape[0]
    lane = lax.broadcasted_iota(jnp.int32, (count, LANES), 1)
    sub = lax.broadcasted_iota(jnp.int32, (count, LANES), 0)
    return jnp.sum(jnp.where(lane == sub + base, column, 0.0), axis=0, keepdims=True)


def triple(x):
    hi, lo = split(x)
    return jnp.concatenate([hi, hi, lo], axis=1)


def apply(rows, table):
    out = []
    for p in range(0, len(rows), DOT):
        some = rows[p : p + DOT] if len(rows) - p > DOT + 1 else rows[p:]
        y = dot(jnp.concatenate([triple(v) for v in some], axis=0), table)
        at = 0
        for v in some:
            out.append(y[at : at + v.shape[0]])
            at += v.shape[0]
        if p + len(some) == len(rows):
            return out


def gather_rows(rows):
    sub = lax.broadcasted_iota(jnp.int32, (8, LANES), 0)
    out = jnp.zeros((8, LANES), F32)
    for i, row in enumerate(rows):
        out = jnp.where(sub == i, row, out)
    return out


def spectra(windows, fore_row, fore_col):
    n = PATCH
    h = n // 2
    count = len(windows)
    first = lax.broadcasted_iota(jnp.int32, (8, n), 0) == 0
    mains = []
    middles = []
    for p in range(0, count, 2):
        x = jnp.concatenate(windows[p : p + 2], axis=1)
        y = dot(fore_row, jnp.concatenate([x, x], axis=0))
        for i in range(2):
            part = y[:, i * n : (i + 1) * n]
            middles.append(part[h : h + 1])
            sine = jnp.concatenate([jnp.where(first, 0.0, part[h : h + 8]), part[h + 8 :]], axis=0)
            mains.append(jnp.concatenate([part[:h], sine], axis=1))
    middle = gather_rows(middles)
    mains.append(jnp.concatenate([jnp.concatenate([middle, jnp.zeros_like(middle)], axis=1)] * 2, axis=0))
    parts = apply(mains, fore_col)
    main = [(f[:, :n], f[:, n:]) for f in parts[:-1]]
    return main, (parts[-1][:8, :n], parts[-1][:8, n:])


def fold(v):
    return sum(v[i : i + 8] for i in range(8, v.shape[0], 8)) + v[:8]


def whiten_terms(first, second):
    (r1, i1), (r2, i2) = first, second
    cross_r = r1 * r2 + i1 * i2
    cross_i = i1 * r2 - r1 * i2
    return cross_r, cross_i, jnp.sqrt(cross_r * cross_r + cross_i * cross_i)


def total(v):
    return jnp.sum(v, axis=1, keepdims=True)


def correlate(first, second, back_row, back_col):
    n = PATCH
    h = n // 2
    cells = float(n * n)
    count = len(first[0])
    terms = [whiten_terms(a, b) for a, b in zip(first[0], second[0])]
    middle = whiten_terms(first[1], second[1])

    def spectrum_sum(values, middle_value):
        folded = jnp.concatenate([jnp.sum(fold(v), axis=0, keepdims=True) for v in values], axis=0)
        edge = jnp.concatenate([v[:1] for v in values], axis=0)
        return 2.0 * folded - edge + middle_value[:count], edge

    mag_sum, _ = spectrum_sum([t[2] for t in terms], middle[2])
    extra = 0.1 * (total(mag_sum) / cells) + 1e-06
    inverses = [1.0 / (t[2] + extra[p : p + 1]) for p, t in enumerate(terms)]
    middle_inverse = 1.0 / (middle[2] + gather_rows([extra[p : p + 1] for p in range(count)]))
    rows = [jnp.concatenate([t[0] * v, t[1] * v], axis=1) for t, v in zip(terms, inverses)]
    middle_row = jnp.concatenate([middle[0] * middle_inverse, middle[1] * middle_inverse], axis=1)
    rows.append(jnp.concatenate([middle_row, middle_row], axis=0))

    def power(m, v):
        return (m * v) * (m * v)

    power_sum, edge = spectrum_sum(
        [power(t[2], v) for t, v in zip(terms, inverses)], power(middle[2], middle_inverse)
    )
    lane = lax.broadcasted_iota(jnp.int32, (count, n), 1)
    variance = total(power_sum - jnp.where(lane == 0, edge, 0.0)) / (cells * cells)
    scale = 2.0 / jnp.sqrt(variance + 1e-06) * math.log2(math.e)

    back = apply(rows, back_col)
    middle_back = back[-1][:8, :n]
    first_row = lax.broadcasted_iota(jnp.int32, (8, n), 0) == 0
    surfaces = []
    for p in range(0, count, 2):
        columns = []
        for q in range(p, p + 2):
            part = back[q]
            imag = part[:, n:]
            head = jnp.where(first_row, middle_back[q : q + 1], imag[:8])
            columns.append(jnp.concatenate([part[:, :n], head, imag[8:]], axis=0))
        hi, lo = split(jnp.concatenate(columns, axis=1))
        wide = dot(back_row, jnp.concatenate([hi, hi, lo], axis=0))
        surfaces += [wide[:, :n], wide[:, n:]]

    tops = []
    for surface in surfaces:
        peak = surface[:8]
        for i in range(8, n, 8):
            peak = jnp.maximum(peak, surface[i : i + 8])
        tops.append(jnp.max(peak, axis=0, keepdims=True))
    top = jnp.max(jnp.concatenate(tops, axis=0), axis=1, keepdims=True)
    sub = lax.broadcasted_iota(jnp.int32, (8, n), 0).astype(F32)
    columns = []
    rows = []
    edges = []
    for p in range(count):
        e = jnp.exp2((surfaces[p] - top[p : p + 1]) * scale[p : p + 1])
        part = [e[i : i + 8] for i in range(0, n, 8)]
        upper = part[h // 8 - 1]
        step = upper
        for v in part[h // 8 - 2 : 0 : -1]:
            upper = upper + v
            step = step + upper
        upper = upper + part[0]
        lower = part[h // 8]
        down = lower
        for v in part[h // 8 + 1 :]:
            lower = lower + v
            down = down + lower
        column = upper + lower
        columns.append(jnp.sum(column, axis=0, keepdims=True))
        rows.append(jnp.sum(8.0 * (step - down) + sub * column, axis=0, keepdims=True))
        edges.append(e[h : h + 1, :])
    columns = jnp.concatenate(columns, axis=0)
    rows = jnp.concatenate(rows, axis=0)
    edges = jnp.concatenate(edges, axis=0)
    lane_coord = ((lane + h) % n - h).astype(F32)
    unit = float(n // 8)
    norm = 1.0 / total(columns)
    row_shift = total(rows) * norm / unit
    col_shift = total(columns * lane_coord) * norm / unit
    row_edge = total(edges) * norm * (float(n) / unit)
    col_edge = total(jnp.where(lane == h, columns, 0.0)) * norm * (float(n) / unit)
    return row_shift, col_shift, -row_shift - row_edge, -col_shift - col_edge


MESH = pl.DeviceIdType.MESH


def stitch(
    colour_hbm,
    offset_hbm,
    live_hbm,
    ids_hbm,
    strips_hbm,
    fore_row_hbm,
    fore_col_hbm,
    back_col_hbm,
    back_row_hbm,
    out_ref,
    colour_ref,
    offset_ref,
    live_ref,
    ids_ref,
    strips,
    fore_row_ref,
    fore_col_ref,
    back_col_ref,
    back_row_ref,
    shifted,
    sent,
    firsts,
    middles,
    arrived,
    line,
    lines,
    tile_out,
    tiles,
    scalar_sem,
    strip_sem,
    table_sem,
    window_send,
    window_recv,
    line_send,
    line_recv,
    tile_send,
    tile_recv,
    hello,
):
    n = PATCH
    rounds, layers, blocks = strips.shape[:3]
    slots = offset_ref.shape[3]
    half = slots // 2
    entries = rounds * slots
    groups = lax.axis_size("grp")
    tile_count = lax.axis_size("tiles")
    devices = tile_count * groups
    tile_index = lax.axis_index("tiles")
    group_index = lax.axis_index("grp")
    me = tile_index * groups + group_index
    strides = [1] + [tile_count // 2] * (rounds - 1)
    sides = [(tile_index // s) % 2 for s in strides]
    partners = [tile_index + s * (1 - 2 * side) for s, side in zip(strides, sides)]

    barrier = pltpu.get_barrier_semaphore()
    neighbours = []
    stride = 1
    while stride < tile_count:
        bit = (tile_index // stride) % 2
        neighbours.append((tile_index + stride * (1 - 2 * bit), group_index))
        stride *= 2
    stride = 1
    while stride < groups:
        bit = (group_index // stride) % 2
        neighbours.append((tile_index, group_index + stride * (1 - 2 * bit)))
        stride *= 2
    stages = len(neighbours)
    for at in neighbours:
        pl.semaphore_signal(barrier, inc=1, device_id=at, device_id_type=MESH)

    scalar_loads = [
        pltpu.make_async_copy(a, b, scalar_sem.at[i])
        for i, (a, b) in enumerate(
            [(offset_hbm, offset_ref), (colour_hbm, colour_ref), (live_hbm, live_ref), (ids_hbm, ids_ref)]
        )
    ]
    for load in scalar_loads:
        load.start()
    strip_loads = [pltpu.make_async_copy(strips_hbm.at[r], strips.at[r], strip_sem.at[r]) for r in range(rounds)]
    for load in strip_loads:
        load.start()
    table_loads = [
        pltpu.make_async_copy(a, b, table_sem.at[i])
        for i, (a, b) in enumerate(
            [(fore_row_hbm, fore_row_ref), (fore_col_hbm, fore_col_ref), (back_col_hbm, back_col_ref), (back_row_hbm, back_row_ref)]
        )
    ]
    for load in table_loads:
        load.start()
    def extract(r, picks):
        rests = []
        lane = lax.broadcasted_iota(jnp.int32, (n + SUB, LANES), 1)
        for i, k in enumerate(picks):
            row, column = offset_ref[0, r, 0, k], offset_ref[0, r, 1, k]
            block = jnp.minimum(lax.div(column, LANES), blocks - 2)
            layer = jnp.minimum(lax.div(row, SUB), layers - n // SUB - 1)
            shift = column - block * LANES
            turn = lax.rem(2 * LANES - shift, LANES)
            left, right = (
                pltpu.roll(
                    strips[colour_ref[0, r], pl.ds(layer, n // SUB + 1), block + side]
                    .reshape(n + SUB, LANES)
                    .astype(F32),
                    turn,
                    1,
                )
                for side in range(2)
            )
            shifted[i] = jnp.where(lane < LANES - shift, left, right)
            rests.append(row - layer * SUB)
        return [shifted[i, pl.ds(rest, n), :].astype(BF16) for i, rest in enumerate(rests)]

    def pick(r, values):
        value = values[0]
        for i in range(1, rounds):
            value = jnp.where(r == i, values[i], value)
        return value

    def window_copy(r, j):
        return pltpu.make_async_remote_copy(
            src_ref=sent.at[r, j],
            dst_ref=arrived.at[r, j],
            send_sem=window_send.at[r, j],
            recv_sem=window_recv.at[r, j],
            device_id=(pick(r, partners), group_index),
            device_id_type=MESH,
        )

    def line_copy(r):
        return pltpu.make_async_remote_copy(
            src_ref=line,
            dst_ref=lines.at[r],
            send_sem=line_send.at[r],
            recv_sem=line_recv.at[r],
            device_id=(partners[r], group_index),
            device_id_type=MESH,
        )

    for load in scalar_loads:
        load.wait()
    lane = lax.broadcasted_iota(jnp.int32, (1, LANES), 1)

    def place_id(i, ids):
        r, k = i // slots, i % slots
        return jnp.where(lane == i, jnp.where(k < live_ref[0, r], ids_ref[0, r, k], -1), ids)

    line[...] = lax.fori_loop(0, entries, place_id, jnp.zeros((1, LANES), jnp.int32)).astype(F32)
    for load in strip_loads:
        load.wait()
    pl.semaphore_wait(barrier, stages)
    for r in range(rounds):
        line_copy(r).start()

    def place_of(q):
        return rounds - 1 - q % rounds, (q // rounds) * PAIR

    def launch(q):
        r, j = place_of(q)
        for i in range(PAIR):
            window_copy(r, j + i).start()

    def produce(q, carry):
        r, j = place_of(q)
        base = (1 - pick(r, sides)) * half + j
        for i, window in enumerate(extract(r, [base + i for i in range(PAIR)])):
            sent[r, j + i] = window

        @pl.when(q > 0)
        def _():
            launch(q - 1)

        return carry

    lax.fori_loop(0, rounds * half // PAIR, produce, 0)
    for load in table_loads:
        load.wait()
    launch(rounds * half // PAIR - 1)
    parts = half // GROUP

    def prepare(g, carry):
        r, part = g // parts, g % parts
        j = part * GROUP
        windows = extract(r, [pick(r, sides) * half + j + i for i in range(GROUP)])
        main, middle = spectra(windows, fore_row_ref[...], fore_col_ref[...])
        for c in range(2):
            for i in range(GROUP):
                firsts[r, j + i, c] = main[i][c]
            middles[r, part, c] = middle[c]
        return carry

    lax.fori_loop(0, rounds * parts, prepare, 0)

    def neighbour(stage):
        tile, group = neighbours[0]
        for i in range(1, stages):
            tile = jnp.where(stage == i, neighbours[i][0], tile)
            group = jnp.where(stage == i, neighbours[i][1], group)
        return tile, group

    def hail(stage):
        pl.semaphore_signal(hello.at[stage], inc=1, device_id=neighbour(stage), device_id_type=MESH)

    def work(g, disp):
        r, part = g // parts, g % parts
        j = part * GROUP
        hail(early + g)
        for i in range(GROUP):
            window_copy(r, j + i).wait_recv()
        seconds = spectra([arrived[r, j + i] for i in range(GROUP)], fore_row_ref[...], fore_col_ref[...])
        a, b, c, d = correlate(
            ([(firsts[r, j + i, 0], firsts[r, j + i, 1]) for i in range(GROUP)], (middles[r, part, 0], middles[r, part, 1])),
            seconds,
            back_row_ref[...],
            back_col_ref[...],
        )
        own = r * slots + pick(r, sides) * half + j
        other = r * slots + (1 - pick(r, sides)) * half + j
        pl.semaphore_wait(hello.at[early + g], 1)
        return (
            disp
            + row_place(a, own)
            + row_place(c, other)
            + row_place(b, own + entries)
            + row_place(d, other + entries)
        )

    early = stages - rounds * parts
    for i in range(early):
        hail(i)
        pl.semaphore_wait(hello.at[i], 1)
    for s in range(rounds):
        line_copy(s).wait()
    ids = line[...]
    id_line = jnp.zeros((1, LANES), F32)
    for s in range(rounds):
        theirs = pltpu.roll(lines[s], jnp.where(sides[s] == 0, half, LANES - half), 1)
        in_round = (lane >= s * slots) & (lane < (s + 1) * slots)
        mine = (lane // half) % 2 == sides[s]
        id_line = id_line + jnp.where(in_round, jnp.where(mine, ids, theirs), 0.0)
    disp = lax.fori_loop(0, rounds * parts, work, pltpu.roll(id_line, 2 * entries, 1))

    tile_out[...] = disp
    tiles[me] = disp

    def start(i, carry):
        to = i + jnp.where(i >= me, 1, 0)
        pltpu.make_async_remote_copy(
            src_ref=tile_out,
            dst_ref=tiles.at[me],
            send_sem=tile_send,
            recv_sem=tile_recv,
            device_id=(to // groups, to % groups),
            device_id_type=MESH,
        ).start()
        return carry

    lax.fori_loop(0, devices - 1, start, 0)

    def drain(i, carry):
        window_copy(i // half, i % half).wait_send()
        return carry

    lax.fori_loop(0, rounds * half, drain, 0)
    everyone = pltpu.make_async_remote_copy(
        src_ref=tiles.at[pl.ds(0, devices - 1)],
        dst_ref=tiles.at[pl.ds(0, devices - 1)],
        send_sem=tile_send,
        recv_sem=tile_recv,
        device_id=neighbours[0],
        device_id_type=MESH,
    )
    everyone.wait_recv()

    pack = LANES // entries
    node = lax.broadcasted_iota(jnp.int32, (NODE_DEV, LANES), 0).astype(F32)
    first_node = (me * NODE_DEV).astype(F32)
    lane = lax.broadcasted_iota(jnp.int32, (1, LANES), 1)
    onehots = []
    values = []
    for g in range(devices // pack):
        parts = [jnp.zeros((1, LANES), F32)] * 3
        for i in range(pack):
            tile = tiles[g * pack + i]
            here = (lane >= i * entries) & (lane < (i + 1) * entries)
            for c in range(3):
                moved = pltpu.roll(tile, ((i - c) * entries) % LANES, 1) if i != c else tile
                parts[c] = jnp.where(here, moved, parts[c])
        onehots.append(jnp.where(parts[2] - first_node == node, 1.0, 0.0).astype(BF16))
        tile = jnp.concatenate(parts[:2], axis=0)
        hi = tile.astype(BF16).astype(F32)
        rest = tile - hi
        mid = rest.astype(BF16).astype(F32)
        values.append(jnp.concatenate([hi, mid, rest - mid, jnp.zeros_like(hi)], axis=0).astype(BF16))
    result = lax.dot_general(
        jnp.concatenate(values, axis=1),
        jnp.concatenate(onehots, axis=1),
        (((1,), (1,)), ((), ())),
        preferred_element_type=F32,
    )
    out_ref[0:2] = result[0:2]
    out_ref[2:4] = result[2:4] + result[4:6]
    everyone.wait_send()


def on_device(strips, edge_colour, patch_offsets, patch_live, node_ids):
    rounds, height, width = strips.shape
    n = PATCH
    slot_count = patch_offsets.shape[2]
    half = slot_count // 2
    devices = lax.axis_size("tiles") * lax.axis_size("grp")
    whole = pl.BlockSpec(memory_space=VMEM)
    anywhere = pl.BlockSpec(memory_space=pl.ANY)
    sem = pltpu.SemaphoreType.DMA
    windows = (rounds, half, n, n)
    tiled = strips.reshape(rounds, height // SUB, SUB, width // LANES, LANES).transpose(0, 1, 3, 2, 4)
    scalars = [jnp.transpose(patch_offsets, (0, 1, 3, 2)), edge_colour, patch_live, node_ids]
    constants = [jnp.asarray(t) for t in tables()]
    sums = pl.pallas_call(
        stitch,
        out_shape=jax.ShapeDtypeStruct((4, NODE_DEV), F32),
        in_specs=[anywhere] * 9,
        out_specs=whole,
        scratch_shapes=[
            pltpu.SMEM(edge_colour.shape, jnp.int32),
            pltpu.SMEM(scalars[0].shape, jnp.int32),
            pltpu.SMEM(patch_live.shape, jnp.int32),
            pltpu.SMEM(node_ids.shape, jnp.int32),
            pltpu.VMEM(tiled.shape, BF16),
            *(pltpu.VMEM(t.shape, BF16) for t in constants),
            pltpu.VMEM((GROUP, n + SUB, n), F32),
            pltpu.VMEM(windows, BF16),
            pltpu.VMEM((rounds, half, 2, n // 2, n), F32),
            pltpu.VMEM((rounds, half // GROUP, 2, 8, n), F32),
            pltpu.VMEM(windows, BF16),
            pltpu.VMEM((1, LANES), F32),
            pltpu.VMEM((rounds, 1, LANES), F32),
            pltpu.VMEM((1, LANES), F32),
            pltpu.VMEM((devices, 1, LANES), F32),
            sem((4,)),
            sem((rounds,)),
            sem((4,)),
            sem((rounds, half)),
            sem((rounds, half)),
            sem((rounds,)),
            sem((rounds,)),
            sem(()),
            sem(()),
            pltpu.SemaphoreType.REGULAR((devices.bit_length() - 1,)),
        ],
        compiler_params=pltpu.CompilerParams(collective_id=0, has_side_effects=True, vmem_limit_bytes=VMEM_LIMIT),
        name="stitch",
    )(edge_colour, scalars[0], patch_live, node_ids, tiled, *constants)
    return sums[0:2] + sums[2:4]


def solution(mesh):
    placed = (
        P(("tiles", "grp"), None, None),
        P(("tiles", "grp"), None),
        P(("tiles", "grp"), None, None, None),
        P(("tiles", "grp"), None),
        P(("tiles", "grp"), None, None),
    )
    return jax.shard_map(
        on_device, mesh=mesh, in_specs=placed, out_specs=P(None, ("tiles", "grp")), check_vma=False
    )
```

```python
import functools
import math

import jax
import jax.numpy as jnp
import numpy as np
from jax import lax
from jax.experimental import pallas as pl
from jax.experimental.pallas import tpu as pltpu
from jax.sharding import PartitionSpec as P

PATCH = 128
NODE_DEV = 128
LANES = 128
GROUP = 4
PAIR = 2
SUB = 8
DOT = 2
VMEM_LIMIT = 32 * 1024 * 1024

F32 = jnp.float32
BF16 = jnp.bfloat16
VMEM = pltpu.MemorySpace.VMEM
SMEM = pltpu.MemorySpace.SMEM


def split_np(x):
    hi = np.asarray(x, np.float32).astype(BF16)
    lo = (np.asarray(x, np.float64) - hi.astype(np.float64)).astype(np.float32).astype(BF16)
    return hi, lo


def tables():
    n = PATCH
    h = n // 2
    j = np.arange(n)
    angle = 2.0 * math.pi / n * ((j[:, None] * j[None, :]) % n)
    c, s = np.cos(angle), np.sin(angle)
    rhi, rlo = split_np(np.concatenate([c[: h + 1], s[1:h]], axis=0))
    fore_row = np.concatenate([rhi, rlo], axis=1)
    chi, clo = split_np(np.block([[c, -s], [-s, -c]]))
    fore_col = np.concatenate([chi, clo, chi], axis=0)
    bhi, blo = split_np(np.block([[c, s], [-s, c]]))
    back_col = np.concatenate([bhi, blo, bhi], axis=0)
    weight = np.where(j[:h] == 0, 1.0, 2.0)[None, :]
    ihi, ilo = split_np(np.concatenate([weight * c[:, :h], c[:, h : h + 1], -2.0 * s[:, 1:h]], axis=1) / float(n * n))
    back_row = np.concatenate([ihi, ilo, ihi], axis=1)
    return fore_row, fore_col, back_col, back_row


def split(x):
    hi = x.astype(BF16)
    return hi, (x - hi.astype(F32)).astype(BF16)


def dot(a, b):
    return jnp.dot(a, b, preferred_element_type=F32)


def row_place(column, base):
    count = column.shape[0]
    lane = lax.broadcasted_iota(jnp.int32, (count, LANES), 1)
    sub = lax.broadcasted_iota(jnp.int32, (count, LANES), 0)
    return jnp.sum(jnp.where(lane == sub + base, column, 0.0), axis=0, keepdims=True)


def triple(x):
    hi, lo = split(x)
    return jnp.concatenate([hi, hi, lo], axis=1)


def apply(rows, table):
    out = []
    for p in range(0, len(rows), DOT):
        some = rows[p : p + DOT] if len(rows) - p > DOT + 1 else rows[p:]
        y = dot(jnp.concatenate([triple(v) for v in some], axis=0), table)
        at = 0
        for v in some:
            out.append(y[at : at + v.shape[0]])
            at += v.shape[0]
        if p + len(some) == len(rows):
            return out


def gather_rows(rows):
    sub = lax.broadcasted_iota(jnp.int32, (8, LANES), 0)
    out = jnp.zeros((8, LANES), F32)
    for i, row in enumerate(rows):
        out = jnp.where(sub == i, row, out)
    return out


def spectra(windows, fore_row, fore_col):
    n = PATCH
    h = n // 2
    count = len(windows)
    first = lax.broadcasted_iota(jnp.int32, (8, n), 0) == 0
    mains = []
    middles = []
    for p in range(0, count, 2):
        x = jnp.concatenate(windows[p : p + 2], axis=1)
        y = dot(fore_row, jnp.concatenate([x, x], axis=0))
        for i in range(2):
            part = y[:, i * n : (i + 1) * n]
            middles.append(part[h : h + 1])
            sine = jnp.concatenate([jnp.where(first, 0.0, part[h : h + 8]), part[h + 8 :]], axis=0)
            mains.append(jnp.concatenate([part[:h], sine], axis=1))
    middle = gather_rows(middles)
    mains.append(jnp.concatenate([jnp.concatenate([middle, jnp.zeros_like(middle)], axis=1)] * 2, axis=0))
    parts = apply(mains, fore_col)
    main = [(f[:, :n], f[:, n:]) for f in parts[:-1]]
    return main, (parts[-1][:8, :n], parts[-1][:8, n:])


def fold(v):
    return sum(v[i : i + 8] for i in range(8, v.shape[0], 8)) + v[:8]


def whiten_terms(first, second):
    (r1, i1), (r2, i2) = first, second
    cross_r = r1 * r2 + i1 * i2
    cross_i = i1 * r2 - r1 * i2
    return cross_r, cross_i, jnp.sqrt(cross_r * cross_r + cross_i * cross_i)


def total(v):
    return jnp.sum(v, axis=1, keepdims=True)


def correlate(first, second, back_row, back_col):
    n = PATCH
    h = n // 2
    cells = float(n * n)
    count = len(first[0])
    terms = [whiten_terms(a, b) for a, b in zip(first[0], second[0])]
    middle = whiten_terms(first[1], second[1])

    def spectrum_sum(values, middle_value):
        folded = jnp.concatenate([jnp.sum(fold(v), axis=0, keepdims=True) for v in values], axis=0)
        edge = jnp.concatenate([v[:1] for v in values], axis=0)
        return 2.0 * folded - edge + middle_value[:count], edge

    mag_sum, _ = spectrum_sum([t[2] for t in terms], middle[2])
    extra = 0.1 * (total(mag_sum) / cells) + 1e-06
    inverses = [1.0 / (t[2] + extra[p : p + 1]) for p, t in enumerate(terms)]
    middle_inverse = 1.0 / (middle[2] + gather_rows([extra[p : p + 1] for p in range(count)]))
    rows = [jnp.concatenate([t[0] * v, t[1] * v], axis=1) for t, v in zip(terms, inverses)]
    middle_row = jnp.concatenate([middle[0] * middle_inverse, middle[1] * middle_inverse], axis=1)
    rows.append(jnp.concatenate([middle_row, middle_row], axis=0))

    def power(m, v):
        return (m * v) * (m * v)

    power_sum, edge = spectrum_sum(
        [power(t[2], v) for t, v in zip(terms, inverses)], power(middle[2], middle_inverse)
    )
    lane = lax.broadcasted_iota(jnp.int32, (count, n), 1)
    variance = total(power_sum - jnp.where(lane == 0, edge, 0.0)) / (cells * cells)
    scale = 2.0 / jnp.sqrt(variance + 1e-06) * math.log2(math.e)

    back = apply(rows, back_col)
    middle_back = back[-1][:8, :n]
    first_row = lax.broadcasted_iota(jnp.int32, (8, n), 0) == 0
    surfaces = []
    for p in range(0, count, 2):
        columns = []
        for q in range(p, p + 2):
            part = back[q]
            imag = part[:, n:]
            head = jnp.where(first_row, middle_back[q : q + 1], imag[:8])
            columns.append(jnp.concatenate([part[:, :n], head, imag[8:]], axis=0))
        hi, lo = split(jnp.concatenate(columns, axis=1))
        wide = dot(back_row, jnp.concatenate([hi, hi, lo], axis=0))
        surfaces += [wide[:, :n], wide[:, n:]]

    tops = []
    for surface in surfaces:
        peak = surface[:8]
        for i in range(8, n, 8):
            peak = jnp.maximum(peak, surface[i : i + 8])
        tops.append(jnp.max(peak, axis=0, keepdims=True))
    top = jnp.max(jnp.concatenate(tops, axis=0), axis=1, keepdims=True)
    sub = lax.broadcasted_iota(jnp.int32, (8, n), 0).astype(F32)
    columns = []
    rows = []
    edges = []
    for p in range(count):
        e = jnp.exp2((surfaces[p] - top[p : p + 1]) * scale[p : p + 1])
        part = [e[i : i + 8] for i in range(0, n, 8)]
        upper = part[h // 8 - 1]
        step = upper
        for v in part[h // 8 - 2 : 0 : -1]:
            upper = upper + v
            step = step + upper
        upper = upper + part[0]
        lower = part[h // 8]
        down = lower
        for v in part[h // 8 + 1 :]:
            lower = lower + v
            down = down + lower
        column = upper + lower
        columns.append(jnp.sum(column, axis=0, keepdims=True))
        rows.append(jnp.sum(8.0 * (step - down) + sub * column, axis=0, keepdims=True))
        edges.append(e[h : h + 1, :])
    columns = jnp.concatenate(columns, axis=0)
    rows = jnp.concatenate(rows, axis=0)
    edges = jnp.concatenate(edges, axis=0)
    lane_coord = ((lane + h) % n - h).astype(F32)
    unit = float(n // 8)
    norm = 1.0 / total(columns)
    row_shift = total(rows) * norm / unit
    col_shift = total(columns * lane_coord) * norm / unit
    row_edge = total(edges) * norm * (float(n) / unit)
    col_edge = total(jnp.where(lane == h, columns, 0.0)) * norm * (float(n) / unit)
    return row_shift, col_shift, -row_shift - row_edge, -col_shift - col_edge


MESH = pl.DeviceIdType.MESH


def stitch(
    colour_hbm,
    offset_hbm,
    live_hbm,
    ids_hbm,
    strips_hbm,
    fore_row_hbm,
    fore_col_hbm,
    back_col_hbm,
    back_row_hbm,
    out_ref,
    colour_ref,
    offset_ref,
    live_ref,
    ids_ref,
    strips,
    fore_row_ref,
    fore_col_ref,
    back_col_ref,
    back_row_ref,
    shifted,
    sent,
    firsts,
    middles,
    arrived,
    line,
    lines,
    tile_out,
    tiles,
    scalar_sem,
    strip_sem,
    table_sem,
    window_send,
    window_recv,
    line_send,
    line_recv,
    tile_send,
    tile_recv,
    hello,
):
    n = PATCH
    rounds, layers, blocks = strips.shape[:3]
    slots = offset_ref.shape[3]
    half = slots // 2
    entries = rounds * slots
    groups = lax.axis_size("grp")
    tile_count = lax.axis_size("tiles")
    devices = tile_count * groups
    tile_index = lax.axis_index("tiles")
    group_index = lax.axis_index("grp")
    me = tile_index * groups + group_index
    strides = [1] + [tile_count // 2] * (rounds - 1)
    sides = [(tile_index // s) % 2 for s in strides]
    partners = [tile_index + s * (1 - 2 * side) for s, side in zip(strides, sides)]

    barrier = pltpu.get_barrier_semaphore()
    neighbours = []
    stride = 1
    while stride < tile_count:
        bit = (tile_index // stride) % 2
        neighbours.append((tile_index + stride * (1 - 2 * bit), group_index))
        stride *= 2
    stride = 1
    while stride < groups:
        bit = (group_index // stride) % 2
        neighbours.append((tile_index, group_index + stride * (1 - 2 * bit)))
        stride *= 2
    stages = len(neighbours)
    for at in neighbours:
        pl.semaphore_signal(barrier, inc=1, device_id=at, device_id_type=MESH)

    scalar_loads = [
        pltpu.make_async_copy(a, b, scalar_sem.at[i])
        for i, (a, b) in enumerate(
            [(offset_hbm, offset_ref), (colour_hbm, colour_ref), (live_hbm, live_ref), (ids_hbm, ids_ref)]
        )
    ]
    for load in scalar_loads:
        load.start()
    strip_loads = [pltpu.make_async_copy(strips_hbm.at[r], strips.at[r], strip_sem.at[r]) for r in range(rounds)]
    for load in strip_loads:
        load.start()
    table_loads = [
        pltpu.make_async_copy(a, b, table_sem.at[i])
        for i, (a, b) in enumerate(
            [(fore_row_hbm, fore_row_ref), (fore_col_hbm, fore_col_ref), (back_col_hbm, back_col_ref), (back_row_hbm, back_row_ref)]
        )
    ]
    for load in table_loads:
        load.start()
    def extract(r, picks):
        rests = []
        lane = lax.broadcasted_iota(jnp.int32, (n + SUB, LANES), 1)
        for i, k in enumerate(picks):
            row, column = offset_ref[0, r, 0, k], offset_ref[0, r, 1, k]
            block = jnp.minimum(lax.div(column, LANES), blocks - 2)
            layer = jnp.minimum(lax.div(row, SUB), layers - n // SUB - 1)
            shift = column - block * LANES
            turn = lax.rem(2 * LANES - shift, LANES)
            left, right = (
                pltpu.roll(
                    strips[colour_ref[0, r], pl.ds(layer, n // SUB + 1), block + side]
                    .reshape(n + SUB, LANES)
                    .astype(F32),
                    turn,
                    1,
                )
                for side in range(2)
            )
            shifted[i] = jnp.where(lane < LANES - shift, left, right)
            rests.append(row - layer * SUB)
        return [shifted[i, pl.ds(rest, n), :].astype(BF16) for i, rest in enumerate(rests)]

    def pick(r, values):
        value = values[0]
        for i in range(1, rounds):
            value = jnp.where(r == i, values[i], value)
        return value

    def window_copy(r, j):
        return pltpu.make_async_remote_copy(
            src_ref=sent.at[r, j],
            dst_ref=arrived.at[r, j],
            send_sem=window_send.at[r, j],
            recv_sem=window_recv.at[r, j],
            device_id=(pick(r, partners), group_index),
            device_id_type=MESH,
        )

    def line_copy(r):
        return pltpu.make_async_remote_copy(
            src_ref=line,
            dst_ref=lines.at[r],
            send_sem=line_send.at[r],
            recv_sem=line_recv.at[r],
            device_id=(partners[r], group_index),
            device_id_type=MESH,
        )

    for load in scalar_loads:
        load.wait()
    lane = lax.broadcasted_iota(jnp.int32, (1, LANES), 1)

    def place_id(i, ids):
        r, k = i // slots, i % slots
        return jnp.where(lane == i, jnp.where(k < live_ref[0, r], ids_ref[0, r, k], -1), ids)

    line[...] = lax.fori_loop(0, entries, place_id, jnp.zeros((1, LANES), jnp.int32)).astype(F32)
    for load in strip_loads:
        load.wait()
    pl.semaphore_wait(barrier, stages)
    for r in range(rounds):
        line_copy(r).start()

    def place_of(q):
        return rounds - 1 - q % rounds, (q // rounds) * PAIR

    def launch(q):
        r, j = place_of(q)
        for i in range(PAIR):
            window_copy(r, j + i).start()

    def produce(q, carry):
        r, j = place_of(q)
        base = (1 - pick(r, sides)) * half + j
        for i, window in enumerate(extract(r, [base + i for i in range(PAIR)])):
            sent[r, j + i] = window

        @pl.when(q > 0)
        def _():
            launch(q - 1)

        return carry

    lax.fori_loop(0, rounds * half // PAIR, produce, 0)
    for load in table_loads:
        load.wait()
    launch(rounds * half // PAIR - 1)
    parts = half // GROUP

    def prepare(g, carry):
        r, part = g // parts, g % parts
        j = part * GROUP
        windows = extract(r, [pick(r, sides) * half + j + i for i in range(GROUP)])
        main, middle = spectra(windows, fore_row_ref[...], fore_col_ref[...])
        for c in range(2):
            for i in range(GROUP):
                firsts[r, j + i, c] = main[i][c]
            middles[r, part, c] = middle[c]
        return carry

    lax.fori_loop(0, rounds * parts, prepare, 0)

    def neighbour(stage):
        tile, group = neighbours[0]
        for i in range(1, stages):
            tile = jnp.where(stage == i, neighbours[i][0], tile)
            group = jnp.where(stage == i, neighbours[i][1], group)
        return tile, group

    def hail(stage):
        pl.semaphore_signal(hello.at[stage], inc=1, device_id=neighbour(stage), device_id_type=MESH)

    def work(g, disp):
        r, part = g // parts, g % parts
        j = part * GROUP
        hail(early + g)
        for i in range(GROUP):
            window_copy(r, j + i).wait_recv()
        seconds = spectra([arrived[r, j + i] for i in range(GROUP)], fore_row_ref[...], fore_col_ref[...])
        a, b, c, d = correlate(
            ([(firsts[r, j + i, 0], firsts[r, j + i, 1]) for i in range(GROUP)], (middles[r, part, 0], middles[r, part, 1])),
            seconds,
            back_row_ref[...],
            back_col_ref[...],
        )
        own = r * slots + pick(r, sides) * half + j
        other = r * slots + (1 - pick(r, sides)) * half + j
        pl.semaphore_wait(hello.at[early + g], 1)
        return (
            disp
            + row_place(a, own)
            + row_place(c, other)
            + row_place(b, own + entries)
            + row_place(d, other + entries)
        )

    early = stages - rounds * parts
    for i in range(early):
        hail(i)
        pl.semaphore_wait(hello.at[i], 1)
    for s in range(rounds):
        line_copy(s).wait()
    ids = line[...]
    id_line = jnp.zeros((1, LANES), F32)
    for s in range(rounds):
        theirs = pltpu.roll(lines[s], jnp.where(sides[s] == 0, half, LANES - half), 1)
        in_round = (lane >= s * slots) & (lane < (s + 1) * slots)
        mine = (lane // half) % 2 == sides[s]
        id_line = id_line + jnp.where(in_round, jnp.where(mine, ids, theirs), 0.0)
    disp = lax.fori_loop(0, rounds * parts, work, pltpu.roll(id_line, 2 * entries, 1))

    tile_out[...] = disp
    tiles[me] = disp

    def start(i, carry):
        to = i + jnp.where(i >= me, 1, 0)
        pltpu.make_async_remote_copy(
            src_ref=tile_out,
            dst_ref=tiles.at[me],
            send_sem=tile_send,
            recv_sem=tile_recv,
            device_id=(to // groups, to % groups),
            device_id_type=MESH,
        ).start()
        return carry

    lax.fori_loop(0, devices - 1, start, 0)

    def drain(i, carry):
        window_copy(i // half, i % half).wait_send()
        return carry

    lax.fori_loop(0, rounds * half, drain, 0)
    everyone = pltpu.make_async_remote_copy(
        src_ref=tiles.at[pl.ds(0, devices - 1)],
        dst_ref=tiles.at[pl.ds(0, devices - 1)],
        send_sem=tile_send,
        recv_sem=tile_recv,
        device_id=neighbours[0],
        device_id_type=MESH,
    )
    everyone.wait_recv()

    pack = LANES // entries
    node = lax.broadcasted_iota(jnp.int32, (NODE_DEV, LANES), 0).astype(F32)
    first_node = (me * NODE_DEV).astype(F32)
    lane = lax.broadcasted_iota(jnp.int32, (1, LANES), 1)
    onehots = []
    values = []
    for g in range(devices // pack):
        parts = [jnp.zeros((1, LANES), F32)] * 3
        for i in range(pack):
            tile = tiles[g * pack + i]
            here = (lane >= i * entries) & (lane < (i + 1) * entries)
            for c in range(3):
                moved = pltpu.roll(tile, ((i - c) * entries) % LANES, 1) if i != c else tile
                parts[c] = jnp.where(here, moved, parts[c])
        onehots.append(jnp.where(parts[2] - first_node == node, 1.0, 0.0).astype(BF16))
        tile = jnp.concatenate(parts[:2], axis=0)
        hi = tile.astype(BF16).astype(F32)
        rest = tile - hi
        mid = rest.astype(BF16).astype(F32)
        values.append(jnp.concatenate([hi, mid, rest - mid, jnp.zeros_like(hi)], axis=0).astype(BF16))
    result = lax.dot_general(
        jnp.concatenate(values, axis=1),
        jnp.concatenate(onehots, axis=1),
        (((1,), (1,)), ((), ())),
        preferred_element_type=F32,
    )
    out_ref[...] = result[0:2] + (result[2:4] + result[4:6])
    everyone.wait_send()


def on_device(strips, edge_colour, patch_offsets, patch_live, node_ids):
    rounds, height, width = strips.shape
    n = PATCH
    slot_count = patch_offsets.shape[2]
    half = slot_count // 2
    devices = lax.axis_size("tiles") * lax.axis_size("grp")
    whole = pl.BlockSpec(memory_space=VMEM)
    anywhere = pl.BlockSpec(memory_space=pltpu.MemorySpace.HBM)
    sem = pltpu.SemaphoreType.DMA
    windows = (rounds, half, n, n)
    tiled = strips.reshape(rounds, height // SUB, SUB, width // LANES, LANES).transpose(0, 1, 3, 2, 4)
    scalars = [jnp.transpose(patch_offsets, (0, 1, 3, 2)), edge_colour, patch_live, node_ids]
    constants = [jnp.asarray(t) for t in tables()]
    sums = pl.pallas_call(
        stitch,
        out_shape=jax.ShapeDtypeStruct((2, NODE_DEV), F32),
        in_specs=[anywhere] * 9,
        out_specs=whole,
        scratch_shapes=[
            pltpu.SMEM(edge_colour.shape, jnp.int32),
            pltpu.SMEM(scalars[0].shape, jnp.int32),
            pltpu.SMEM(patch_live.shape, jnp.int32),
            pltpu.SMEM(node_ids.shape, jnp.int32),
            pltpu.VMEM(tiled.shape, BF16),
            *(pltpu.VMEM(t.shape, BF16) for t in constants),
            pltpu.VMEM((GROUP, n + SUB, n), F32),
            pltpu.VMEM(windows, BF16),
            pltpu.VMEM((rounds, half, 2, n // 2, n), F32),
            pltpu.VMEM((rounds, half // GROUP, 2, 8, n), F32),
            pltpu.VMEM(windows, BF16),
            pltpu.VMEM((1, LANES), F32),
            pltpu.VMEM((rounds, 1, LANES), F32),
            pltpu.VMEM((1, LANES), F32),
            pltpu.VMEM((devices, 1, LANES), F32),
            sem((4,)),
            sem((rounds,)),
            sem((4,)),
            sem((rounds, half)),
            sem((rounds, half)),
            sem((rounds,)),
            sem((rounds,)),
            sem(()),
            sem(()),
            pltpu.SemaphoreType.REGULAR((devices.bit_length() - 1,)),
        ],
        compiler_params=pltpu.CompilerParams(collective_id=0, has_side_effects=True, vmem_limit_bytes=VMEM_LIMIT),
        name="stitch",
    )(*(pltpu.with_memory_space_constraint(v, pltpu.MemorySpace.HBM) for v in (edge_colour, scalars[0], patch_live, node_ids, tiled, *constants)))
    return sums


def solution(mesh):
    placed = (
        P(("tiles", "grp"), None, None),
        P(("tiles", "grp"), None),
        P(("tiles", "grp"), None, None, None),
        P(("tiles", "grp"), None),
        P(("tiles", "grp"), None, None),
    )
    return jax.shard_map(
        on_device, mesh=mesh, in_specs=placed, out_specs=P(None, ("tiles", "grp")), check_vma=False
    )
```

```python
import functools
import math

import jax
import jax.numpy as jnp
import numpy as np
from jax import lax
from jax.experimental import pallas as pl
from jax.experimental.pallas import tpu as pltpu
from jax.sharding import PartitionSpec as P

PATCH = 128
NODE_DEV = 128
LANES = 128
GROUP = 4
PAIR = 2
CUTS = 2
SUB = 8
DOT = 2
LATE = (0,)
LATE_STEP = 1
VMEM_LIMIT = 32 * 1024 * 1024

F32 = jnp.float32
BF16 = jnp.bfloat16
VMEM = pltpu.MemorySpace.VMEM
SMEM = pltpu.MemorySpace.SMEM


def split_np(x):
    hi = np.asarray(x, np.float32).astype(BF16)
    lo = (np.asarray(x, np.float64) - hi.astype(np.float64)).astype(np.float32).astype(BF16)
    return hi, lo


def tables():
    n = PATCH
    h = n // 2
    j = np.arange(n)
    angle = 2.0 * math.pi / n * ((j[:, None] * j[None, :]) % n)
    c, s = np.cos(angle), np.sin(angle)
    rhi, rlo = split_np(np.concatenate([c[: h + 1], s[1:h]], axis=0))
    fore_row = np.concatenate([rhi, rlo], axis=1)
    chi, clo = split_np(np.block([[c, -s], [-s, -c]]))
    fore_col = np.concatenate([chi, clo, chi], axis=0)
    bhi, blo = split_np(np.block([[c, s], [-s, c]]))
    back_col = np.concatenate([bhi, blo, bhi], axis=0)
    weight = np.where(j[:h] == 0, 1.0, 2.0)[None, :]
    ihi, ilo = split_np(np.concatenate([weight * c[:, :h], c[:, h : h + 1], -2.0 * s[:, 1:h]], axis=1) / float(n * n))
    back_row = np.concatenate([ihi, ilo, ihi], axis=1)
    return fore_row, fore_col, back_col, back_row


def split(x):
    hi = x.astype(BF16)
    return hi, (x - hi.astype(F32)).astype(BF16)


def dot(a, b):
    return jnp.dot(a, b, preferred_element_type=F32)


def row_place(column, base):
    count = column.shape[0]
    lane = lax.broadcasted_iota(jnp.int32, (count, LANES), 1)
    sub = lax.broadcasted_iota(jnp.int32, (count, LANES), 0)
    return jnp.sum(jnp.where(lane == sub + base, column, 0.0), axis=0, keepdims=True)


def triple(x):
    hi, lo = split(x)
    return jnp.concatenate([hi, hi, lo], axis=1)


def apply(rows, table):
    out = []
    for p in range(0, len(rows), DOT):
        some = rows[p : p + DOT] if len(rows) - p > DOT + 1 else rows[p:]
        y = dot(jnp.concatenate([triple(v) for v in some], axis=0), table)
        at = 0
        for v in some:
            out.append(y[at : at + v.shape[0]])
            at += v.shape[0]
        if p + len(some) == len(rows):
            return out


def gather_rows(rows):
    sub = lax.broadcasted_iota(jnp.int32, (8, LANES), 0)
    out = jnp.zeros((8, LANES), F32)
    for i, row in enumerate(rows):
        out = jnp.where(sub == i, row, out)
    return out


def spectra(windows, fore_row, fore_col):
    n = PATCH
    h = n // 2
    count = len(windows)
    first = lax.broadcasted_iota(jnp.int32, (8, n), 0) == 0
    mains = []
    middles = []
    for p in range(0, count, 2):
        x = jnp.concatenate(windows[p : p + 2], axis=1)
        y = dot(fore_row, jnp.concatenate([x, x], axis=0))
        for i in range(2):
            part = y[:, i * n : (i + 1) * n]
            middles.append(part[h : h + 1])
            sine = jnp.concatenate([jnp.where(first, 0.0, part[h : h + 8]), part[h + 8 :]], axis=0)
            mains.append(jnp.concatenate([part[:h], sine], axis=1))
    middle = gather_rows(middles)
    mains.append(jnp.concatenate([jnp.concatenate([middle, jnp.zeros_like(middle)], axis=1)] * 2, axis=0))
    parts = apply(mains, fore_col)
    main = [(f[:, :n], f[:, n:]) for f in parts[:-1]]
    return main, (parts[-1][:8, :n], parts[-1][:8, n:])


def fold(v):
    return sum(v[i : i + 8] for i in range(8, v.shape[0], 8)) + v[:8]


def whiten_terms(first, second):
    (r1, i1), (r2, i2) = first, second
    cross_r = r1 * r2 + i1 * i2
    cross_i = i1 * r2 - r1 * i2
    return cross_r, cross_i, jnp.sqrt(cross_r * cross_r + cross_i * cross_i)


def total(v):
    return jnp.sum(v, axis=1, keepdims=True)


def correlate(first, second, back_row, back_col):
    n = PATCH
    h = n // 2
    cells = float(n * n)
    count = len(first[0])
    terms = [whiten_terms(a, b) for a, b in zip(first[0], second[0])]
    middle = whiten_terms(first[1], second[1])

    def spectrum_sum(values, middle_value):
        folded = jnp.concatenate([jnp.sum(fold(v), axis=0, keepdims=True) for v in values], axis=0)
        edge = jnp.concatenate([v[:1] for v in values], axis=0)
        return 2.0 * folded - edge + middle_value[:count], edge

    mag_sum, _ = spectrum_sum([t[2] for t in terms], middle[2])
    extra = 0.1 * (total(mag_sum) / cells) + 1e-06
    inverses = [1.0 / (t[2] + extra[p : p + 1]) for p, t in enumerate(terms)]
    middle_inverse = 1.0 / (middle[2] + gather_rows([extra[p : p + 1] for p in range(count)]))
    rows = [jnp.concatenate([t[0] * v, t[1] * v], axis=1) for t, v in zip(terms, inverses)]
    middle_row = jnp.concatenate([middle[0] * middle_inverse, middle[1] * middle_inverse], axis=1)
    rows.append(jnp.concatenate([middle_row, middle_row], axis=0))

    def power(m, v):
        return (m * v) * (m * v)

    power_sum, edge = spectrum_sum(
        [power(t[2], v) for t, v in zip(terms, inverses)], power(middle[2], middle_inverse)
    )
    lane = lax.broadcasted_iota(jnp.int32, (count, n), 1)
    variance = total(power_sum - jnp.where(lane == 0, edge, 0.0)) / (cells * cells)
    scale = 2.0 / jnp.sqrt(variance + 1e-06) * math.log2(math.e)

    back = apply(rows, back_col)
    middle_back = back[-1][:8, :n]
    first_row = lax.broadcasted_iota(jnp.int32, (8, n), 0) == 0
    surfaces = []
    for p in range(0, count, 2):
        columns = []
        for q in range(p, p + 2):
            part = back[q]
            imag = part[:, n:]
            head = jnp.where(first_row, middle_back[q : q + 1], imag[:8])
            columns.append(jnp.concatenate([part[:, :n], head, imag[8:]], axis=0))
        hi, lo = split(jnp.concatenate(columns, axis=1))
        wide = dot(back_row, jnp.concatenate([hi, hi, lo], axis=0))
        surfaces += [wide[:, :n], wide[:, n:]]

    tops = []
    for surface in surfaces:
        peak = surface[:8]
        for i in range(8, n, 8):
            peak = jnp.maximum(peak, surface[i : i + 8])
        tops.append(jnp.max(peak, axis=0, keepdims=True))
    top = jnp.max(jnp.concatenate(tops, axis=0), axis=1, keepdims=True)
    sub = lax.broadcasted_iota(jnp.int32, (8, n), 0).astype(F32)
    columns = []
    rows = []
    edges = []
    for p in range(count):
        e = jnp.exp2((surfaces[p] - top[p : p + 1]) * scale[p : p + 1])
        part = [e[i : i + 8] for i in range(0, n, 8)]
        upper = part[h // 8 - 1]
        step = upper
        for v in part[h // 8 - 2 : 0 : -1]:
            upper = upper + v
            step = step + upper
        upper = upper + part[0]
        lower = part[h // 8]
        down = lower
        for v in part[h // 8 + 1 :]:
            lower = lower + v
            down = down + lower
        column = upper + lower
        columns.append(jnp.sum(column, axis=0, keepdims=True))
        rows.append(jnp.sum(8.0 * (step - down) + sub * column, axis=0, keepdims=True))
        edges.append(e[h : h + 1, :])
    columns = jnp.concatenate(columns, axis=0)
    rows = jnp.concatenate(rows, axis=0)
    edges = jnp.concatenate(edges, axis=0)
    lane_coord = ((lane + h) % n - h).astype(F32)
    unit = float(n // 8)
    norm = 1.0 / total(columns)
    row_shift = total(rows) * norm / unit
    col_shift = total(columns * lane_coord) * norm / unit
    row_edge = total(edges) * norm * (float(n) / unit)
    col_edge = total(jnp.where(lane == h, columns, 0.0)) * norm * (float(n) / unit)
    return row_shift, col_shift, -row_shift - row_edge, -col_shift - col_edge


MESH = pl.DeviceIdType.MESH


def stitch(
    colour_hbm,
    offset_hbm,
    live_hbm,
    ids_hbm,
    strips_hbm,
    fore_row_hbm,
    fore_col_hbm,
    back_col_hbm,
    back_row_hbm,
    out_ref,
    colour_ref,
    offset_ref,
    live_ref,
    ids_ref,
    strips,
    fore_row_ref,
    fore_col_ref,
    back_col_ref,
    back_row_ref,
    shifted,
    sent,
    firsts,
    middles,
    arrived,
    line,
    lines,
    tile_out,
    tiles,
    scalar_sem,
    strip_sem,
    table_sem,
    window_send,
    window_recv,
    line_send,
    line_recv,
    tile_send,
    tile_recv,
    hello,
):
    n = PATCH
    rounds, layers, blocks = strips.shape[:3]
    slots = offset_ref.shape[3]
    half = slots // 2
    entries = rounds * slots
    groups = lax.axis_size("grp")
    tile_count = lax.axis_size("tiles")
    devices = tile_count * groups
    tile_index = lax.axis_index("tiles")
    group_index = lax.axis_index("grp")
    me = tile_index * groups + group_index
    strides = [1] + [tile_count // 2] * (rounds - 1)
    sides = [(tile_index // s) % 2 for s in strides]
    partners = [tile_index + s * (1 - 2 * side) for s, side in zip(strides, sides)]

    barrier = pltpu.get_barrier_semaphore()
    neighbours = []
    stride = 1
    while stride < tile_count:
        bit = (tile_index // stride) % 2
        neighbours.append((tile_index + stride * (1 - 2 * bit), group_index))
        stride *= 2
    stride = 1
    while stride < groups:
        bit = (group_index // stride) % 2
        neighbours.append((tile_index, group_index + stride * (1 - 2 * bit)))
        stride *= 2
    stages = len(neighbours)
    for at in neighbours:
        pl.semaphore_signal(barrier, inc=1, device_id=at, device_id_type=MESH)

    scalar_loads = [
        pltpu.make_async_copy(a, b, scalar_sem.at[i])
        for i, (a, b) in enumerate(
            [(offset_hbm, offset_ref), (colour_hbm, colour_ref), (live_hbm, live_ref), (ids_hbm, ids_ref)]
        )
    ]
    for load in scalar_loads:
        load.start()
    strip_loads = [
        pltpu.make_async_copy(strips_hbm.at[r, pl.ds(i, layers // CUTS)], strips.at[r, pl.ds(i, layers // CUTS)], strip_sem.at[r, c])
        for r in range(rounds)
        for c, i in enumerate(range(0, layers, layers // CUTS))
    ]
    for load in strip_loads:
        load.start()
    table_loads = [
        pltpu.make_async_copy(a, b, table_sem.at[i])
        for i, (a, b) in enumerate(
            [(fore_row_hbm, fore_row_ref), (fore_col_hbm, fore_col_ref), (back_col_hbm, back_col_ref), (back_row_hbm, back_row_ref)]
        )
    ]
    def extract(r, picks):
        rests = []
        lane = lax.broadcasted_iota(jnp.int32, (n + SUB, LANES), 1)
        for i, k in enumerate(picks):
            row, column = offset_ref[0, r, 0, k], offset_ref[0, r, 1, k]
            block = jnp.minimum(lax.div(column, LANES), blocks - 2)
            layer = jnp.minimum(lax.div(row, SUB), layers - n // SUB - 1)
            shift = column - block * LANES
            turn = lax.rem(2 * LANES - shift, LANES)
            left, right = (
                pltpu.roll(
                    strips[colour_ref[0, r], pl.ds(layer, n // SUB + 1), block + side]
                    .reshape(n + SUB, LANES)
                    .astype(F32),
                    turn,
                    1,
                )
                for side in range(2)
            )
            shifted[i] = jnp.where(lane < LANES - shift, left, right)
            rests.append(row - layer * SUB)
        return [shifted[i, pl.ds(rest, n), :].astype(BF16) for i, rest in enumerate(rests)]

    def pick(r, values):
        value = values[0]
        for i in range(1, rounds):
            value = jnp.where(r == i, values[i], value)
        return value

    def window_copy(r, j):
        return pltpu.make_async_remote_copy(
            src_ref=sent.at[r, j],
            dst_ref=arrived.at[r, j],
            send_sem=window_send.at[r, j],
            recv_sem=window_recv.at[r, j],
            device_id=(pick(r, partners), group_index),
            device_id_type=MESH,
        )

    def line_copy(r):
        return pltpu.make_async_remote_copy(
            src_ref=line,
            dst_ref=lines.at[r],
            send_sem=line_send.at[r],
            recv_sem=line_recv.at[r],
            device_id=(partners[r], group_index),
            device_id_type=MESH,
        )

    for load in scalar_loads:
        load.wait()
    lane = lax.broadcasted_iota(jnp.int32, (1, LANES), 1)

    def place_id(i, ids):
        r, k = i // slots, i % slots
        return jnp.where(lane == i, jnp.where(k < live_ref[0, r], ids_ref[0, r, k], -1), ids)

    line[...] = lax.fori_loop(0, entries, place_id, jnp.zeros((1, LANES), jnp.int32)).astype(F32)
    for load in strip_loads:
        load.wait()
    for load in table_loads:
        load.start()
    pl.semaphore_wait(barrier, stages)
    for r in range(rounds):
        line_copy(r).start()

    def place_of(q):
        return rounds - 1 - q % rounds, (q // rounds) * PAIR

    def launch(q):
        r, j = place_of(q)
        for i in range(PAIR):
            window_copy(r, j + i).start()

    def produce(q, carry):
        r, j = place_of(q)
        base = (1 - pick(r, sides)) * half + j
        for i, window in enumerate(extract(r, [base + i for i in range(PAIR)])):
            sent[r, j + i] = window

        @pl.when((q > 0) & ((place_of(q - 1)[0] < rounds - 1) | jnp.logical_not(late)))
        def _():
            launch(q - 1)

        return carry

    quarter = tile_index // (tile_count // 4)
    late = functools.reduce(jnp.logical_or, [quarter == v for v in LATE])
    lax.fori_loop(0, rounds * half // PAIR, produce, 0)
    for load in table_loads:
        load.wait()
    launch(rounds * half // PAIR - 1)
    parts = half // GROUP

    def prepare(g, carry):
        r, part = g // parts, g % parts
        j = part * GROUP
        windows = extract(r, [pick(r, sides) * half + j + i for i in range(GROUP)])
        main, middle = spectra(windows, fore_row_ref[...], fore_col_ref[...])
        for c in range(2):
            for i in range(GROUP):
                firsts[r, j + i, c] = main[i][c]
            middles[r, part, c] = middle[c]
        return carry

    lax.fori_loop(0, rounds * parts, prepare, 0)

    def neighbour(stage):
        tile, group = neighbours[0]
        for i in range(1, stages):
            tile = jnp.where(stage == i, neighbours[i][0], tile)
            group = jnp.where(stage == i, neighbours[i][1], group)
        return tile, group

    def hail(stage):
        pl.semaphore_signal(hello.at[stage], inc=1, device_id=neighbour(stage), device_id_type=MESH)

    def work(g, disp):
        r, part = g // parts, g % parts
        j = part * GROUP

        @pl.when(late & (g == LATE_STEP))
        def _():
            def send(j, carry):
                window_copy(rounds - 1, j).start()
                return carry

            lax.fori_loop(0, half, send, 0)

        @pl.when(g < stages)
        def _():
            hail(g)

        for i in range(GROUP):
            window_copy(r, j + i).wait_recv()
        seconds = spectra([arrived[r, j + i] for i in range(GROUP)], fore_row_ref[...], fore_col_ref[...])
        a, b, c, d = correlate(
            ([(firsts[r, j + i, 0], firsts[r, j + i, 1]) for i in range(GROUP)], (middles[r, part, 0], middles[r, part, 1])),
            seconds,
            back_row_ref[...],
            back_col_ref[...],
        )
        own = r * slots + pick(r, sides) * half + j
        other = r * slots + (1 - pick(r, sides)) * half + j

        @pl.when(g < stages)
        def _():
            pl.semaphore_wait(hello.at[g], 1)

        return (
            disp
            + row_place(a, own)
            + row_place(c, other)
            + row_place(b, own + entries)
            + row_place(d, other + entries)
        )

    for s in range(rounds):
        line_copy(s).wait()
    ids = line[...]
    id_line = jnp.zeros((1, LANES), F32)
    for s in range(rounds):
        theirs = pltpu.roll(lines[s], jnp.where(sides[s] == 0, half, LANES - half), 1)
        in_round = (lane >= s * slots) & (lane < (s + 1) * slots)
        mine = (lane // half) % 2 == sides[s]
        id_line = id_line + jnp.where(in_round, jnp.where(mine, ids, theirs), 0.0)
    done = rounds * parts
    for i in range(done, stages):
        hail(i)
        pl.semaphore_wait(hello.at[i], 1)
    disp = lax.fori_loop(0, done, work, pltpu.roll(id_line, 2 * entries, 1))

    tile_out[...] = disp
    tiles[me] = disp

    def start(i, carry):
        to = i + jnp.where(i >= me, 1, 0)
        pltpu.make_async_remote_copy(
            src_ref=tile_out,
            dst_ref=tiles.at[me],
            send_sem=tile_send,
            recv_sem=tile_recv,
            device_id=(to // groups, to % groups),
            device_id_type=MESH,
        ).start()
        return carry

    lax.fori_loop(0, devices - 1, start, 0)

    def drain(i, carry):
        window_copy(i // half, i % half).wait_send()
        return carry

    lax.fori_loop(0, rounds * half, drain, 0)
    everyone = pltpu.make_async_remote_copy(
        src_ref=tiles.at[pl.ds(0, devices - 1)],
        dst_ref=tiles.at[pl.ds(0, devices - 1)],
        send_sem=tile_send,
        recv_sem=tile_recv,
        device_id=neighbours[0],
        device_id_type=MESH,
    )
    everyone.wait_recv()

    pack = LANES // entries
    node = lax.broadcasted_iota(jnp.int32, (NODE_DEV, LANES), 0).astype(F32)
    first_node = (me * NODE_DEV).astype(F32)
    lane = lax.broadcasted_iota(jnp.int32, (1, LANES), 1)
    onehots = []
    values = []
    for g in range(devices // pack):
        parts = [jnp.zeros((1, LANES), F32)] * 3
        for i in range(pack):
            tile = tiles[g * pack + i]
            here = (lane >= i * entries) & (lane < (i + 1) * entries)
            for c in range(3):
                moved = pltpu.roll(tile, ((i - c) * entries) % LANES, 1) if i != c else tile
                parts[c] = jnp.where(here, moved, parts[c])
        onehots.append(jnp.where(parts[2] - first_node == node, 1.0, 0.0).astype(BF16))
        tile = jnp.concatenate(parts[:2], axis=0)
        hi = tile.astype(BF16).astype(F32)
        rest = tile - hi
        mid = rest.astype(BF16).astype(F32)
        values.append(jnp.concatenate([hi, mid, rest - mid, jnp.zeros_like(hi)], axis=0).astype(BF16))
    result = lax.dot_general(
        jnp.concatenate(values, axis=1),
        jnp.concatenate(onehots, axis=1),
        (((1,), (1,)), ((), ())),
        preferred_element_type=F32,
    )
    out_ref[...] = result[0:2] + (result[2:4] + result[4:6])
    everyone.wait_send()


def on_device(strips, edge_colour, patch_offsets, patch_live, node_ids):
    rounds, height, width = strips.shape
    n = PATCH
    slot_count = patch_offsets.shape[2]
    half = slot_count // 2
    devices = lax.axis_size("tiles") * lax.axis_size("grp")
    whole = pl.BlockSpec(memory_space=VMEM)
    anywhere = pl.BlockSpec(memory_space=pltpu.MemorySpace.HBM)
    sem = pltpu.SemaphoreType.DMA
    windows = (rounds, half, n, n)
    tiled = strips.reshape(rounds, height // SUB, SUB, width // LANES, LANES).transpose(0, 1, 3, 2, 4)
    scalars = [jnp.transpose(patch_offsets, (0, 1, 3, 2)), edge_colour, patch_live, node_ids]
    constants = [jnp.asarray(t) for t in tables()]
    sums = pl.pallas_call(
        stitch,
        out_shape=jax.ShapeDtypeStruct((2, NODE_DEV), F32),
        in_specs=[anywhere] * 9,
        out_specs=whole,
        scratch_shapes=[
            pltpu.SMEM(edge_colour.shape, jnp.int32),
            pltpu.SMEM(scalars[0].shape, jnp.int32),
            pltpu.SMEM(patch_live.shape, jnp.int32),
            pltpu.SMEM(node_ids.shape, jnp.int32),
            pltpu.VMEM(tiled.shape, BF16),
            *(pltpu.VMEM(t.shape, BF16) for t in constants),
            pltpu.VMEM((GROUP, n + SUB, n), F32),
            pltpu.VMEM(windows, BF16),
            pltpu.VMEM((rounds, half, 2, n // 2, n), F32),
            pltpu.VMEM((rounds, half // GROUP, 2, 8, n), F32),
            pltpu.VMEM(windows, BF16),
            pltpu.VMEM((1, LANES), F32),
            pltpu.VMEM((rounds, 1, LANES), F32),
            pltpu.VMEM((1, LANES), F32),
            pltpu.VMEM((devices, 1, LANES), F32),
            sem((4,)),
            sem((rounds, CUTS)),
            sem((4,)),
            sem((rounds, half)),
            sem((rounds, half)),
            sem((rounds,)),
            sem((rounds,)),
            sem(()),
            sem(()),
            pltpu.SemaphoreType.REGULAR((devices.bit_length() - 1,)),
        ],
        compiler_params=pltpu.CompilerParams(collective_id=0, has_side_effects=True, vmem_limit_bytes=VMEM_LIMIT),
        name="stitch",
    )(*(pltpu.with_memory_space_constraint(v, pltpu.MemorySpace.HBM) for v in (edge_colour, scalars[0], patch_live, node_ids, tiled, *constants)))
    return sums


def solution(mesh):
    placed = (
        P(("tiles", "grp"), None, None),
        P(("tiles", "grp"), None),
        P(("tiles", "grp"), None, None, None),
        P(("tiles", "grp"), None),
        P(("tiles", "grp"), None, None),
    )
    return jax.shard_map(
        on_device, mesh=mesh, in_specs=placed, out_specs=P(None, ("tiles", "grp")), check_vma=False
    )
```

```python
import functools
import math

import jax
import jax.numpy as jnp
import numpy as np
from jax import lax
from jax.experimental import pallas as pl
from jax.experimental.pallas import tpu as pltpu
from jax.sharding import PartitionSpec as P

PATCH = 128
NODE_DEV = 128
LANES = 128
GROUP = 4
PAIR = 2
CUTS = 2
SUB = 8
DOT = 2
LATE = {0: (1, 0), 3: (1, 4)}
VMEM_LIMIT = 32 * 1024 * 1024

F32 = jnp.float32
BF16 = jnp.bfloat16
VMEM = pltpu.MemorySpace.VMEM
SMEM = pltpu.MemorySpace.SMEM


def split_np(x):
    hi = np.asarray(x, np.float32).astype(BF16)
    lo = (np.asarray(x, np.float64) - hi.astype(np.float64)).astype(np.float32).astype(BF16)
    return hi, lo


def tables():
    n = PATCH
    h = n // 2
    j = np.arange(n)
    angle = 2.0 * math.pi / n * ((j[:, None] * j[None, :]) % n)
    c, s = np.cos(angle), np.sin(angle)
    rhi, rlo = split_np(np.concatenate([c[: h + 1], s[1:h]], axis=0))
    fore_row = np.concatenate([rhi, rlo], axis=1)
    chi, clo = split_np(np.block([[c, -s], [-s, -c]]))
    fore_col = np.concatenate([chi, clo, chi], axis=0)
    bhi, blo = split_np(np.block([[c, s], [-s, c]]))
    back_col = np.concatenate([bhi, blo, bhi], axis=0)
    weight = np.where(j[:h] == 0, 1.0, 2.0)[None, :]
    ihi, ilo = split_np(np.concatenate([weight * c[:, :h], c[:, h : h + 1], -2.0 * s[:, 1:h]], axis=1) / float(n * n))
    back_row = np.concatenate([ihi, ilo, ihi], axis=1)
    return fore_row, fore_col, back_col, back_row


def split(x):
    hi = x.astype(BF16)
    return hi, (x - hi.astype(F32)).astype(BF16)


def dot(a, b):
    return jnp.dot(a, b, preferred_element_type=F32)


def row_place(column, base):
    count = column.shape[0]
    lane = lax.broadcasted_iota(jnp.int32, (count, LANES), 1)
    sub = lax.broadcasted_iota(jnp.int32, (count, LANES), 0)
    return jnp.sum(jnp.where(lane == sub + base, column, 0.0), axis=0, keepdims=True)


def triple(x):
    hi, lo = split(x)
    return jnp.concatenate([hi, hi, lo], axis=1)


def apply(rows, table):
    out = []
    for p in range(0, len(rows), DOT):
        some = rows[p : p + DOT] if len(rows) - p > DOT + 1 else rows[p:]
        y = dot(jnp.concatenate([triple(v) for v in some], axis=0), table)
        at = 0
        for v in some:
            out.append(y[at : at + v.shape[0]])
            at += v.shape[0]
        if p + len(some) == len(rows):
            return out


def gather_rows(rows):
    sub = lax.broadcasted_iota(jnp.int32, (8, LANES), 0)
    out = jnp.zeros((8, LANES), F32)
    for i, row in enumerate(rows):
        out = jnp.where(sub == i, row, out)
    return out


def spectra(windows, fore_row, fore_col):
    n = PATCH
    h = n // 2
    count = len(windows)
    first = lax.broadcasted_iota(jnp.int32, (8, n), 0) == 0
    mains = []
    middles = []
    for p in range(0, count, 2):
        x = jnp.concatenate(windows[p : p + 2], axis=1)
        y = dot(fore_row, jnp.concatenate([x, x], axis=0))
        for i in range(2):
            part = y[:, i * n : (i + 1) * n]
            middles.append(part[h : h + 1])
            sine = jnp.concatenate([jnp.where(first, 0.0, part[h : h + 8]), part[h + 8 :]], axis=0)
            mains.append(jnp.concatenate([part[:h], sine], axis=1))
    middle = gather_rows(middles)
    mains.append(jnp.concatenate([jnp.concatenate([middle, jnp.zeros_like(middle)], axis=1)] * 2, axis=0))
    parts = apply(mains, fore_col)
    main = [(f[:, :n], f[:, n:]) for f in parts[:-1]]
    return main, (parts[-1][:8, :n], parts[-1][:8, n:])


def fold(v):
    return sum(v[i : i + 8] for i in range(8, v.shape[0], 8)) + v[:8]


def whiten_terms(first, second):
    (r1, i1), (r2, i2) = first, second
    cross_r = r1 * r2 + i1 * i2
    cross_i = i1 * r2 - r1 * i2
    return cross_r, cross_i, jnp.sqrt(cross_r * cross_r + cross_i * cross_i)


def total(v):
    return jnp.sum(v, axis=1, keepdims=True)


def correlate(first, second, back_row, back_col):
    n = PATCH
    h = n // 2
    cells = float(n * n)
    count = len(first[0])
    terms = [whiten_terms(a, b) for a, b in zip(first[0], second[0])]
    middle = whiten_terms(first[1], second[1])

    def spectrum_sum(values, middle_value):
        folded = jnp.concatenate([jnp.sum(fold(v), axis=0, keepdims=True) for v in values], axis=0)
        edge = jnp.concatenate([v[:1] for v in values], axis=0)
        return 2.0 * folded - edge + middle_value[:count], edge

    mag_sum, _ = spectrum_sum([t[2] for t in terms], middle[2])
    extra = 0.1 * (total(mag_sum) / cells) + 1e-06
    inverses = [1.0 / (t[2] + extra[p : p + 1]) for p, t in enumerate(terms)]
    middle_inverse = 1.0 / (middle[2] + gather_rows([extra[p : p + 1] for p in range(count)]))
    rows = [jnp.concatenate([t[0] * v, t[1] * v], axis=1) for t, v in zip(terms, inverses)]
    middle_row = jnp.concatenate([middle[0] * middle_inverse, middle[1] * middle_inverse], axis=1)
    rows.append(jnp.concatenate([middle_row, middle_row], axis=0))

    def power(m, v):
        return (m * v) * (m * v)

    power_sum, edge = spectrum_sum(
        [power(t[2], v) for t, v in zip(terms, inverses)], power(middle[2], middle_inverse)
    )
    lane = lax.broadcasted_iota(jnp.int32, (count, n), 1)
    variance = total(power_sum - jnp.where(lane == 0, edge, 0.0)) / (cells * cells)
    scale = 2.0 / jnp.sqrt(variance + 1e-06) * math.log2(math.e)

    back = apply(rows, back_col)
    middle_back = back[-1][:8, :n]
    first_row = lax.broadcasted_iota(jnp.int32, (8, n), 0) == 0
    surfaces = []
    for p in range(0, count, 2):
        columns = []
        for q in range(p, p + 2):
            part = back[q]
            imag = part[:, n:]
            head = jnp.where(first_row, middle_back[q : q + 1], imag[:8])
            columns.append(jnp.concatenate([part[:, :n], head, imag[8:]], axis=0))
        hi, lo = split(jnp.concatenate(columns, axis=1))
        wide = dot(back_row, jnp.concatenate([hi, hi, lo], axis=0))
        surfaces += [wide[:, :n], wide[:, n:]]

    tops = []
    for surface in surfaces:
        peak = surface[:8]
        for i in range(8, n, 8):
            peak = jnp.maximum(peak, surface[i : i + 8])
        tops.append(jnp.max(peak, axis=0, keepdims=True))
    top = jnp.max(jnp.concatenate(tops, axis=0), axis=1, keepdims=True)
    sub = lax.broadcasted_iota(jnp.int32, (8, n), 0).astype(F32)
    columns = []
    rows = []
    edges = []
    for p in range(count):
        e = jnp.exp2((surfaces[p] - top[p : p + 1]) * scale[p : p + 1])
        part = [e[i : i + 8] for i in range(0, n, 8)]
        upper = part[h // 8 - 1]
        step = upper
        for v in part[h // 8 - 2 : 0 : -1]:
            upper = upper + v
            step = step + upper
        upper = upper + part[0]
        lower = part[h // 8]
        down = lower
        for v in part[h // 8 + 1 :]:
            lower = lower + v
            down = down + lower
        column = upper + lower
        columns.append(jnp.sum(column, axis=0, keepdims=True))
        rows.append(jnp.sum(8.0 * (step - down) + sub * column, axis=0, keepdims=True))
        edges.append(e[h : h + 1, :])
    columns = jnp.concatenate(columns, axis=0)
    rows = jnp.concatenate(rows, axis=0)
    edges = jnp.concatenate(edges, axis=0)
    lane_coord = ((lane + h) % n - h).astype(F32)
    unit = float(n // 8)
    norm = 1.0 / total(columns)
    row_shift = total(rows) * norm / unit
    col_shift = total(columns * lane_coord) * norm / unit
    row_edge = total(edges) * norm * (float(n) / unit)
    col_edge = total(jnp.where(lane == h, columns, 0.0)) * norm * (float(n) / unit)
    return row_shift, col_shift, -row_shift - row_edge, -col_shift - col_edge


MESH = pl.DeviceIdType.MESH


def stitch(
    colour_hbm,
    offset_hbm,
    live_hbm,
    ids_hbm,
    strips_hbm,
    fore_row_hbm,
    fore_col_hbm,
    back_col_hbm,
    back_row_hbm,
    out_ref,
    colour_ref,
    offset_ref,
    live_ref,
    ids_ref,
    strips,
    fore_row_ref,
    fore_col_ref,
    back_col_ref,
    back_row_ref,
    shifted,
    sent,
    firsts,
    middles,
    arrived,
    line,
    lines,
    tile_out,
    tiles,
    scalar_sem,
    strip_sem,
    table_sem,
    window_send,
    window_recv,
    line_send,
    line_recv,
    tile_send,
    tile_recv,
    hello,
):
    n = PATCH
    rounds, layers, blocks = strips.shape[:3]
    slots = offset_ref.shape[3]
    half = slots // 2
    entries = rounds * slots
    groups = lax.axis_size("grp")
    tile_count = lax.axis_size("tiles")
    devices = tile_count * groups
    tile_index = lax.axis_index("tiles")
    group_index = lax.axis_index("grp")
    me = tile_index * groups + group_index
    strides = [1] + [tile_count // 2] * (rounds - 1)
    sides = [(tile_index // s) % 2 for s in strides]
    partners = [tile_index + s * (1 - 2 * side) for s, side in zip(strides, sides)]

    barrier = pltpu.get_barrier_semaphore()
    neighbours = []
    stride = 1
    while stride < tile_count:
        bit = (tile_index // stride) % 2
        neighbours.append((tile_index + stride * (1 - 2 * bit), group_index))
        stride *= 2
    stride = 1
    while stride < groups:
        bit = (group_index // stride) % 2
        neighbours.append((tile_index, group_index + stride * (1 - 2 * bit)))
        stride *= 2
    stages = len(neighbours)
    for at in neighbours:
        pl.semaphore_signal(barrier, inc=1, device_id=at, device_id_type=MESH)

    scalar_loads = [
        pltpu.make_async_copy(a, b, scalar_sem.at[i])
        for i, (a, b) in enumerate(
            [(offset_hbm, offset_ref), (colour_hbm, colour_ref), (live_hbm, live_ref), (ids_hbm, ids_ref)]
        )
    ]
    for load in scalar_loads:
        load.start()
    strip_loads = [
        pltpu.make_async_copy(strips_hbm.at[r, pl.ds(i, layers // CUTS)], strips.at[r, pl.ds(i, layers // CUTS)], strip_sem.at[r, c])
        for r in range(rounds)
        for c, i in enumerate(range(0, layers, layers // CUTS))
    ]
    for load in strip_loads:
        load.start()
    table_loads = [
        pltpu.make_async_copy(a, b, table_sem.at[i])
        for i, (a, b) in enumerate(
            [(fore_row_hbm, fore_row_ref), (fore_col_hbm, fore_col_ref), (back_col_hbm, back_col_ref), (back_row_hbm, back_row_ref)]
        )
    ]
    def extract(r, picks):
        rests = []
        lane = lax.broadcasted_iota(jnp.int32, (n + SUB, LANES), 1)
        for i, k in enumerate(picks):
            row, column = offset_ref[0, r, 0, k], offset_ref[0, r, 1, k]
            block = jnp.minimum(lax.div(column, LANES), blocks - 2)
            layer = jnp.minimum(lax.div(row, SUB), layers - n // SUB - 1)
            shift = column - block * LANES
            turn = lax.rem(2 * LANES - shift, LANES)
            left, right = (
                pltpu.roll(
                    strips[colour_ref[0, r], pl.ds(layer, n // SUB + 1), block + side]
                    .reshape(n + SUB, LANES)
                    .astype(F32),
                    turn,
                    1,
                )
                for side in range(2)
            )
            shifted[i] = jnp.where(lane < LANES - shift, left, right)
            rests.append(row - layer * SUB)
        return [shifted[i, pl.ds(rest, n), :].astype(BF16) for i, rest in enumerate(rests)]

    def pick(r, values):
        value = values[0]
        for i in range(1, rounds):
            value = jnp.where(r == i, values[i], value)
        return value

    def window_copy(r, j):
        return pltpu.make_async_remote_copy(
            src_ref=sent.at[r, j],
            dst_ref=arrived.at[r, j],
            send_sem=window_send.at[r, j],
            recv_sem=window_recv.at[r, j],
            device_id=(pick(r, partners), group_index),
            device_id_type=MESH,
        )

    def line_copy(r):
        return pltpu.make_async_remote_copy(
            src_ref=line,
            dst_ref=lines.at[r],
            send_sem=line_send.at[r],
            recv_sem=line_recv.at[r],
            device_id=(partners[r], group_index),
            device_id_type=MESH,
        )

    for load in scalar_loads:
        load.wait()
    lane = lax.broadcasted_iota(jnp.int32, (1, LANES), 1)

    def place_id(i, ids):
        r, k = i // slots, i % slots
        return jnp.where(lane == i, jnp.where(k < live_ref[0, r], ids_ref[0, r, k], -1), ids)

    line[...] = lax.fori_loop(0, entries, place_id, jnp.zeros((1, LANES), jnp.int32)).astype(F32)
    for load in strip_loads:
        load.wait()
    for load in table_loads:
        load.start()
    pl.semaphore_wait(barrier, stages)
    for r in range(rounds):
        line_copy(r).start()

    def place_of(q):
        return rounds - 1 - q % rounds, (q // rounds) * PAIR

    def launch(q):
        r, j = place_of(q)
        for i in range(PAIR):
            window_copy(r, j + i).start()

    def produce(q, carry):
        r, j = place_of(q)
        base = (1 - pick(r, sides)) * half + j
        for i, window in enumerate(extract(r, [base + i for i in range(PAIR)])):
            sent[r, j + i] = window

        before, window = place_of(q - 1)

        @pl.when((q > 0) & ((before < rounds - 1) | (window < late_from)))
        def _():
            launch(q - 1)

        return carry

    quarter = tile_index // (tile_count // 4)
    late_from, late_step = half, -1
    for at, (step, window) in LATE.items():
        late_from = jnp.where(quarter == at, window, late_from)
        late_step = jnp.where(quarter == at, step, late_step)
    lax.fori_loop(0, rounds * half // PAIR, produce, 0)
    for load in table_loads:
        load.wait()
    launch(rounds * half // PAIR - 1)
    parts = half // GROUP

    def prepare(g, carry):
        r, part = g // parts, g % parts
        j = part * GROUP
        windows = extract(r, [pick(r, sides) * half + j + i for i in range(GROUP)])
        main, middle = spectra(windows, fore_row_ref[...], fore_col_ref[...])
        for c in range(2):
            for i in range(GROUP):
                firsts[r, j + i, c] = main[i][c]
            middles[r, part, c] = middle[c]
        return carry

    lax.fori_loop(0, rounds * parts, prepare, 0)

    def neighbour(stage):
        tile, group = neighbours[0]
        for i in range(1, stages):
            tile = jnp.where(stage == i, neighbours[i][0], tile)
            group = jnp.where(stage == i, neighbours[i][1], group)
        return tile, group

    def hail(stage):
        pl.semaphore_signal(hello.at[stage], inc=1, device_id=neighbour(stage), device_id_type=MESH)

    def work(g, disp):
        r, part = g // parts, g % parts
        j = part * GROUP

        @pl.when(g == late_step)
        def _():
            def send(j, carry):
                window_copy(rounds - 1, j).start()
                return carry

            lax.fori_loop(late_from, half, send, 0)

        @pl.when(g < stages)
        def _():
            hail(g)

        for i in range(GROUP):
            window_copy(r, j + i).wait_recv()
        seconds = spectra([arrived[r, j + i] for i in range(GROUP)], fore_row_ref[...], fore_col_ref[...])
        a, b, c, d = correlate(
            ([(firsts[r, j + i, 0], firsts[r, j + i, 1]) for i in range(GROUP)], (middles[r, part, 0], middles[r, part, 1])),
            seconds,
            back_row_ref[...],
            back_col_ref[...],
        )
        own = r * slots + pick(r, sides) * half + j
        other = r * slots + (1 - pick(r, sides)) * half + j

        @pl.when(g < stages)
        def _():
            pl.semaphore_wait(hello.at[g], 1)

        return (
            disp
            + row_place(a, own)
            + row_place(c, other)
            + row_place(b, own + entries)
            + row_place(d, other + entries)
        )

    for s in range(rounds):
        line_copy(s).wait()
    ids = line[...]
    id_line = jnp.zeros((1, LANES), F32)
    for s in range(rounds):
        theirs = pltpu.roll(lines[s], jnp.where(sides[s] == 0, half, LANES - half), 1)
        in_round = (lane >= s * slots) & (lane < (s + 1) * slots)
        mine = (lane // half) % 2 == sides[s]
        id_line = id_line + jnp.where(in_round, jnp.where(mine, ids, theirs), 0.0)
    done = rounds * parts
    for i in range(done, stages):
        hail(i)
        pl.semaphore_wait(hello.at[i], 1)
    disp = lax.fori_loop(0, done, work, pltpu.roll(id_line, 2 * entries, 1))

    tile_out[...] = disp
    tiles[me] = disp

    def start(i, carry):
        to = i + jnp.where(i >= me, 1, 0)
        pltpu.make_async_remote_copy(
            src_ref=tile_out,
            dst_ref=tiles.at[me],
            send_sem=tile_send,
            recv_sem=tile_recv,
            device_id=(to // groups, to % groups),
            device_id_type=MESH,
        ).start()
        return carry

    lax.fori_loop(0, devices - 1, start, 0)

    def drain(i, carry):
        window_copy(i // half, i % half).wait_send()
        return carry

    lax.fori_loop(0, rounds * half, drain, 0)
    everyone = pltpu.make_async_remote_copy(
        src_ref=tiles.at[pl.ds(0, devices - 1)],
        dst_ref=tiles.at[pl.ds(0, devices - 1)],
        send_sem=tile_send,
        recv_sem=tile_recv,
        device_id=neighbours[0],
        device_id_type=MESH,
    )
    everyone.wait_recv()

    pack = LANES // entries
    node = lax.broadcasted_iota(jnp.int32, (NODE_DEV, LANES), 0).astype(F32)
    first_node = (me * NODE_DEV).astype(F32)
    lane = lax.broadcasted_iota(jnp.int32, (1, LANES), 1)
    onehots = []
    values = []
    for g in range(devices // pack):
        parts = [jnp.zeros((1, LANES), F32)] * 3
        for i in range(pack):
            tile = tiles[g * pack + i]
            here = (lane >= i * entries) & (lane < (i + 1) * entries)
            for c in range(3):
                moved = pltpu.roll(tile, ((i - c) * entries) % LANES, 1) if i != c else tile
                parts[c] = jnp.where(here, moved, parts[c])
        onehots.append(jnp.where(parts[2] - first_node == node, 1.0, 0.0).astype(BF16))
        tile = jnp.concatenate(parts[:2], axis=0)
        hi = tile.astype(BF16).astype(F32)
        rest = tile - hi
        mid = rest.astype(BF16).astype(F32)
        values.append(jnp.concatenate([hi, mid, rest - mid, jnp.zeros_like(hi)], axis=0).astype(BF16))
    result = lax.dot_general(
        jnp.concatenate(values, axis=1),
        jnp.concatenate(onehots, axis=1),
        (((1,), (1,)), ((), ())),
        preferred_element_type=F32,
    )
    out_ref[...] = result[0:2] + (result[2:4] + result[4:6])
    everyone.wait_send()


def on_device(strips, edge_colour, patch_offsets, patch_live, node_ids):
    rounds, height, width = strips.shape
    n = PATCH
    slot_count = patch_offsets.shape[2]
    half = slot_count // 2
    devices = lax.axis_size("tiles") * lax.axis_size("grp")
    whole = pl.BlockSpec(memory_space=VMEM)
    anywhere = pl.BlockSpec(memory_space=pltpu.MemorySpace.HBM)
    sem = pltpu.SemaphoreType.DMA
    windows = (rounds, half, n, n)
    tiled = strips.reshape(rounds, height // SUB, SUB, width // LANES, LANES).transpose(0, 1, 3, 2, 4)
    scalars = [jnp.transpose(patch_offsets, (0, 1, 3, 2)), edge_colour, patch_live, node_ids]
    constants = [jnp.asarray(t) for t in tables()]
    sums = pl.pallas_call(
        stitch,
        out_shape=jax.ShapeDtypeStruct((2, NODE_DEV), F32),
        in_specs=[anywhere] * 9,
        out_specs=whole,
        scratch_shapes=[
            pltpu.SMEM(edge_colour.shape, jnp.int32),
            pltpu.SMEM(scalars[0].shape, jnp.int32),
            pltpu.SMEM(patch_live.shape, jnp.int32),
            pltpu.SMEM(node_ids.shape, jnp.int32),
            pltpu.VMEM(tiled.shape, BF16),
            *(pltpu.VMEM(t.shape, BF16) for t in constants),
            pltpu.VMEM((GROUP, n + SUB, n), F32),
            pltpu.VMEM(windows, BF16),
            pltpu.VMEM((rounds, half, 2, n // 2, n), F32),
            pltpu.VMEM((rounds, half // GROUP, 2, 8, n), F32),
            pltpu.VMEM(windows, BF16),
            pltpu.VMEM((1, LANES), F32),
            pltpu.VMEM((rounds, 1, LANES), F32),
            pltpu.VMEM((1, LANES), F32),
            pltpu.VMEM((devices, 1, LANES), F32),
            sem((4,)),
            sem((rounds, CUTS)),
            sem((4,)),
            sem((rounds, half)),
            sem((rounds, half)),
            sem((rounds,)),
            sem((rounds,)),
            sem(()),
            sem(()),
            pltpu.SemaphoreType.REGULAR((devices.bit_length() - 1,)),
        ],
        compiler_params=pltpu.CompilerParams(collective_id=0, has_side_effects=True, vmem_limit_bytes=VMEM_LIMIT),
        name="stitch",
    )(*(pltpu.with_memory_space_constraint(v, pltpu.MemorySpace.HBM) for v in (edge_colour, scalars[0], patch_live, node_ids, tiled, *constants)))
    return sums


def solution(mesh):
    placed = (
        P(("tiles", "grp"), None, None),
        P(("tiles", "grp"), None),
        P(("tiles", "grp"), None, None, None),
        P(("tiles", "grp"), None),
        P(("tiles", "grp"), None, None),
    )
    return jax.shard_map(
        on_device, mesh=mesh, in_specs=placed, out_specs=P(None, ("tiles", "grp")), check_vma=False
    )
```

```python
import functools
import math

import jax
import jax.numpy as jnp
import numpy as np
from jax import lax
from jax.experimental import pallas as pl
from jax.experimental.pallas import tpu as pltpu
from jax.sharding import PartitionSpec as P

PATCH = 128
NODE_DEV = 128
LANES = 128
GROUP = 4
PAIR = 2
CUTS = 2
SUB = 8
DOT = 2
LATE = {0: (1, 0), 3: (0, 0)}
VMEM_LIMIT = 32 * 1024 * 1024

F32 = jnp.float32
BF16 = jnp.bfloat16
VMEM = pltpu.MemorySpace.VMEM
SMEM = pltpu.MemorySpace.SMEM


def split_np(x):
    hi = np.asarray(x, np.float32).astype(BF16)
    lo = (np.asarray(x, np.float64) - hi.astype(np.float64)).astype(np.float32).astype(BF16)
    return hi, lo


def tables():
    n = PATCH
    h = n // 2
    j = np.arange(n)
    angle = 2.0 * math.pi / n * ((j[:, None] * j[None, :]) % n)
    c, s = np.cos(angle), np.sin(angle)
    rhi, rlo = split_np(np.concatenate([c[: h + 1], s[1:h]], axis=0))
    fore_row = np.concatenate([rhi, rlo], axis=1)
    chi, clo = split_np(np.block([[c, -s], [-s, -c]]))
    fore_col = np.concatenate([chi, clo, chi], axis=0)
    bhi, blo = split_np(np.block([[c, s], [-s, c]]))
    back_col = np.concatenate([bhi, blo, bhi], axis=0)
    weight = np.where(j[:h] == 0, 1.0, 2.0)[None, :]
    ihi, ilo = split_np(np.concatenate([weight * c[:, :h], c[:, h : h + 1], -2.0 * s[:, 1:h]], axis=1) / float(n * n))
    back_row = np.concatenate([ihi, ilo, ihi], axis=1)
    return fore_row, fore_col, back_col, back_row


def split(x):
    hi = x.astype(BF16)
    return hi, (x - hi.astype(F32)).astype(BF16)


def dot(a, b):
    return jnp.dot(a, b, preferred_element_type=F32)


def row_place(column, base):
    count = column.shape[0]
    lane = lax.broadcasted_iota(jnp.int32, (count, LANES), 1)
    sub = lax.broadcasted_iota(jnp.int32, (count, LANES), 0)
    return jnp.sum(jnp.where(lane == sub + base, column, 0.0), axis=0, keepdims=True)


def triple(x):
    hi, lo = split(x)
    return jnp.concatenate([hi, hi, lo], axis=1)


def apply(rows, table):
    out = []
    for p in range(0, len(rows), DOT):
        some = rows[p : p + DOT] if len(rows) - p > DOT + 1 else rows[p:]
        y = dot(jnp.concatenate([triple(v) for v in some], axis=0), table)
        at = 0
        for v in some:
            out.append(y[at : at + v.shape[0]])
            at += v.shape[0]
        if p + len(some) == len(rows):
            return out


def gather_rows(rows):
    sub = lax.broadcasted_iota(jnp.int32, (8, LANES), 0)
    out = jnp.zeros((8, LANES), F32)
    for i, row in enumerate(rows):
        out = jnp.where(sub == i, row, out)
    return out


def spectra(windows, fore_row, fore_col):
    n = PATCH
    h = n // 2
    count = len(windows)
    first = lax.broadcasted_iota(jnp.int32, (8, n), 0) == 0
    mains = []
    middles = []
    for p in range(0, count, 2):
        x = jnp.concatenate(windows[p : p + 2], axis=1)
        y = dot(fore_row, jnp.concatenate([x, x], axis=0))
        for i in range(2):
            part = y[:, i * n : (i + 1) * n]
            middles.append(part[h : h + 1])
            sine = jnp.concatenate([jnp.where(first, 0.0, part[h : h + 8]), part[h + 8 :]], axis=0)
            mains.append(jnp.concatenate([part[:h], sine], axis=1))
    middle = gather_rows(middles)
    mains.append(jnp.concatenate([jnp.concatenate([middle, jnp.zeros_like(middle)], axis=1)] * 2, axis=0))
    parts = apply(mains, fore_col)
    main = [(f[:, :n], f[:, n:]) for f in parts[:-1]]
    return main, (parts[-1][:8, :n], parts[-1][:8, n:])


def fold(v):
    return sum(v[i : i + 8] for i in range(8, v.shape[0], 8)) + v[:8]


def whiten_terms(first, second):
    (r1, i1), (r2, i2) = first, second
    cross_r = r1 * r2 + i1 * i2
    cross_i = i1 * r2 - r1 * i2
    return cross_r, cross_i, jnp.sqrt(cross_r * cross_r + cross_i * cross_i)


def total(v):
    return jnp.sum(v, axis=1, keepdims=True)


def correlate(first, second, back_row, back_col):
    n = PATCH
    h = n // 2
    cells = float(n * n)
    count = len(first[0])
    terms = [whiten_terms(a, b) for a, b in zip(first[0], second[0])]
    middle = whiten_terms(first[1], second[1])

    def spectrum_sum(values, middle_value):
        folded = jnp.concatenate([jnp.sum(fold(v), axis=0, keepdims=True) for v in values], axis=0)
        edge = jnp.concatenate([v[:1] for v in values], axis=0)
        return 2.0 * folded - edge + middle_value[:count], edge

    mag_sum, _ = spectrum_sum([t[2] for t in terms], middle[2])
    extra = 0.1 * (total(mag_sum) / cells) + 1e-06
    inverses = [1.0 / (t[2] + extra[p : p + 1]) for p, t in enumerate(terms)]
    middle_inverse = 1.0 / (middle[2] + gather_rows([extra[p : p + 1] for p in range(count)]))
    rows = [jnp.concatenate([t[0] * v, t[1] * v], axis=1) for t, v in zip(terms, inverses)]
    middle_row = jnp.concatenate([middle[0] * middle_inverse, middle[1] * middle_inverse], axis=1)
    rows.append(jnp.concatenate([middle_row, middle_row], axis=0))

    def power(m, v):
        return (m * v) * (m * v)

    power_sum, edge = spectrum_sum(
        [power(t[2], v) for t, v in zip(terms, inverses)], power(middle[2], middle_inverse)
    )
    lane = lax.broadcasted_iota(jnp.int32, (count, n), 1)
    variance = total(power_sum - jnp.where(lane == 0, edge, 0.0)) / (cells * cells)
    scale = 2.0 / jnp.sqrt(variance + 1e-06) * math.log2(math.e)

    back = apply(rows, back_col)
    middle_back = back[-1][:8, :n]
    first_row = lax.broadcasted_iota(jnp.int32, (8, n), 0) == 0
    surfaces = []
    for p in range(0, count, 2):
        columns = []
        for q in range(p, p + 2):
            part = back[q]
            imag = part[:, n:]
            head = jnp.where(first_row, middle_back[q : q + 1], imag[:8])
            columns.append(jnp.concatenate([part[:, :n], head, imag[8:]], axis=0))
        hi, lo = split(jnp.concatenate(columns, axis=1))
        wide = dot(back_row, jnp.concatenate([hi, hi, lo], axis=0))
        surfaces += [wide[:, :n], wide[:, n:]]

    tops = []
    for surface in surfaces:
        peak = surface[:8]
        for i in range(8, n, 8):
            peak = jnp.maximum(peak, surface[i : i + 8])
        tops.append(jnp.max(peak, axis=0, keepdims=True))
    top = jnp.max(jnp.concatenate(tops, axis=0), axis=1, keepdims=True)
    sub = lax.broadcasted_iota(jnp.int32, (8, n), 0).astype(F32)
    columns = []
    rows = []
    edges = []
    for p in range(count):
        e = jnp.exp2((surfaces[p] - top[p : p + 1]) * scale[p : p + 1])
        part = [e[i : i + 8] for i in range(0, n, 8)]
        upper = part[h // 8 - 1]
        step = upper
        for v in part[h // 8 - 2 : 0 : -1]:
            upper = upper + v
            step = step + upper
        upper = upper + part[0]
        lower = part[h // 8]
        down = lower
        for v in part[h // 8 + 1 :]:
            lower = lower + v
            down = down + lower
        column = upper + lower
        columns.append(jnp.sum(column, axis=0, keepdims=True))
        rows.append(jnp.sum(8.0 * (step - down) + sub * column, axis=0, keepdims=True))
        edges.append(e[h : h + 1, :])
    columns = jnp.concatenate(columns, axis=0)
    rows = jnp.concatenate(rows, axis=0)
    edges = jnp.concatenate(edges, axis=0)
    lane_coord = ((lane + h) % n - h).astype(F32)
    unit = float(n // 8)
    norm = 1.0 / total(columns)
    row_shift = total(rows) * norm / unit
    col_shift = total(columns * lane_coord) * norm / unit
    row_edge = total(edges) * norm * (float(n) / unit)
    col_edge = total(jnp.where(lane == h, columns, 0.0)) * norm * (float(n) / unit)
    return row_shift, col_shift, -row_shift - row_edge, -col_shift - col_edge


MESH = pl.DeviceIdType.MESH


def stitch(
    colour_hbm,
    offset_hbm,
    live_hbm,
    ids_hbm,
    strips_hbm,
    fore_row_hbm,
    fore_col_hbm,
    back_col_hbm,
    back_row_hbm,
    out_ref,
    colour_ref,
    offset_ref,
    live_ref,
    ids_ref,
    strips,
    fore_row_ref,
    fore_col_ref,
    back_col_ref,
    back_row_ref,
    shifted,
    sent,
    firsts,
    middles,
    arrived,
    line,
    lines,
    tile_out,
    tiles,
    scalar_sem,
    strip_sem,
    table_sem,
    window_send,
    window_recv,
    line_send,
    line_recv,
    tile_send,
    tile_recv,
    hello,
):
    n = PATCH
    rounds, layers, blocks = strips.shape[:3]
    slots = offset_ref.shape[3]
    half = slots // 2
    entries = rounds * slots
    groups = lax.axis_size("grp")
    tile_count = lax.axis_size("tiles")
    devices = tile_count * groups
    tile_index = lax.axis_index("tiles")
    group_index = lax.axis_index("grp")
    me = tile_index * groups + group_index
    strides = [1] + [tile_count // 2] * (rounds - 1)
    sides = [(tile_index // s) % 2 for s in strides]
    partners = [tile_index + s * (1 - 2 * side) for s, side in zip(strides, sides)]

    barrier = pltpu.get_barrier_semaphore()
    neighbours = []
    stride = 1
    while stride < tile_count:
        bit = (tile_index // stride) % 2
        neighbours.append((tile_index + stride * (1 - 2 * bit), group_index))
        stride *= 2
    stride = 1
    while stride < groups:
        bit = (group_index // stride) % 2
        neighbours.append((tile_index, group_index + stride * (1 - 2 * bit)))
        stride *= 2
    stages = len(neighbours)
    for at in neighbours:
        pl.semaphore_signal(barrier, inc=1, device_id=at, device_id_type=MESH)

    scalar_loads = [
        pltpu.make_async_copy(a, b, scalar_sem.at[i])
        for i, (a, b) in enumerate(
            [(offset_hbm, offset_ref), (colour_hbm, colour_ref), (live_hbm, live_ref), (ids_hbm, ids_ref)]
        )
    ]
    for load in scalar_loads:
        load.start()
    strip_loads = [
        pltpu.make_async_copy(strips_hbm.at[r, pl.ds(i, layers // CUTS)], strips.at[r, pl.ds(i, layers // CUTS)], strip_sem.at[r, c])
        for r in range(rounds)
        for c, i in enumerate(range(0, layers, layers // CUTS))
    ]
    for load in strip_loads:
        load.start()
    table_loads = [
        pltpu.make_async_copy(a, b, table_sem.at[i])
        for i, (a, b) in enumerate(
            [(fore_row_hbm, fore_row_ref), (fore_col_hbm, fore_col_ref), (back_col_hbm, back_col_ref), (back_row_hbm, back_row_ref)]
        )
    ]
    def extract(r, picks):
        rests = []
        lane = lax.broadcasted_iota(jnp.int32, (n + SUB, LANES), 1)
        for i, k in enumerate(picks):
            row, column = offset_ref[0, r, 0, k], offset_ref[0, r, 1, k]
            block = jnp.minimum(lax.div(column, LANES), blocks - 2)
            layer = jnp.minimum(lax.div(row, SUB), layers - n // SUB - 1)
            shift = column - block * LANES
            turn = lax.rem(2 * LANES - shift, LANES)
            left, right = (
                pltpu.roll(
                    strips[colour_ref[0, r], pl.ds(layer, n // SUB + 1), block + side]
                    .reshape(n + SUB, LANES)
                    .astype(F32),
                    turn,
                    1,
                )
                for side in range(2)
            )
            shifted[i] = jnp.where(lane < LANES - shift, left, right)
            rests.append(row - layer * SUB)
        return [shifted[i, pl.ds(rest, n), :].astype(BF16) for i, rest in enumerate(rests)]

    def pick(r, values):
        value = values[0]
        for i in range(1, rounds):
            value = jnp.where(r == i, values[i], value)
        return value

    def window_copy(r, j):
        return pltpu.make_async_remote_copy(
            src_ref=sent.at[r, j],
            dst_ref=arrived.at[r, j],
            send_sem=window_send.at[r, j],
            recv_sem=window_recv.at[r, j],
            device_id=(pick(r, partners), group_index),
            device_id_type=MESH,
        )

    def line_copy(r):
        return pltpu.make_async_remote_copy(
            src_ref=line,
            dst_ref=lines.at[r],
            send_sem=line_send.at[r],
            recv_sem=line_recv.at[r],
            device_id=(partners[r], group_index),
            device_id_type=MESH,
        )

    for load in scalar_loads:
        load.wait()
    lane = lax.broadcasted_iota(jnp.int32, (1, LANES), 1)

    def place_id(i, ids):
        r, k = i // slots, i % slots
        return jnp.where(lane == i, jnp.where(k < live_ref[0, r], ids_ref[0, r, k], -1), ids)

    line[...] = lax.fori_loop(0, entries, place_id, jnp.zeros((1, LANES), jnp.int32)).astype(F32)
    for load in strip_loads:
        load.wait()
    for load in table_loads:
        load.start()
    pl.semaphore_wait(barrier, stages)
    for r in range(rounds):
        line_copy(r).start()

    def place_of(q):
        return rounds - 1 - q // (half // PAIR), q % (half // PAIR) * PAIR

    def launch(q):
        r, j = place_of(q)
        for i in range(PAIR):
            window_copy(r, j + i).start()

    def produce(q, carry):
        r, j = place_of(q)
        base = (1 - pick(r, sides)) * half + j
        for i, window in enumerate(extract(r, [base + i for i in range(PAIR)])):
            sent[r, j + i] = window

        before, window = place_of(q - 1)

        @pl.when((q > 0) & ((before < rounds - 1) | (window < late_from)))
        def _():
            launch(q - 1)

        return carry

    quarter = tile_index // (tile_count // 4)
    late_from, late_step = half, -1
    for at, (step, window) in LATE.items():
        late_from = jnp.where(quarter == at, window, late_from)
        late_step = jnp.where(quarter == at, step, late_step)
    lax.fori_loop(0, rounds * half // PAIR, produce, 0)
    for load in table_loads:
        load.wait()
    launch(rounds * half // PAIR - 1)
    parts = half // GROUP

    def prepare(g, carry):
        r, part = g // parts, g % parts
        j = part * GROUP
        windows = extract(r, [pick(r, sides) * half + j + i for i in range(GROUP)])
        main, middle = spectra(windows, fore_row_ref[...], fore_col_ref[...])
        for c in range(2):
            for i in range(GROUP):
                firsts[r, j + i, c] = main[i][c]
            middles[r, part, c] = middle[c]
        return carry

    lax.fori_loop(0, rounds * parts, prepare, 0)

    def neighbour(stage):
        tile, group = neighbours[0]
        for i in range(1, stages):
            tile = jnp.where(stage == i, neighbours[i][0], tile)
            group = jnp.where(stage == i, neighbours[i][1], group)
        return tile, group

    def hail(stage):
        pl.semaphore_signal(hello.at[stage], inc=1, device_id=neighbour(stage), device_id_type=MESH)

    def work(g, disp):
        r, part = g // parts, g % parts
        j = part * GROUP

        @pl.when(g == late_step)
        def _():
            def send(j, carry):
                window_copy(rounds - 1, j).start()
                return carry

            lax.fori_loop(late_from, half, send, 0)

        @pl.when(g < stages)
        def _():
            hail(g)

        for i in range(GROUP):
            window_copy(r, j + i).wait_recv()
        seconds = spectra([arrived[r, j + i] for i in range(GROUP)], fore_row_ref[...], fore_col_ref[...])
        a, b, c, d = correlate(
            ([(firsts[r, j + i, 0], firsts[r, j + i, 1]) for i in range(GROUP)], (middles[r, part, 0], middles[r, part, 1])),
            seconds,
            back_row_ref[...],
            back_col_ref[...],
        )
        own = r * slots + pick(r, sides) * half + j
        other = r * slots + (1 - pick(r, sides)) * half + j

        @pl.when(g < stages)
        def _():
            pl.semaphore_wait(hello.at[g], 1)

        return (
            disp
            + row_place(a, own)
            + row_place(c, other)
            + row_place(b, own + entries)
            + row_place(d, other + entries)
        )

    for s in range(rounds):
        line_copy(s).wait()
    ids = line[...]
    id_line = jnp.zeros((1, LANES), F32)
    for s in range(rounds):
        theirs = pltpu.roll(lines[s], jnp.where(sides[s] == 0, half, LANES - half), 1)
        in_round = (lane >= s * slots) & (lane < (s + 1) * slots)
        mine = (lane // half) % 2 == sides[s]
        id_line = id_line + jnp.where(in_round, jnp.where(mine, ids, theirs), 0.0)
    done = rounds * parts
    for i in range(done, stages):
        hail(i)
        pl.semaphore_wait(hello.at[i], 1)
    disp = lax.fori_loop(0, done, work, pltpu.roll(id_line, 2 * entries, 1))

    tile_out[...] = disp
    tiles[me] = disp

    def start(i, carry):
        to = i + jnp.where(i >= me, 1, 0)
        pltpu.make_async_remote_copy(
            src_ref=tile_out,
            dst_ref=tiles.at[me],
            send_sem=tile_send,
            recv_sem=tile_recv,
            device_id=(to // groups, to % groups),
            device_id_type=MESH,
        ).start()
        return carry

    lax.fori_loop(0, devices - 1, start, 0)

    def drain(i, carry):
        window_copy(i // half, i % half).wait_send()
        return carry

    lax.fori_loop(0, rounds * half, drain, 0)
    everyone = pltpu.make_async_remote_copy(
        src_ref=tiles.at[pl.ds(0, devices - 1)],
        dst_ref=tiles.at[pl.ds(0, devices - 1)],
        send_sem=tile_send,
        recv_sem=tile_recv,
        device_id=neighbours[0],
        device_id_type=MESH,
    )
    everyone.wait_recv()

    pack = LANES // entries
    node = lax.broadcasted_iota(jnp.int32, (NODE_DEV, LANES), 0).astype(F32)
    first_node = (me * NODE_DEV).astype(F32)
    lane = lax.broadcasted_iota(jnp.int32, (1, LANES), 1)
    onehots = []
    values = []
    for g in range(devices // pack):
        parts = [jnp.zeros((1, LANES), F32)] * 3
        for i in range(pack):
            tile = tiles[g * pack + i]
            here = (lane >= i * entries) & (lane < (i + 1) * entries)
            for c in range(3):
                moved = pltpu.roll(tile, ((i - c) * entries) % LANES, 1) if i != c else tile
                parts[c] = jnp.where(here, moved, parts[c])
        onehots.append(jnp.where(parts[2] - first_node == node, 1.0, 0.0).astype(BF16))
        tile = jnp.concatenate(parts[:2], axis=0)
        hi = tile.astype(BF16).astype(F32)
        rest = tile - hi
        mid = rest.astype(BF16).astype(F32)
        values.append(jnp.concatenate([hi, mid, rest - mid, jnp.zeros_like(hi)], axis=0).astype(BF16))
    result = lax.dot_general(
        jnp.concatenate(values, axis=1),
        jnp.concatenate(onehots, axis=1),
        (((1,), (1,)), ((), ())),
        preferred_element_type=F32,
    )
    out_ref[...] = result[0:2] + (result[2:4] + result[4:6])
    everyone.wait_send()


def on_device(strips, edge_colour, patch_offsets, patch_live, node_ids):
    rounds, height, width = strips.shape
    n = PATCH
    slot_count = patch_offsets.shape[2]
    half = slot_count // 2
    devices = lax.axis_size("tiles") * lax.axis_size("grp")
    whole = pl.BlockSpec(memory_space=VMEM)
    anywhere = pl.BlockSpec(memory_space=pltpu.MemorySpace.HBM)
    sem = pltpu.SemaphoreType.DMA
    windows = (rounds, half, n, n)
    tiled = strips.reshape(rounds, height // SUB, SUB, width // LANES, LANES).transpose(0, 1, 3, 2, 4)
    scalars = [jnp.transpose(patch_offsets, (0, 1, 3, 2)), edge_colour, patch_live, node_ids]
    constants = [jnp.asarray(t) for t in tables()]
    sums = pl.pallas_call(
        stitch,
        out_shape=jax.ShapeDtypeStruct((2, NODE_DEV), F32),
        in_specs=[anywhere] * 9,
        out_specs=whole,
        scratch_shapes=[
            pltpu.SMEM(edge_colour.shape, jnp.int32),
            pltpu.SMEM(scalars[0].shape, jnp.int32),
            pltpu.SMEM(patch_live.shape, jnp.int32),
            pltpu.SMEM(node_ids.shape, jnp.int32),
            pltpu.VMEM(tiled.shape, BF16),
            *(pltpu.VMEM(t.shape, BF16) for t in constants),
            pltpu.VMEM((GROUP, n + SUB, n), F32),
            pltpu.VMEM(windows, BF16),
            pltpu.VMEM((rounds, half, 2, n // 2, n), F32),
            pltpu.VMEM((rounds, half // GROUP, 2, 8, n), F32),
            pltpu.VMEM(windows, BF16),
            pltpu.VMEM((1, LANES), F32),
            pltpu.VMEM((rounds, 1, LANES), F32),
            pltpu.VMEM((1, LANES), F32),
            pltpu.VMEM((devices, 1, LANES), F32),
            sem((4,)),
            sem((rounds, CUTS)),
            sem((4,)),
            sem((rounds, half)),
            sem((rounds, half)),
            sem((rounds,)),
            sem((rounds,)),
            sem(()),
            sem(()),
            pltpu.SemaphoreType.REGULAR((devices.bit_length() - 1,)),
        ],
        compiler_params=pltpu.CompilerParams(collective_id=0, has_side_effects=True, vmem_limit_bytes=VMEM_LIMIT),
        name="stitch",
    )(*(pltpu.with_memory_space_constraint(v, pltpu.MemorySpace.HBM) for v in (edge_colour, scalars[0], patch_live, node_ids, tiled, *constants)))
    return sums


def solution(mesh):
    placed = (
        P(("tiles", "grp"), None, None),
        P(("tiles", "grp"), None),
        P(("tiles", "grp"), None, None, None),
        P(("tiles", "grp"), None),
        P(("tiles", "grp"), None, None),
    )
    return jax.shard_map(
        on_device, mesh=mesh, in_specs=placed, out_specs=P(None, ("tiles", "grp")), check_vma=False
    )
```

```python
import functools
import math

import jax
import jax.numpy as jnp
import numpy as np
from jax import lax
from jax.experimental import pallas as pl
from jax.experimental.pallas import tpu as pltpu
from jax.sharding import PartitionSpec as P

PATCH = 128
NODE_DEV = 128
LANES = 128
GROUP = 4
PAIR = 4
CUTS = 2
SUB = 8
DOT = 2
LATE = {0: (1, 0), 3: (0, 0)}
VMEM_LIMIT = 32 * 1024 * 1024

F32 = jnp.float32
BF16 = jnp.bfloat16
VMEM = pltpu.MemorySpace.VMEM
SMEM = pltpu.MemorySpace.SMEM


def split_np(x):
    hi = np.asarray(x, np.float32).astype(BF16)
    lo = (np.asarray(x, np.float64) - hi.astype(np.float64)).astype(np.float32).astype(BF16)
    return hi, lo


def tables():
    n = PATCH
    h = n // 2
    j = np.arange(n)
    angle = 2.0 * math.pi / n * ((j[:, None] * j[None, :]) % n)
    c, s = np.cos(angle), np.sin(angle)
    rhi, rlo = split_np(np.concatenate([c[: h + 1], s[1:h]], axis=0))
    fore_row = np.concatenate([rhi, rlo], axis=1)
    chi, clo = split_np(np.block([[c, -s], [-s, -c]]))
    fore_col = np.concatenate([chi, clo, chi], axis=0)
    bhi, blo = split_np(np.block([[c, s], [-s, c]]))
    back_col = np.concatenate([bhi, blo, bhi], axis=0)
    weight = np.where(j[:h] == 0, 1.0, 2.0)[None, :]
    ihi, ilo = split_np(np.concatenate([weight * c[:, :h], c[:, h : h + 1], -2.0 * s[:, 1:h]], axis=1) / float(n * n))
    back_row = np.concatenate([ihi, ilo, ihi], axis=1)
    return fore_row, fore_col, back_col, back_row


def split(x):
    hi = x.astype(BF16)
    return hi, (x - hi.astype(F32)).astype(BF16)


def dot(a, b):
    return jnp.dot(a, b, preferred_element_type=F32)


def row_place(column, base):
    count = column.shape[0]
    lane = lax.broadcasted_iota(jnp.int32, (count, LANES), 1)
    sub = lax.broadcasted_iota(jnp.int32, (count, LANES), 0)
    return jnp.sum(jnp.where(lane == sub + base, column, 0.0), axis=0, keepdims=True)


def triple(x):
    hi, lo = split(x)
    return jnp.concatenate([hi, hi, lo], axis=1)


def apply(rows, table):
    out = []
    for p in range(0, len(rows), DOT):
        some = rows[p : p + DOT] if len(rows) - p > DOT + 1 else rows[p:]
        y = dot(jnp.concatenate([triple(v) for v in some], axis=0), table)
        at = 0
        for v in some:
            out.append(y[at : at + v.shape[0]])
            at += v.shape[0]
        if p + len(some) == len(rows):
            return out


def gather_rows(rows):
    sub = lax.broadcasted_iota(jnp.int32, (8, LANES), 0)
    out = jnp.zeros((8, LANES), F32)
    for i, row in enumerate(rows):
        out = jnp.where(sub == i, row, out)
    return out


def spectra(windows, fore_row, fore_col):
    n = PATCH
    h = n // 2
    count = len(windows)
    first = lax.broadcasted_iota(jnp.int32, (8, n), 0) == 0
    mains = []
    middles = []
    for p in range(0, count, 2):
        x = jnp.concatenate(windows[p : p + 2], axis=1)
        y = dot(fore_row, jnp.concatenate([x, x], axis=0))
        for i in range(2):
            part = y[:, i * n : (i + 1) * n]
            middles.append(part[h : h + 1])
            sine = jnp.concatenate([jnp.where(first, 0.0, part[h : h + 8]), part[h + 8 :]], axis=0)
            mains.append(jnp.concatenate([part[:h], sine], axis=1))
    middle = gather_rows(middles)
    mains.append(jnp.concatenate([jnp.concatenate([middle, jnp.zeros_like(middle)], axis=1)] * 2, axis=0))
    parts = apply(mains, fore_col)
    main = [(f[:, :n], f[:, n:]) for f in parts[:-1]]
    return main, (parts[-1][:8, :n], parts[-1][:8, n:])


def fold(v):
    return sum(v[i : i + 8] for i in range(8, v.shape[0], 8)) + v[:8]


def whiten_terms(first, second):
    (r1, i1), (r2, i2) = first, second
    cross_r = r1 * r2 + i1 * i2
    cross_i = i1 * r2 - r1 * i2
    return cross_r, cross_i, jnp.sqrt(cross_r * cross_r + cross_i * cross_i)


def total(v):
    return jnp.sum(v, axis=1, keepdims=True)


def correlate(first, second, back_row, back_col):
    n = PATCH
    h = n // 2
    cells = float(n * n)
    count = len(first[0])
    terms = [whiten_terms(a, b) for a, b in zip(first[0], second[0])]
    middle = whiten_terms(first[1], second[1])

    def spectrum_sum(values, middle_value):
        folded = jnp.concatenate([jnp.sum(fold(v), axis=0, keepdims=True) for v in values], axis=0)
        edge = jnp.concatenate([v[:1] for v in values], axis=0)
        return 2.0 * folded - edge + middle_value[:count], edge

    mag_sum, _ = spectrum_sum([t[2] for t in terms], middle[2])
    extra = 0.1 * (total(mag_sum) / cells) + 1e-06
    inverses = [1.0 / (t[2] + extra[p : p + 1]) for p, t in enumerate(terms)]
    middle_inverse = 1.0 / (middle[2] + gather_rows([extra[p : p + 1] for p in range(count)]))
    rows = [jnp.concatenate([t[0] * v, t[1] * v], axis=1) for t, v in zip(terms, inverses)]
    middle_row = jnp.concatenate([middle[0] * middle_inverse, middle[1] * middle_inverse], axis=1)
    rows.append(jnp.concatenate([middle_row, middle_row], axis=0))

    def power(m, v):
        return (m * v) * (m * v)

    power_sum, edge = spectrum_sum(
        [power(t[2], v) for t, v in zip(terms, inverses)], power(middle[2], middle_inverse)
    )
    lane = lax.broadcasted_iota(jnp.int32, (count, n), 1)
    variance = total(power_sum - jnp.where(lane == 0, edge, 0.0)) / (cells * cells)
    scale = 2.0 / jnp.sqrt(variance + 1e-06) * math.log2(math.e)

    back = apply(rows, back_col)
    middle_back = back[-1][:8, :n]
    first_row = lax.broadcasted_iota(jnp.int32, (8, n), 0) == 0
    surfaces = []
    for p in range(0, count, 2):
        columns = []
        for q in range(p, p + 2):
            part = back[q]
            imag = part[:, n:]
            head = jnp.where(first_row, middle_back[q : q + 1], imag[:8])
            columns.append(jnp.concatenate([part[:, :n], head, imag[8:]], axis=0))
        hi, lo = split(jnp.concatenate(columns, axis=1))
        wide = dot(back_row, jnp.concatenate([hi, hi, lo], axis=0))
        surfaces += [wide[:, :n], wide[:, n:]]

    tops = []
    for surface in surfaces:
        peak = surface[:8]
        for i in range(8, n, 8):
            peak = jnp.maximum(peak, surface[i : i + 8])
        tops.append(jnp.max(peak, axis=0, keepdims=True))
    top = jnp.max(jnp.concatenate(tops, axis=0), axis=1, keepdims=True)
    sub = lax.broadcasted_iota(jnp.int32, (8, n), 0).astype(F32)
    columns = []
    rows = []
    edges = []
    for p in range(count):
        e = jnp.exp2((surfaces[p] - top[p : p + 1]) * scale[p : p + 1])
        part = [e[i : i + 8] for i in range(0, n, 8)]
        upper = part[h // 8 - 1]
        step = upper
        for v in part[h // 8 - 2 : 0 : -1]:
            upper = upper + v
            step = step + upper
        upper = upper + part[0]
        lower = part[h // 8]
        down = lower
        for v in part[h // 8 + 1 :]:
            lower = lower + v
            down = down + lower
        column = upper + lower
        columns.append(jnp.sum(column, axis=0, keepdims=True))
        rows.append(jnp.sum(8.0 * (step - down) + sub * column, axis=0, keepdims=True))
        edges.append(e[h : h + 1, :])
    columns = jnp.concatenate(columns, axis=0)
    rows = jnp.concatenate(rows, axis=0)
    edges = jnp.concatenate(edges, axis=0)
    lane_coord = ((lane + h) % n - h).astype(F32)
    unit = float(n // 8)
    norm = 1.0 / total(columns)
    row_shift = total(rows) * norm / unit
    col_shift = total(columns * lane_coord) * norm / unit
    row_edge = total(edges) * norm * (float(n) / unit)
    col_edge = total(jnp.where(lane == h, columns, 0.0)) * norm * (float(n) / unit)
    return row_shift, col_shift, -row_shift - row_edge, -col_shift - col_edge


MESH = pl.DeviceIdType.MESH


def stitch(
    colour_hbm,
    offset_hbm,
    live_hbm,
    ids_hbm,
    strips_hbm,
    fore_row_hbm,
    fore_col_hbm,
    back_col_hbm,
    back_row_hbm,
    out_ref,
    colour_ref,
    offset_ref,
    live_ref,
    ids_ref,
    strips,
    fore_row_ref,
    fore_col_ref,
    back_col_ref,
    back_row_ref,
    shifted,
    sent,
    firsts,
    middles,
    arrived,
    line,
    lines,
    tile_out,
    tiles,
    scalar_sem,
    strip_sem,
    table_sem,
    window_send,
    window_recv,
    line_send,
    line_recv,
    tile_send,
    tile_recv,
    hello,
):
    n = PATCH
    rounds, layers, blocks = strips.shape[:3]
    slots = offset_ref.shape[3]
    half = slots // 2
    entries = rounds * slots
    groups = lax.axis_size("grp")
    tile_count = lax.axis_size("tiles")
    devices = tile_count * groups
    tile_index = lax.axis_index("tiles")
    group_index = lax.axis_index("grp")
    me = tile_index * groups + group_index
    strides = [1] + [tile_count // 2] * (rounds - 1)
    sides = [(tile_index // s) % 2 for s in strides]
    partners = [tile_index + s * (1 - 2 * side) for s, side in zip(strides, sides)]

    barrier = pltpu.get_barrier_semaphore()
    neighbours = []
    stride = 1
    while stride < tile_count:
        bit = (tile_index // stride) % 2
        neighbours.append((tile_index + stride * (1 - 2 * bit), group_index))
        stride *= 2
    stride = 1
    while stride < groups:
        bit = (group_index // stride) % 2
        neighbours.append((tile_index, group_index + stride * (1 - 2 * bit)))
        stride *= 2
    stages = len(neighbours)
    for at in neighbours:
        pl.semaphore_signal(barrier, inc=1, device_id=at, device_id_type=MESH)

    scalar_loads = [
        pltpu.make_async_copy(a, b, scalar_sem.at[i])
        for i, (a, b) in enumerate(
            [(offset_hbm, offset_ref), (colour_hbm, colour_ref), (live_hbm, live_ref), (ids_hbm, ids_ref)]
        )
    ]
    for load in scalar_loads:
        load.start()
    strip_loads = [
        pltpu.make_async_copy(strips_hbm.at[r, pl.ds(i, layers // CUTS)], strips.at[r, pl.ds(i, layers // CUTS)], strip_sem.at[r, c])
        for r in range(rounds)
        for c, i in enumerate(range(0, layers, layers // CUTS))
    ]
    for load in strip_loads:
        load.start()
    table_loads = [
        pltpu.make_async_copy(a, b, table_sem.at[i])
        for i, (a, b) in enumerate(
            [(fore_row_hbm, fore_row_ref), (fore_col_hbm, fore_col_ref), (back_col_hbm, back_col_ref), (back_row_hbm, back_row_ref)]
        )
    ]
    def extract(r, picks):
        rests = []
        lane = lax.broadcasted_iota(jnp.int32, (n + SUB, LANES), 1)
        for i, k in enumerate(picks):
            row, column = offset_ref[0, r, 0, k], offset_ref[0, r, 1, k]
            block = jnp.minimum(lax.div(column, LANES), blocks - 2)
            layer = jnp.minimum(lax.div(row, SUB), layers - n // SUB - 1)
            shift = column - block * LANES
            turn = lax.rem(2 * LANES - shift, LANES)
            left, right = (
                pltpu.roll(
                    strips[colour_ref[0, r], pl.ds(layer, n // SUB + 1), block + side]
                    .reshape(n + SUB, LANES)
                    .astype(F32),
                    turn,
                    1,
                )
                for side in range(2)
            )
            shifted[i] = jnp.where(lane < LANES - shift, left, right)
            rests.append(row - layer * SUB)
        return [shifted[i, pl.ds(rest, n), :].astype(BF16) for i, rest in enumerate(rests)]

    def pick(r, values):
        value = values[0]
        for i in range(1, rounds):
            value = jnp.where(r == i, values[i], value)
        return value

    def window_copy(r, j):
        return pltpu.make_async_remote_copy(
            src_ref=sent.at[r, j],
            dst_ref=arrived.at[r, j],
            send_sem=window_send.at[r, j],
            recv_sem=window_recv.at[r, j],
            device_id=(pick(r, partners), group_index),
            device_id_type=MESH,
        )

    def line_copy(r):
        return pltpu.make_async_remote_copy(
            src_ref=line,
            dst_ref=lines.at[r],
            send_sem=line_send.at[r],
            recv_sem=line_recv.at[r],
            device_id=(partners[r], group_index),
            device_id_type=MESH,
        )

    for load in scalar_loads:
        load.wait()
    lane = lax.broadcasted_iota(jnp.int32, (1, LANES), 1)

    def place_id(i, ids):
        r, k = i // slots, i % slots
        return jnp.where(lane == i, jnp.where(k < live_ref[0, r], ids_ref[0, r, k], -1), ids)

    line[...] = lax.fori_loop(0, entries, place_id, jnp.zeros((1, LANES), jnp.int32)).astype(F32)
    for load in strip_loads:
        load.wait()
    for load in table_loads:
        load.start()
    pl.semaphore_wait(barrier, stages)
    for r in range(rounds):
        line_copy(r).start()

    def place_of(q):
        return rounds - 1 - q // (half // PAIR), q % (half // PAIR) * PAIR

    def launch(q):
        r, j = place_of(q)
        for i in range(PAIR):
            window_copy(r, j + i).start()

    def produce(q, carry):
        r, j = place_of(q)
        base = (1 - pick(r, sides)) * half + j
        for i, window in enumerate(extract(r, [base + i for i in range(PAIR)])):
            sent[r, j + i] = window

        before, window = place_of(q - 1)

        @pl.when((q > 0) & ((before < rounds - 1) | (window < late_from)))
        def _():
            launch(q - 1)

        return carry

    quarter = tile_index // (tile_count // 4)
    late_from, late_step = half, -1
    for at, (step, window) in LATE.items():
        late_from = jnp.where(quarter == at, window, late_from)
        late_step = jnp.where(quarter == at, step, late_step)
    lax.fori_loop(0, rounds * half // PAIR, produce, 0)
    for load in table_loads:
        load.wait()
    launch(rounds * half // PAIR - 1)
    parts = half // GROUP

    def prepare(g, carry):
        r, part = g // parts, g % parts
        j = part * GROUP
        windows = extract(r, [pick(r, sides) * half + j + i for i in range(GROUP)])
        main, middle = spectra(windows, fore_row_ref[...], fore_col_ref[...])
        for c in range(2):
            for i in range(GROUP):
                firsts[r, j + i, c] = main[i][c]
            middles[r, part, c] = middle[c]
        return carry

    lax.fori_loop(0, rounds * parts, prepare, 0)

    def neighbour(stage):
        tile, group = neighbours[0]
        for i in range(1, stages):
            tile = jnp.where(stage == i, neighbours[i][0], tile)
            group = jnp.where(stage == i, neighbours[i][1], group)
        return tile, group

    def hail(stage):
        pl.semaphore_signal(hello.at[stage], inc=1, device_id=neighbour(stage), device_id_type=MESH)

    def work(g, disp):
        r, part = g // parts, g % parts
        j = part * GROUP

        @pl.when(g == late_step)
        def _():
            def send(j, carry):
                window_copy(rounds - 1, j).start()
                return carry

            lax.fori_loop(late_from, half, send, 0)

        @pl.when(g < stages)
        def _():
            hail(g)

        for i in range(GROUP):
            window_copy(r, j + i).wait_recv()
        seconds = spectra([arrived[r, j + i] for i in range(GROUP)], fore_row_ref[...], fore_col_ref[...])
        a, b, c, d = correlate(
            ([(firsts[r, j + i, 0], firsts[r, j + i, 1]) for i in range(GROUP)], (middles[r, part, 0], middles[r, part, 1])),
            seconds,
            back_row_ref[...],
            back_col_ref[...],
        )
        own = r * slots + pick(r, sides) * half + j
        other = r * slots + (1 - pick(r, sides)) * half + j

        @pl.when(g < stages)
        def _():
            pl.semaphore_wait(hello.at[g], 1)

        return (
            disp
            + row_place(a, own)
            + row_place(c, other)
            + row_place(b, own + entries)
            + row_place(d, other + entries)
        )

    for s in range(rounds):
        line_copy(s).wait()
    ids = line[...]
    id_line = jnp.zeros((1, LANES), F32)
    for s in range(rounds):
        theirs = pltpu.roll(lines[s], jnp.where(sides[s] == 0, half, LANES - half), 1)
        in_round = (lane >= s * slots) & (lane < (s + 1) * slots)
        mine = (lane // half) % 2 == sides[s]
        id_line = id_line + jnp.where(in_round, jnp.where(mine, ids, theirs), 0.0)
    done = rounds * parts
    for i in range(done, stages):
        hail(i)
        pl.semaphore_wait(hello.at[i], 1)
    disp = lax.fori_loop(0, done, work, pltpu.roll(id_line, 2 * entries, 1))

    tile_out[...] = disp
    tiles[me] = disp

    def start(i, carry):
        to = i + jnp.where(i >= me, 1, 0)
        pltpu.make_async_remote_copy(
            src_ref=tile_out,
            dst_ref=tiles.at[me],
            send_sem=tile_send,
            recv_sem=tile_recv,
            device_id=(to // groups, to % groups),
            device_id_type=MESH,
        ).start()
        return carry

    lax.fori_loop(0, devices - 1, start, 0)

    def drain(i, carry):
        window_copy(i // half, i % half).wait_send()
        return carry

    lax.fori_loop(0, rounds * half, drain, 0)
    everyone = pltpu.make_async_remote_copy(
        src_ref=tiles.at[pl.ds(0, devices - 1)],
        dst_ref=tiles.at[pl.ds(0, devices - 1)],
        send_sem=tile_send,
        recv_sem=tile_recv,
        device_id=neighbours[0],
        device_id_type=MESH,
    )
    everyone.wait_recv()

    pack = LANES // entries
    node = lax.broadcasted_iota(jnp.int32, (NODE_DEV, LANES), 0).astype(F32)
    first_node = (me * NODE_DEV).astype(F32)
    lane = lax.broadcasted_iota(jnp.int32, (1, LANES), 1)
    onehots = []
    values = []
    for g in range(devices // pack):
        parts = [jnp.zeros((1, LANES), F32)] * 3
        for i in range(pack):
            tile = tiles[g * pack + i]
            here = (lane >= i * entries) & (lane < (i + 1) * entries)
            for c in range(3):
                moved = pltpu.roll(tile, ((i - c) * entries) % LANES, 1) if i != c else tile
                parts[c] = jnp.where(here, moved, parts[c])
        onehots.append(jnp.where(parts[2] - first_node == node, 1.0, 0.0).astype(BF16))
        tile = jnp.concatenate(parts[:2], axis=0)
        hi = tile.astype(BF16).astype(F32)
        rest = tile - hi
        mid = rest.astype(BF16).astype(F32)
        values.append(jnp.concatenate([hi, mid, rest - mid, jnp.zeros_like(hi)], axis=0).astype(BF16))
    result = lax.dot_general(
        jnp.concatenate(values, axis=1),
        jnp.concatenate(onehots, axis=1),
        (((1,), (1,)), ((), ())),
        preferred_element_type=F32,
    )
    out_ref[...] = result[0:2] + (result[2:4] + result[4:6])
    everyone.wait_send()


def on_device(strips, edge_colour, patch_offsets, patch_live, node_ids):
    rounds, height, width = strips.shape
    n = PATCH
    slot_count = patch_offsets.shape[2]
    half = slot_count // 2
    devices = lax.axis_size("tiles") * lax.axis_size("grp")
    whole = pl.BlockSpec(memory_space=VMEM)
    anywhere = pl.BlockSpec(memory_space=pltpu.MemorySpace.HBM)
    sem = pltpu.SemaphoreType.DMA
    windows = (rounds, half, n, n)
    tiled = strips.reshape(rounds, height // SUB, SUB, width // LANES, LANES).transpose(0, 1, 3, 2, 4)
    scalars = [jnp.transpose(patch_offsets, (0, 1, 3, 2)), edge_colour, patch_live, node_ids]
    constants = [jnp.asarray(t) for t in tables()]
    sums = pl.pallas_call(
        stitch,
        out_shape=jax.ShapeDtypeStruct((2, NODE_DEV), F32),
        in_specs=[anywhere] * 9,
        out_specs=whole,
        scratch_shapes=[
            pltpu.SMEM(edge_colour.shape, jnp.int32),
            pltpu.SMEM(scalars[0].shape, jnp.int32),
            pltpu.SMEM(patch_live.shape, jnp.int32),
            pltpu.SMEM(node_ids.shape, jnp.int32),
            pltpu.VMEM(tiled.shape, BF16),
            *(pltpu.VMEM(t.shape, BF16) for t in constants),
            pltpu.VMEM((GROUP, n + SUB, n), F32),
            pltpu.VMEM(windows, BF16),
            pltpu.VMEM((rounds, half, 2, n // 2, n), F32),
            pltpu.VMEM((rounds, half // GROUP, 2, 8, n), F32),
            pltpu.VMEM(windows, BF16),
            pltpu.VMEM((1, LANES), F32),
            pltpu.VMEM((rounds, 1, LANES), F32),
            pltpu.VMEM((1, LANES), F32),
            pltpu.VMEM((devices, 1, LANES), F32),
            sem((4,)),
            sem((rounds, CUTS)),
            sem((4,)),
            sem((rounds, half)),
            sem((rounds, half)),
            sem((rounds,)),
            sem((rounds,)),
            sem(()),
            sem(()),
            pltpu.SemaphoreType.REGULAR((devices.bit_length() - 1,)),
        ],
        compiler_params=pltpu.CompilerParams(collective_id=0, has_side_effects=True, vmem_limit_bytes=VMEM_LIMIT),
        name="stitch",
    )(*(pltpu.with_memory_space_constraint(v, pltpu.MemorySpace.HBM) for v in (edge_colour, scalars[0], patch_live, node_ids, tiled, *constants)))
    return sums


def solution(mesh):
    placed = (
        P(("tiles", "grp"), None, None),
        P(("tiles", "grp"), None),
        P(("tiles", "grp"), None, None, None),
        P(("tiles", "grp"), None),
        P(("tiles", "grp"), None, None),
    )
    return jax.shard_map(
        on_device, mesh=mesh, in_specs=placed, out_specs=P(None, ("tiles", "grp")), check_vma=False
    )
```
